32 devices in a mesh: dp: 8 (over z, core), expert: 4 (over y, x).
Axes of the slice: x: 2, y: 2, z: 4, core: 2. Of those that a mesh axis runs over, the one named last changes fastest.
Arguments:
- inputs: bfloat16 [8, 2, 512, 2048], P('dp', None, 'expert'), may hold values from -6 to 6
- attn_routes: int32 [8, 2, 512, 2], P('dp', None, 'expert'), may hold values from 0 to 3, all different within a row; in each aligned block of 128 rows (0 to 127, 128 to 255, ..., all dimensions but the last counted through in order) at most 64 rows name the same one
- mlp_routes: int32 [8, 2, 512, 2], P('dp', None, 'expert'), may hold values from 0 to 3, all different within a row; in each aligned block of 128 rows (0 to 127, 128 to 255, ..., all dimensions but the last counted through in order) at most 64 rows name the same one
- pic_start: int32 [8], P('dp'), may hold values from 0 to 768, as said below
- kv_weight: bfloat16 [2048, 4096], P(('dp', 'expert')), may hold values from -0.125 to 0.125
- router_weight: bfloat16 [2048, 8], P(('dp', 'expert')), may hold values from -0.09375 to 0.09375
- norm_gains: bfloat16 [2048, 2], P(('dp', 'expert')), may hold values from 0.5 to 1.5
- q_weight: bfloat16 [4, 2048, 2048], P('expert', 'dp'), may hold values from -1 to 1
- o_weight: bfloat16 [4, 2048, 2048], P('expert', 'dp'), may hold values from -1.5 to 1.5
- gate_weight: bfloat16 [4, 2048, 5632], P('expert', 'dp'), may hold values from -0.125 to 0.125
- up_weight: bfloat16 [4, 2048, 5632], P('expert', 'dp'), may hold values from -0.125 to 0.125
- down_weight: bfloat16 [4, 5632, 2048], P('expert', 'dp'), may hold values from -0.078125 to 0.078125
- cotangent: bfloat16 [8, 2, 512, 2048], P('dp', None, 'expert'), may hold values from -6 to 6
Outputs:
- out_act: bfloat16 [8, 2, 512, 2048], P('dp', None, 'expert')
- grad_x: float32 [8, 2, 512, 2048], P('dp', None, 'expert')
- grad_kv: float32 [2048, 4096], P(('dp', 'expert'))
- grad_router: float32 [2048, 8], P(('dp', 'expert'))
- grad_gains: float32 [2048, 2], P(('dp', 'expert'))
- grad_q: float32 [4, 2048, 2048], P('expert', 'dp')
- grad_o: float32 [4, 2048, 2048], P('expert', 'dp')
- grad_gate: float32 [4, 2048, 5632], P('expert', 'dp')
- grad_up: float32 [4, 2048, 5632], P('expert', 'dp')
- grad_down: float32 [4, 5632, 2048], P('expert', 'dp')
- clipped_q: bfloat16 [4, 2048, 2048], P('expert', 'dp')
- clipped_key: bfloat16 [2048, 2048], P(('dp', 'expert'))
The draws below stay inside these ranges and needn't reach their ends.
Inputs may be any that keep to these rules, and one draw needn't show every extreme that they name: `attn_routes`: in every micro-batch, among the 128 tokens of one device each expert is chosen by exactly 64 (token, choice) pairs; a token's 2 choices differ. `mlp_routes`: in every micro-batch, among the 128 tokens of one device each expert is chosen by exactly 64 (token, choice) pairs; a token's 2 choices differ. `pic_start`: each picture piece lies inside one micro-batch of its sequence.
All inputs are finite; a program needn't handle non-finite values.
Results may differ from the reference program's by a relative error of at most 0.02.
Values may be sent and summed in bfloat16 or wider, within the bound.
No kernel may reach another device: no remote copies, remote signals or barrier semaphores. Data moves between devices by JAX's collectives and lax.ppermute only.
A program may use at most 384 MiB of HBM per device.

```python
import math
import jax
import jax.numpy as jnp
import numpy as np
from jax import lax

D = 2048
HEADS = 16
HSZ = 128
FF = 5632
TOPK = 2
EXPERTS = 4
HD = 2048
PIC = 256
SEQ = 1024
MICRO = 2
SEQH = 512
TOK = 128
CAP = 64
SEQS = 8


def draw_pic_start(key, part):
    key_half, key_offset = jax.random.split(jax.random.fold_in(key, 11))
    halves = jax.random.randint(key_half, (SEQS,), 0, MICRO)
    offsets = jax.random.randint(key_offset, (SEQS,), 0, SEQH - PIC + 1)
    halves = halves.at[0].set(MICRO - 1).at[1].set(0)
    offsets = offsets.at[0].set(SEQH - PIC).at[1].set(0)
    return (halves * SEQH + offsets).astype(jnp.int32)


def draw_q_weight(key, part):
    key_base, key_spread = jax.random.split(jax.random.fold_in(key, 23))
    draw_shape = (EXPERTS, D, HEADS, HSZ)
    base_values = jnp.clip(jax.random.normal(key_base, draw_shape, jnp.float32), -4.0, 4.0)
    spread = jnp.exp(jax.random.uniform(key_spread, (EXPERTS, 1, HEADS, 1), jnp.float32, 0.0, math.log(2.5)))
    return (base_values * spread / math.sqrt(D)).reshape(EXPERTS, D, HEADS * HSZ).astype(jnp.bfloat16)


def steps_of(own_key, dims, pieces, least, high):
    loudness, own = 1.0, jax.random.fold_in(own_key, 6)
    for dim, parts in pieces:
        steps = jnp.exp(jax.random.uniform(jax.random.fold_in(own, dim), (parts,), jnp.float32, least / len(pieces), high / len(pieces)))
        loudness = loudness * jnp.repeat(steps, dims[dim] // parts).reshape([-1 if axis == dim else 1 for axis in range(len(dims))])
    return loudness


def shared_out(rng, own, number, rows, count, top, reach, lean):
    order = jax.random.permutation(rng, count)
    crowded, usual = load_shares(count, rows * top, reach, lean, True), load_shares(count, rows * top, reach, lean, False)
    places = jnp.arange(count)

    def named(tallies, rotation):
        used = int((tallies > 0).sum())
        fixed = max(1, used // 4)
        moved = fixed + (places - fixed + rotation * (used - fixed)) % max(1, count - fixed)
        return jnp.zeros((count,), jnp.int32).at[order[jnp.where(places < fixed, places, moved)]].set(jnp.asarray(tallies, jnp.int32))

    tallies = jnp.where(number % 4 == 0, named(crowded, number // 4), named(usual, number - number // 4 - 1))
    mixed = jax.random.permutation(jax.random.fold_in(own, 3), count)
    source_of, receiver = mixed[0:count // 2 * 2:2], mixed[1:count // 2 * 2:2]
    room = jnp.minimum(tallies[source_of] - 1, reach - tallies[receiver]) // 2
    room = jnp.where((source_of == order[0]) | (receiver == order[0]) | (tallies[receiver] == 0), 0, jnp.maximum(room, 0))
    moved = jax.random.randint(jax.random.fold_in(own, 4), (count // 2,), 0, 1 << 20) % (room + 1)
    tallies = tallies.at[source_of].add(-moved).at[receiver].add(moved)
    members = jnp.searchsorted(jnp.cumsum(tallies), jnp.arange(rows * top), side="right").astype(jnp.int32)
    grid = members.reshape(top, rows).T
    grid = grid[jax.random.permutation(jax.random.fold_in(own, 1), rows)]
    rotation = jax.random.randint(jax.random.fold_in(own, 2), (rows, 1), 0, top)
    return jnp.take_along_axis(grid, (jnp.arange(top)[None, :] + rotation) % top, axis=1)


def load_shares(amount, total, bound, lean, full):
    weights = [(1 << 20) // math.isqrt(rank ** lean) + 1 for rank in range(1, amount + 1)]
    largest = bound if full else min(bound, max(-(-total // amount), total * weights[0] // sum(weights)))
    least = 1 if total - largest >= amount - 1 else 0
    counts, surplus = [largest] + [least] * (amount - 1), total - largest - least * (amount - 1)
    while surplus > 0:
        movable = [i for i in range(1, amount) if counts[i] < largest] or [i for i in range(1, amount) if counts[i] < bound]
        mass, left = sum([weights[i] for i in movable]), surplus
        for i in movable:
            more = min(bound - counts[i], max(1, left * weights[i] // mass), surplus)
            counts[i] = counts[i] + more
            surplus = surplus - more
    return np.array(counts)


def centred(stream_key, shape, scale, limit, shards=(), held_as=jnp.bfloat16):
    drawn = scale * jax.random.normal(stream_key, shape, jnp.float32)
    if shards:
        drawn = drawn * steps_of(stream_key, shape, shards, -0.22, 0.18)
    return jnp.clip(drawn, -limit, limit).astype(held_as)


def setup_inputs(seed: int = 0) -> dict:
    key_list = jax.random.split(jax.random.key(seed), 14)
    inputs = centred(key_list[0], (SEQS, MICRO, SEQH, D), 1.0, 6.0, ((0, 8), (2, 4)))
    attn_routes_keys = jax.random.split(jax.random.fold_in(key_list[1], 1), SEQS * MICRO * SEQH // TOK)
    attn_routes_turns = jax.random.permutation(jax.random.fold_in(key_list[1], 3), SEQS * MICRO * SEQH // TOK)
    attn_routes = jax.vmap(lambda own, number: shared_out(jax.random.fold_in(key_list[1], 2), own, number, TOK, EXPERTS, TOPK, CAP, 0))(attn_routes_keys, attn_routes_turns).reshape((SEQS, MICRO, SEQH, TOPK))
    mlp_routes_keys = jax.random.split(jax.random.fold_in(key_list[2], 1), SEQS * MICRO * SEQH // TOK)
    mlp_routes_turns = jax.random.permutation(jax.random.fold_in(key_list[2], 3), SEQS * MICRO * SEQH // TOK)
    mlp_routes = jax.vmap(lambda own, number: shared_out(jax.random.fold_in(key_list[2], 2), own, number, TOK, EXPERTS, TOPK, CAP, 0))(mlp_routes_keys, mlp_routes_turns).reshape((SEQS, MICRO, SEQH, TOPK))
    pic_start = draw_pic_start(jax.random.fold_in(key_list[13], 71), 0)
    kv_weight = centred(key_list[4], (D, 2 * HD), D ** -0.5, 0.125, ((0, 32),))
    router_weight = centred(key_list[5], (D, 2 * EXPERTS), (16 * D // 9) ** -0.5, 0.09375, ((0, 32),))
    norm_gains = jnp.clip(1.0 + 0.1 * jax.random.normal(key_list[6], (D, 2), jnp.float32), 0.5, 1.5).astype(jnp.bfloat16)
    q_weight = draw_q_weight(jax.random.fold_in(key_list[13], 71), 0)
    o_weight = centred(key_list[8], (EXPERTS, HD, D), (max(HD // 128, 1)) ** -0.5, 1.5, ((0, 4), (1, 8)))
    gate_weight = centred(key_list[9], (EXPERTS, D, FF), D ** -0.5, 0.125, ((0, 4), (1, 8)))
    up_weight = centred(key_list[10], (EXPERTS, D, FF), D ** -0.5, 0.125, ((0, 4), (1, 8)))
    down_weight = centred(key_list[11], (EXPERTS, FF, D), FF ** -0.5, 0.078125, ((0, 4), (1, 8)))
    cotangent = centred(key_list[12], (SEQS, MICRO, SEQH, D), 1.0, 6.0, ((0, 8), (2, 4)))
    return dict(inputs=inputs, attn_routes=attn_routes, mlp_routes=mlp_routes, pic_start=pic_start, kv_weight=kv_weight, router_weight=router_weight, norm_gains=norm_gains, q_weight=q_weight, o_weight=o_weight, gate_weight=gate_weight, up_weight=up_weight, down_weight=down_weight, cotangent=cotangent)


@jax.custom_vjp
def lowered_state(v):
    return lax.optimization_barrier(v.astype(jnp.bfloat16)).astype(jnp.float32)

@jax.custom_vjp
def lowered_state_backward(v):
    return v

def low_keep(v):
    return (lowered_state(v), None)

def low_pass(kept, grad):
    return (grad,)

def back_keep(v):
    return (v, None)

def back_low(kept, grad):
    return (lowered_state(grad),)
lowered_state.defvjp(low_keep, low_pass)
lowered_state_backward.defvjp(back_keep, back_low)
norm_eps = 1e-06
logit_cap = 8.0
masked_low = -1e+30

def dense(left, right):
    return jnp.dot(left, right, precision=lax.Precision.HIGHEST, preferred_element_type=jnp.float32)

def normalize(values, norm_gain):
    return values * lax.rsqrt(lax.optimization_barrier(jnp.mean(values * values, axis=-1, keepdims=True)) + norm_eps) * norm_gain

def rope_tables(positions):
    half_size = HSZ // 2
    freq_rows = jnp.exp(jnp.arange(half_size, dtype=jnp.float32) * (-math.log(10000.0) / half_size))
    angles = positions[:, None] * freq_rows[None, :]
    return (jnp.cos(angles), jnp.sin(angles))

def rotate(vectors, cosine, sine):
    half_size = HSZ // 2
    leading = vectors[..., :half_size]
    trailing = vectors[..., half_size:]
    cos_rows = cosine[:, None, :]
    sin_rows = sine[:, None, :]
    return jnp.concatenate([leading * cos_rows - trailing * sin_rows, trailing * cos_rows + leading * sin_rows], axis=-1)

def allowed(query_pos, key_pos, piece_start):
    query_in = (query_pos >= piece_start) & (query_pos < piece_start + PIC)
    key_in = (key_pos >= piece_start) & (key_pos < piece_start + PIC)
    return (key_pos[None, :] <= query_pos[:, None]) | query_in[:, None] & key_in[None, :]

def gates_of(rows_low, router_cols, routes_seq):
    logits = dense(rows_low, router_cols)
    chosen = jnp.take_along_axis(logits, routes_seq, axis=1)
    return jax.nn.softmax(chosen, axis=-1)

def grouped(routes_seq):
    pair_count = SEQ * TOPK
    sort_keys = routes_seq.reshape(-1) * pair_count + jnp.arange(pair_count, dtype=jnp.int32)
    sorted_pairs = jnp.argsort(sort_keys).astype(jnp.int32)
    pair_slots = jnp.argsort(sorted_pairs).astype(jnp.int32)
    return (sorted_pairs.reshape(EXPERTS, pair_count // EXPERTS), pair_slots)

def sequence(values, seq_attn, seq_mlp, piece_start, kv_w, router_w, gains, query_w, output_w, gate_w, upward_w, down_w):
    inner_width = HEADS * HSZ
    positions = jnp.arange(SEQ, dtype=jnp.int32)
    cosine, sine = rope_tables(positions.astype(jnp.float32))
    first_low = lowered_state(normalize(values, gains[:, 0]))
    gathered_keys = lowered_state(rotate(lowered_state_backward(dense(first_low, kv_w[:, :inner_width])).reshape(SEQ, HEADS, HSZ), cosine, sine))
    gathered_values = lowered_state(lowered_state_backward(dense(first_low, kv_w[:, inner_width:]))).reshape(SEQ, HEADS, HSZ)
    attn_gates = gates_of(first_low, router_w[:, :EXPERTS], seq_attn)
    attn_sorted, attn_slots = grouped(seq_attn)
    attn_tokens = attn_sorted // TOPK
    score_factor = HSZ ** (-0.5)

    def attend(packed):
        rows_in, query_mat, output_mat, query_pos = packed
        rotated_query = lowered_state(rotate(lowered_state_backward(dense(rows_in, query_mat)).reshape(-1, HEADS, HSZ), cosine[query_pos], sine[query_pos]))
        attention_scores = lowered_state_backward(jnp.einsum('cln,tln->lct', rotated_query, gathered_keys, precision=lax.Precision.HIGHEST) * score_factor)
        visible = allowed(query_pos, positions, piece_start)[None]
        masked = jnp.where(visible, attention_scores, masked_low)
        attention_probabilities = jax.nn.softmax(masked, axis=-1)
        blended_rows = lowered_state_backward(lowered_state(jnp.einsum('yjq,qyc->jyc', lowered_state(attention_probabilities), gathered_values, precision=lax.Precision.HIGHEST)))
        return (lowered_state(dense(blended_rows.reshape(-1, inner_width), output_mat)), lax.optimization_barrier(jnp.max(masked, axis=(1, 2))))
    attn_rows, peaks = lax.map(jax.checkpoint(attend), (lowered_state_backward(first_low[attn_tokens]), query_w, output_w, attn_tokens))
    attn_pairs = lowered_state_backward(attn_rows.reshape(-1, D)[attn_slots].reshape(SEQ, TOPK, D))
    middle = values + lax.optimization_barrier(jnp.sum(attn_gates[:, :, None] * attn_pairs, axis=1))
    second_low = lowered_state(normalize(middle, gains[:, 1]))
    mlp_gates = gates_of(second_low, router_w[:, EXPERTS:], seq_mlp)
    mlp_sorted, mlp_slots = grouped(seq_mlp)

    def feed(packed):
        rows_in, gate_mat, upward_mat, down_mat = packed
        gate_pre = lowered_state_backward(dense(rows_in, gate_mat))
        up_pre = lowered_state_backward(dense(rows_in, upward_mat))
        return lowered_state(dense(lowered_state(jax.nn.silu(gate_pre) * up_pre), down_mat))
    mlp_rows = lax.map(jax.checkpoint(feed), (lowered_state_backward(second_low[mlp_sorted // TOPK]), gate_w, upward_w, down_w))
    mlp_pairs = lowered_state_backward(mlp_rows.reshape(-1, D)[mlp_slots].reshape(SEQ, TOPK, D))
    return (middle + lax.optimization_barrier(jnp.sum(mlp_gates[:, :, None] * mlp_pairs, axis=1)), peaks)

def reference(inputs, attn_routes, mlp_routes, pic_start, kv_weight, router_weight, norm_gains, q_weight, o_weight, gate_weight, up_weight, down_weight, cotangent):
    routes_attn = attn_routes.reshape(SEQS, SEQ, TOPK)
    routes_mlp = mlp_routes.reshape(SEQS, SEQ, TOPK)

    def forward(values, kv_w, router_w, gains, query_w, output_w, gate_w, upward_w, down_w):

        def one_sequence(packed):
            seq_values, seq_attn, seq_mlp, seq_start = packed
            return sequence(seq_values, seq_attn, seq_mlp, seq_start, kv_w, router_w, gains, query_w, output_w, gate_w, upward_w, down_w)
        results, peaks = lax.map(one_sequence, (values, routes_attn, routes_mlp, pic_start))
        return (results, lax.optimization_barrier(jnp.max(peaks, axis=0)))
    floats = (inputs.astype(jnp.float32).reshape(SEQS, SEQ, D), kv_weight.astype(jnp.float32), router_weight.astype(jnp.float32), norm_gains.astype(jnp.float32), q_weight.astype(jnp.float32), o_weight.astype(jnp.float32), gate_weight.astype(jnp.float32), up_weight.astype(jnp.float32), down_weight.astype(jnp.float32))
    results, pullback, biggest = jax.vjp(forward, *floats, has_aux=True)
    grads = pullback(cotangent.astype(jnp.float32).reshape(SEQS, SEQ, D))
    ratio = logit_cap / jnp.maximum(biggest, logit_cap)
    root_query = jnp.sqrt(ratio)
    root_key = jnp.sqrt(lax.optimization_barrier(jnp.min(ratio, axis=0)))
    inner_width = HEADS * HSZ
    clipped_q = (floats[4].reshape(EXPERTS, D, HEADS, HSZ) * root_query[:, None, :, None]).reshape(EXPERTS, D, inner_width).astype(jnp.bfloat16)
    clipped_key = (floats[1][:, :inner_width].reshape(D, HEADS, HSZ) * root_key[None, :, None]).reshape(D, inner_width).astype(jnp.bfloat16)
    out_act = results.reshape(inputs.shape).astype(jnp.bfloat16)
    grad_x = grads[0].reshape(inputs.shape)
    return (out_act, grad_x, grads[1], grads[2], grads[3], grads[4], grads[5], grads[6], grads[7], grads[8], clipped_q, clipped_key)
```

```python
import math

import jax
import jax.numpy as jnp
from jax import lax
from jax.experimental import pallas as pl
from jax.experimental.pallas import tpu as pltpu
from jax.sharding import PartitionSpec as P

HEADS = 16
HSZ = 128
TOPK = 2
PIC = 256
MICRO = 2
ORDER = (1, 0)

norm_eps = 1e-06
logit_cap = 8.0
masked_low = -1e30
bf16 = jnp.bfloat16
f32 = jnp.float32


def mm(left, right):
    return jnp.dot(left, right, preferred_element_type=f32)


def mm_t(left, right):
    return lax.dot_general(left, right, (((1,), (1,)), ((), ())), preferred_element_type=f32)


def t_mm(left, right):
    return lax.dot_general(left, right, (((0,), (0,)), ((), ())), preferred_element_type=f32)


def exact(left, right, dims):
    return lax.dot_general(
        left, right, (dims, ((), ())), precision=lax.Precision.HIGHEST, preferred_element_type=f32
    )


def rope_tables(positions):
    half = HSZ // 2
    freq = jnp.exp(jnp.arange(half, dtype=f32) * (-math.log(10000.0) / half))
    angles = positions.astype(f32)[..., None] * freq
    cosine, sine = jnp.cos(angles), jnp.sin(angles)
    return (
        jnp.concatenate([cosine, cosine], axis=-1),
        jnp.concatenate([-sine, sine], axis=-1),
    )


def inverse_rms(values):
    return lax.rsqrt(jnp.mean(values * values, axis=-1, keepdims=True) + norm_eps)


def norm_back(values, inverse, gain, upstream):
    scaled = upstream * gain
    gain_grad = jnp.sum(upstream * values * inverse, axis=0)
    values_grad = inverse * scaled - values * inverse * inverse * inverse * jnp.mean(
        scaled * values, axis=-1, keepdims=True
    )
    return values_grad, gain_grad


def selection(hot, slots):
    tokens = hot.shape[-1]
    before = jnp.triu(jnp.ones((tokens, tokens), bf16), 1)
    rank = jnp.dot(hot.astype(bf16), before, preferred_element_type=f32)
    slot = jnp.arange(slots, dtype=jnp.int32)[:, None]
    taken = (rank.astype(jnp.int32)[..., None, :] == slot) & (hot[..., None, :] > 0)
    return taken.astype(bf16)


def kv_kernel(a_ref, w_ref, cos_ref, sin_ref, o_ref):
    got = jnp.dot(a_ref[...], w_ref[...], preferred_element_type=f32)
    cosine, sine = cos_ref[0], sin_ref[0]
    for part in range(got.shape[1] // HSZ):
        piece = got[:, part * HSZ : (part + 1) * HSZ]
        turned = piece * cosine + pltpu.roll(piece, HSZ // 2, 1) * sine
        o_ref[0, :, part * HSZ : (part + 1) * HSZ] = turned.astype(bf16)


def project_kv(a_rows, kv_cols, cosine, sine):
    rows, width = a_rows.shape
    group = kv_cols.shape[1] // 2
    step = min(256, group)
    per = group // step
    return pl.pallas_call(
        kv_kernel,
        grid=(2 * per,),
        in_specs=[
            pl.BlockSpec((rows, width), lambda g: (0, 0)),
            pl.BlockSpec((width, step), lambda g: (0, g)),
            pl.BlockSpec((1, rows, HSZ), lambda g: (g // per, 0, 0)),
            pl.BlockSpec((1, rows, HSZ), lambda g: (g // per, 0, 0)),
        ],
        out_specs=pl.BlockSpec((1, rows, step), lambda g: (g // per, 0, g % per)),
        out_shape=jax.ShapeDtypeStruct((2, rows, group), bf16),
        name="project_kv",
    )(a_rows, kv_cols, cosine, sine)


def kv_back_kernel(*refs):
    pieces, (cos_ref, sin_ref, o_ref) = refs[:-3], refs[-3:]
    cosine, sine = cos_ref[0], sin_ref[0]
    total = pieces[0][0].astype(f32)
    for piece in pieces[1:]:
        total = total + piece[0].astype(f32)
    for part in range(total.shape[1] // HSZ):
        cut = total[:, part * HSZ : (part + 1) * HSZ]
        turned = cut * cosine - pltpu.roll(cut, HSZ // 2, 1) * sine
        o_ref[:, part * HSZ : (part + 1) * HSZ] = turned.astype(bf16)


def sum_kv_grads(pieces, cosine, sine):
    _, rows, group = pieces[0].shape
    return pl.pallas_call(
        kv_back_kernel,
        grid=(2,),
        in_specs=[pl.BlockSpec((1, rows, group), lambda g: (g, 0, 0)) for _ in pieces]
        + [pl.BlockSpec((1, rows, HSZ), lambda g: (g, 0, 0))] * 2,
        out_specs=pl.BlockSpec((rows, group), lambda g: (0, g)),
        out_shape=jax.ShapeDtypeStruct((rows, 2 * group), bf16),
        name="sum_kv_grads",
    )(*pieces, cosine, sine)


def scores_of(query, keys, place_ref, qpos, micro, tokens, group_index):
    parts = []
    flip = (place_ref[0] ^ group_index) * tokens
    start = place_ref[1]
    for m in range(micro + 1):
        got = lax.dot_general(
            query, keys[m], (((1,), (1,)), ((), ())), preferred_element_type=f32
        ) * (HSZ**-0.5)
        if m == micro:
            count = got.shape[1]
            kpos = micro * count + (lax.broadcasted_iota(jnp.int32, got.shape, 1) ^ flip)
            inside_q = (qpos >= start) & (qpos < start + PIC)
            inside_k = (kpos >= start) & (kpos < start + PIC)
            keep = (kpos <= qpos) | (inside_q & inside_k)
            got = jnp.where(keep, got, masked_low)
        parts.append(got)
    peak = parts[0].max(axis=1, keepdims=True)
    for got in parts[1:]:
        peak = jnp.maximum(peak, got.max(axis=1, keepdims=True))
    lifted = [jnp.exp(got - peak) for got in parts]
    total = lifted[0].sum(axis=1, keepdims=True)
    for got in lifted[1:]:
        total = total + got.sum(axis=1, keepdims=True)
    scale = 1.0 / total
    return [got * scale for got in lifted], peak


def attend(q_pre, cosine, sine, qpos, kvs, place, tokens):
    micro = len(kvs) - 1
    rows, inner = q_pre.shape
    experts, _, keys, group = kvs[0].shape
    hg = group // HSZ

    def kernel(place_ref, q_ref, cos_ref, sin_ref, pos_ref, *rest):
        kv_refs, (mixed_ref, rot_ref, peak_ref) = rest[:-3], rest[-3:]
        g = pl.program_id(0)
        q = q_ref[...]
        turned = (q * cos_ref[...] + pltpu.roll(q, HSZ // 2, 1) * sin_ref[...]).astype(bf16)
        rot_ref[...] = turned
        probs, peak = scores_of(
            turned, [r[0, 0] for r in kv_refs], place_ref, pos_ref[...], micro, tokens, g // hg
        )
        mixed = jnp.zeros((rows, HSZ), f32)
        for m in range(micro + 1):
            mixed = mixed + jnp.dot(
                probs[m].astype(bf16), kv_refs[m][0, 1], preferred_element_type=f32
            )
        mixed_ref[...] = mixed.astype(bf16)
        peak_ref[...] = jnp.full(peak_ref.shape, jnp.max(peak), f32)

    def head(g, s):
        return (s[0] ^ (g // hg)) * hg + g % hg

    column = pl.BlockSpec((rows, HSZ), lambda g, s: (0, head(g, s)))
    full = lambda shape: pl.BlockSpec(shape, lambda g, s: (0,) * len(shape))
    return pl.pallas_call(
        kernel,
        grid_spec=pltpu.PrefetchScalarGridSpec(
            num_scalar_prefetch=1,
            grid=(HEADS,),
            in_specs=[column, full((rows, HSZ)), full((rows, HSZ)), full((rows, 1))]
            + [
                pl.BlockSpec((1, 2, keys, HSZ), lambda g, s: (g // hg, 0, 0, g % hg))
                for _ in kvs
            ],
            out_specs=[
                column,
                column,
                pl.BlockSpec((1, 8, 128), lambda g, s: (head(g, s), 0, 0)),
            ],
        ),
        out_shape=[
            jax.ShapeDtypeStruct((rows, inner), bf16),
            jax.ShapeDtypeStruct((rows, inner), bf16),
            jax.ShapeDtypeStruct((HEADS, 8, 128), f32),
        ],
        name="attend",
    )(place, q_pre, cosine, sine, qpos, *kvs)


def attend_back(q_rot, d_mixed, cosine, sine, qpos, kvs, later, place, tokens):
    micro = len(kvs) - 1
    rows, inner = q_rot.shape
    experts, _, keys, group = kvs[0].shape
    hg = group // HSZ
    held = len(later)

    def kernel(place_ref, q_ref, dm_ref, cos_ref, sin_ref, pos_ref, *rest):
        kv_refs = rest[: micro + 1]
        later_refs = rest[micro + 1 : micro + 1 + held]
        dq_ref, dkv_refs = rest[micro + 1 + held], rest[micro + 2 + held :]
        g = pl.program_id(0)
        q = q_ref[...]
        dm = dm_ref[...]
        probs, _ = scores_of(
            q, [r[0, 0] for r in kv_refs], place_ref, pos_ref[...], micro, tokens, g // hg
        )
        d_probs = [
            lax.dot_general(dm, r[0, 1], (((1,), (1,)), ((), ())), preferred_element_type=f32)
            for r in kv_refs
        ]
        inner_sum = jnp.sum(d_probs[0] * probs[0], axis=1, keepdims=True)
        for m in range(1, micro + 1):
            inner_sum = inner_sum + jnp.sum(d_probs[m] * probs[m], axis=1, keepdims=True)
        d_q = jnp.zeros((rows, HSZ), f32)
        for m in range(micro + 1):
            d_scores = (probs[m] * (d_probs[m] - inner_sum)).astype(bf16)
            d_q = d_q + jnp.dot(d_scores, kv_refs[m][0, 0], preferred_element_type=f32)
            d_k = lax.dot_general(
                d_scores, q, (((0,), (0,)), ((), ())), preferred_element_type=f32
            ) * (HSZ**-0.5)
            d_v = lax.dot_general(
                probs[m].astype(bf16), dm, (((0,), (0,)), ((), ())), preferred_element_type=f32
            )
            if m < held:
                d_k = d_k + later_refs[m][0, 0].astype(f32)
                d_v = d_v + later_refs[m][0, 1].astype(f32)
            dkv_refs[m][0, 0] = d_k.astype(bf16)
            dkv_refs[m][0, 1] = d_v.astype(bf16)
        d_q = d_q * (HSZ**-0.5)
        dq_ref[...] = (d_q * cos_ref[...] - pltpu.roll(d_q, HSZ // 2, 1) * sin_ref[...]).astype(
            bf16
        )

    def head(g, s):
        return (s[0] ^ (g // hg)) * hg + g % hg

    column = pl.BlockSpec((rows, HSZ), lambda g, s: (0, head(g, s)))
    full = lambda shape: pl.BlockSpec(shape, lambda g, s: (0,) * len(shape))
    kv_spec = pl.BlockSpec((1, 2, keys, HSZ), lambda g, s: (g // hg, 0, 0, g % hg))
    return pl.pallas_call(
        kernel,
        grid_spec=pltpu.PrefetchScalarGridSpec(
            num_scalar_prefetch=1,
            grid=(HEADS,),
            in_specs=[column, column, full((rows, HSZ)), full((rows, HSZ)), full((rows, 1))]
            + [kv_spec] * (micro + 1 + held),
            out_specs=[column] + [kv_spec] * (micro + 1),
        ),
        out_shape=[jax.ShapeDtypeStruct((rows, inner), bf16)]
        + [jax.ShapeDtypeStruct(kvs[0].shape, bf16) for _ in kvs],
        name="attend_back",
    )(place, q_rot, d_mixed, cosine, sine, qpos, *kvs, *later)


def per_device(
    inputs,
    attn_routes,
    mlp_routes,
    pic_start,
    kv_weight,
    router_weight,
    norm_gains,
    q_weight,
    o_weight,
    gate_weight,
    up_weight,
    down_weight,
    cotangent,
):
    experts = lax.axis_size("expert")
    dp_size = lax.axis_size("dp")
    stages = dp_size // 2
    own = lax.axis_index("expert")
    dp_index = lax.axis_index("dp")
    stage, core = dp_index // 2, dp_index % 2
    tokens, width = inputs.shape[2], inputs.shape[3]
    inner = HEADS * HSZ
    group = inner // experts
    slots = tokens * TOPK // experts
    span = tokens * experts
    rows_each = kv_weight.shape[0]
    hidden = gate_weight.shape[2]
    part = hidden // stages
    routed = experts * slots

    def across(block, k):
        if k == 0:
            return block
        return lax.ppermute(block, "expert", [(j, j ^ k) for j in range(experts)])

    def along(block, k):
        if k % stages == 0:
            return block
        return lax.ppermute(
            block, "dp", [(j, ((j // 2 + k) % stages) * 2 + j % 2) for j in range(dp_size)]
        )

    def partner(block):
        return lax.ppermute(block, "dp", [(j, j ^ 1) for j in range(dp_size)])

    def pick(array, index, axis=0):
        return lax.dynamic_index_in_dim(array, index, axis, keepdims=False)

    small = jnp.concatenate(
        [
            attn_routes.reshape(-1).astype(bf16),
            mlp_routes.reshape(-1).astype(bf16),
            router_weight.reshape(-1),
            norm_gains.reshape(-1),
        ]
    )
    length = small.shape[0]
    small = jnp.pad(small, (0, -length % 128)).reshape(-1, 128)
    small = lax.all_gather(lax.all_gather(small, "expert", axis=0), "dp", axis=0)
    small = small.reshape(dp_size, experts, -1)
    count = MICRO * tokens * TOPK
    xor_order = own ^ jnp.arange(experts, dtype=jnp.int32)
    stage_order = (stage - jnp.arange(stages, dtype=jnp.int32)) % stages
    routes_a = pick(small[:, :, :count], dp_index).astype(jnp.int32)
    routes_a = routes_a.reshape(experts, MICRO, tokens, TOPK)[xor_order]
    routes_m = small[:, :, count : 2 * count].reshape(stages, 2, experts, count)
    routes_m = pick(routes_m, core, 1).astype(jnp.int32)
    routes_m = routes_m.reshape(stages, experts, MICRO, tokens, TOPK)[stage_order][:, xor_order]
    router = small[:, :, 2 * count : 2 * count + rows_each * 2 * experts].reshape(
        width, 2 * experts
    )
    gains = small[:, :, 2 * count + rows_each * 2 * experts : length].reshape(width, 2)
    gain_1, gain_2 = gains[:, 0].astype(f32), gains[:, 1].astype(f32)
    router_a, router_m = router[:, :experts], router[:, experts:]

    kv_split = kv_weight.reshape(rows_each, 2, experts, group)
    kv_got = [
        across(pick(kv_split, own ^ k, 2).reshape(rows_each, 2 * group), k) for k in range(experts)
    ]
    kv_rows = jnp.stack(kv_got)[xor_order].reshape(experts * rows_each, 2 * group)
    kv_cols = lax.all_gather(kv_rows, "dp", axis=0, tiled=True)
    q_full = lax.all_gather(q_weight[0], "dp", axis=0, tiled=True)
    o_full = lax.all_gather(o_weight[0], "dp", axis=0, tiled=True)

    x_blocks = jnp.stack([across(inputs[0], k) for k in range(experts)], axis=1)
    x_all = x_blocks.reshape(MICRO, span, width).astype(f32)
    a_all = (x_all * inverse_rms(x_all) * gain_1).astype(bf16)

    def stage_columns(weight):
        split = weight.reshape(weight.shape[0], stages, part)
        got = [along(pick(split, (stage + k) % stages, 1), k) for k in range(stages)]
        mine = jnp.stack(got)[stage_order]
        theirs = partner(mine)
        first = jnp.where(core == 0, mine, theirs)
        second = jnp.where(core == 0, theirs, mine)
        return jnp.stack([first, second], axis=1).reshape(width, part)

    gate_in, up_in, _ = lax.optimization_barrier((gate_weight[0], up_weight[0], q_full))
    gate_w, up_w = stage_columns(gate_in), stage_columns(up_in)
    down_other = partner(down_weight[0])
    down_w = jnp.concatenate(
        [
            jnp.where(core == 0, down_weight[0], down_other),
            jnp.where(core == 0, down_other, down_weight[0]),
        ]
    )

    token = jnp.arange(tokens, dtype=jnp.int32)
    pick_a = selection((routes_a == own).any(-1).astype(f32), slots)
    place_a = jnp.einsum("kmst,t->kms", pick_a, token.astype(bf16), preferred_element_type=f32)
    other_a = jnp.einsum(
        "kmst,kmt->kms",
        pick_a,
        (routes_a.sum(-1) - own).astype(bf16),
        preferred_element_type=f32,
    ).astype(jnp.int32)
    query_pos = (
        place_a.astype(jnp.int32)
        + xor_order[:, None, None] * tokens
        + jnp.arange(MICRO, dtype=jnp.int32)[None, :, None] * span
    )
    home_a = selection(
        (routes_a[0][None] == xor_order[:, None, None, None]).any(-1).astype(f32), slots
    )
    home_m = selection(
        (routes_m[:, 0][:, None] == xor_order[None, :, None, None, None]).any(-1).astype(f32),
        slots,
    )
    pick_m = selection((routes_m == own).any(-1).astype(f32), slots)
    other_m = jnp.einsum(
        "kjmst,kjmt->jkms",
        pick_m,
        (routes_m.sum(-1) - own).astype(bf16),
        preferred_element_type=f32,
    ).astype(jnp.int32)

    def pair_gates(rows_low, router_cols, other):
        logits = mm(rows_low, router_cols)
        column = jnp.arange(experts, dtype=jnp.int32)[None, :]
        mine = (column == own).astype(f32)
        theirs = (column == other[:, None]).astype(f32)
        turn = mine - theirs
        gate = jax.nn.sigmoid(jnp.sum(logits * turn, axis=1, keepdims=True))
        rest = jax.nn.sigmoid(-jnp.sum(logits * turn, axis=1, keepdims=True))
        return gate, rest, turn

    place = jnp.stack([own, pic_start[0]]).astype(jnp.int32)
    sequence_pos = (
        jnp.arange(MICRO, dtype=jnp.int32)[:, None] * span
        + (jnp.arange(span, dtype=jnp.int32) ^ (own * tokens))[None, :]
    )
    key_cos, key_sin = rope_tables(sequence_pos)
    plain_cos, plain_sin = jnp.ones_like(key_cos), jnp.zeros_like(key_sin)
    key_cos = jnp.stack([key_cos, plain_cos], axis=1)
    key_sin = jnp.stack([key_sin, plain_sin], axis=1)
    query_cos, query_sin = rope_tables(query_pos)

    kv_all = []
    for m in range(MICRO):
        mine = project_kv(a_all[m], kv_cols, key_cos[m], key_sin[m])
        kv_all.append(jnp.stack([across(mine, k) for k in range(experts)]))

    kept = {}
    for m in ORDER:
        a_blocks = a_all[m].reshape(experts, tokens, width)
        a_pairs = jnp.einsum(
            "kst,ktd->ksd", pick_a[:, m], a_blocks, preferred_element_type=f32
        ).astype(bf16)
        a_pairs = a_pairs.reshape(routed, width)
        gate, rest, turn = pair_gates(a_pairs, router_a, other_a[:, m].reshape(-1))
        q_cos = query_cos[:, m].reshape(routed, HSZ)
        q_sin = query_sin[:, m].reshape(routed, HSZ)
        q_pos = query_pos[:, m].reshape(routed, 1)
        mixed, q_rot, peak = attend(
            mm(a_pairs, q_full), q_cos, q_sin, q_pos, kv_all[: m + 1], place, tokens
        )
        rows = mm(mixed, o_full)
        kept[m] = (a_pairs, gate, rest, turn, q_cos, q_sin, q_pos, mixed, q_rot, peak, rows)

    g_in, _ = lax.optimization_barrier((cotangent[0], gate_w))
    middles, inverses, routed_rows, routed_grads = {}, {}, {}, {}
    for m in ORDER:
        gated = (kept[m][1] * kept[m][-1]).astype(bf16).reshape(experts, slots, width)
        back = jnp.stack([across(gated[k], k) for k in range(experts)])
        summed = jnp.einsum("kst,ksd->td", home_a[:, m], back, preferred_element_type=f32)
        middle = inputs[0, m].astype(f32) + summed
        inverse = inverse_rms(middle)
        b_low = (middle * inverse * gain_2).astype(bf16)
        middles[m], inverses[m] = middle, inverse

        def dispatch(low):
            stack = jnp.stack([along(low, k) for k in range(stages)])
            sent = []
            for j in range(experts):
                block = jnp.einsum(
                    "kst,ktd->ksd", home_m[:, j, m], stack, preferred_element_type=f32
                ).astype(bf16)
                sent.append(across(block.reshape(stages * slots, width), j))
            return jnp.concatenate(sent)

        routed_rows[m] = dispatch(b_low)
        routed_grads[m] = dispatch(g_in[m])

    def collect(rows, m):
        rows = rows.reshape(experts, stages, slots, width)
        back = jnp.stack([across(rows[j], j) for j in range(experts)])
        summed = jnp.einsum(
            "kjst,jksd->ktd", home_m[:, :, m], back, preferred_element_type=f32
        )
        total = summed[0]
        for k in range(1, stages):
            total = total + along(summed[k].astype(bf16), -k).astype(f32)
        return total

    gate_grad = up_grad = down_grad = None
    router_m_grad = jnp.zeros((width, experts), f32)
    out_rows, d_bs = {}, {}
    for m in ORDER:
        rows, grads = routed_rows[m], routed_grads[m]
        gate, rest, turn = pair_gates(rows, router_m, other_m[:, :, m].reshape(-1))
        d_rows = (gate * grads.astype(f32)).astype(bf16)
        gate_pre, up_pre = mm(rows, gate_w), mm(rows, up_w)
        sigma = jax.nn.sigmoid(gate_pre)
        low = (gate_pre * sigma * up_pre).astype(bf16)
        result = mm(low, down_w)
        out_rows[m] = (gate * result).astype(bf16)
        d_gate_value = jnp.sum(grads.astype(f32) * result, axis=1, keepdims=True)
        d_logits = (gate * rest * d_gate_value) * turn
        d_low = mm_t(d_rows, down_w)
        d_gate = (d_low * up_pre * sigma * (1.0 + gate_pre * (1.0 - sigma))).astype(bf16)
        d_up = (d_low * gate_pre * sigma).astype(bf16)
        d_b = (
            mm_t(d_gate, gate_w)
            + mm_t(d_up, up_w)
            + exact(d_logits, router_m.astype(f32), ((1,), (1,)))
        ).astype(bf16)
        d_bs[m] = collect(d_b, m)
        router_m_grad = router_m_grad + exact(rows.astype(f32), d_logits, ((0,), (0,)))
        here = (t_mm(rows, d_gate), t_mm(rows, d_up), t_mm(low, d_rows))
        if gate_grad is None:
            gate_grad, up_grad, down_grad = here
        else:
            gate_grad, up_grad, down_grad = (
                gate_grad + here[0],
                up_grad + here[1],
                down_grad + here[2],
            )

    def stage_rows(grad):
        split = grad.reshape(stages, 2, width // dp_size, part)
        mine = pick(split, core, 1)
        other = partner(pick(split, 1 - core, 1).astype(bf16))
        total = (mine + other.astype(f32)).astype(bf16)
        got = jnp.stack([along(pick(total, (stage + k) % stages), k) for k in range(stages)])
        got = got[stage_order].astype(f32)
        return jnp.concatenate([got[s] for s in range(stages)], axis=1)[None]

    gate_share, up_share = stage_rows(gate_grad), stage_rows(up_grad)
    down_split = down_grad.reshape(2, part // 2, width)
    down_share = (
        pick(down_split, core) + partner(pick(down_split, 1 - core).astype(bf16)).astype(f32)
    )[None]

    outs = [None] * MICRO
    for m in ORDER:
        outs[m] = middles[m] + collect(out_rows[m], m)
    out_act = jnp.stack(outs)[None].astype(bf16)

    gain_2_grad = jnp.zeros((width,), f32)
    router_a_grad = jnp.zeros((width, experts), f32)
    d_middles, d_queries, d_attn, pair_back, kv_grads = {}, {}, {}, {}, []
    for m in ORDER:
        a_pairs, gate, rest, turn, q_cos, q_sin, q_pos, mixed, q_rot, peak, attn = kept[m]
        norm_grad, gain_part = norm_back(middles[m], inverses[m], gain_2, d_bs[m])
        gain_2_grad = gain_2_grad + gain_part
        d_middle = cotangent[0, m].astype(f32) + norm_grad
        d_middles[m] = d_middle
        sent = jnp.einsum(
            "kst,td->ksd", home_a[:, m], d_middle.astype(bf16), preferred_element_type=f32
        ).astype(bf16)
        got = jnp.concatenate([across(sent[k], k) for k in range(experts)]).astype(f32)
        d_attn[m] = (gate * got).astype(bf16)
        d_gate_value = jnp.sum(got * attn, axis=1, keepdims=True)
        d_logits = (gate * rest * d_gate_value) * turn
        d_mixed = mm_t(d_attn[m], o_full).astype(bf16)
        d_queries[m], *fresh = attend_back(
            q_rot, d_mixed, q_cos, q_sin, q_pos, kv_all[: m + 1], kv_grads[: m + 1], place, tokens
        )
        kv_grads = list(fresh) + list(kv_grads[m + 1 :])
        d_pair = mm_t(d_queries[m], q_full) + exact(
            d_logits, router_a.astype(f32), ((1,), (1,))
        )
        pair_back[m] = jnp.einsum(
            "kst,ksd->ktd",
            pick_a[:, m],
            d_pair.astype(bf16).reshape(experts, slots, width),
            preferred_element_type=f32,
        )
        router_a_grad = router_a_grad + exact(a_pairs.astype(f32), d_logits, ((0,), (0,)))

    def scattered(grad):
        return lax.psum_scatter(grad.astype(bf16), "dp", scatter_dimension=0, tiled=True)

    def both(fn):
        return fn(ORDER[0]) + fn(ORDER[1])

    o_share = scattered(both(lambda m: t_mm(kept[m][7], d_attn[m]))).astype(f32)[None]
    q_share = scattered(both(lambda m: t_mm(kept[m][0], d_queries[m]))).astype(f32)[None]

    kv_grad = jnp.zeros((width, 2 * group), f32)
    gain_1_grad = jnp.zeros((width,), f32)
    grad_x = [None] * MICRO
    for m in ORDER:
        d_kv = sum_kv_grads(
            [across(kv_grads[m][k], k) for k in range(experts)], key_cos[m], key_sin[m]
        )
        kv_grad = kv_grad + t_mm(a_all[m], d_kv)
        d_a = mm_t(d_kv, kv_cols).reshape(experts, tokens, width) + pair_back[m]
        total = d_a[0]
        for k in range(1, experts):
            total = total + across(d_a[k].astype(bf16), k).astype(f32)
        values = inputs[0, m].astype(f32)
        d_x, gain_part = norm_back(values, inverse_rms(values), gain_1, total)
        gain_1_grad = gain_1_grad + gain_part
        grad_x[m] = d_middles[m] + d_x
    grad_x = jnp.stack(grad_x)[None]
    kv_mine = scattered(kv_grad).reshape(experts, rows_each, 2 * group)
    kv_got = [across(pick(kv_mine, own ^ k), k) for k in range(experts)]
    kv_got = jnp.stack(kv_got)[xor_order].reshape(experts, rows_each, 2, group)
    kv_share = kv_got.transpose(1, 2, 0, 3).reshape(rows_each, 2 * inner).astype(f32)

    tail = jnp.concatenate(
        [router_a_grad, router_m_grad, gain_1_grad[:, None], gain_2_grad[:, None]], axis=1
    )
    tail = lax.psum_scatter(tail, "dp", scatter_dimension=0, tiled=True)
    tail = lax.psum_scatter(tail, "expert", scatter_dimension=0, tiled=True)
    router_share, gains_share = tail[:, : 2 * experts], tail[:, 2 * experts :]

    largest = jnp.maximum(kept[0][9], kept[1][9])[:, 0, :]
    hop = 1
    while hop < dp_size:
        largest = jnp.maximum(
            largest, lax.ppermute(largest, "dp", [(j, j ^ hop) for j in range(dp_size)])
        )
        hop *= 2
    largest = jnp.stack([across(largest, k) for k in range(experts)])
    ratio = logit_cap / jnp.maximum(largest, logit_cap)
    root_q = jnp.sqrt(ratio[0]).reshape(1, inner)
    root_k = jnp.sqrt(jnp.min(ratio, axis=0)).reshape(1, inner)
    clipped_q = (q_weight.astype(f32) * root_q[None]).astype(bf16)
    clipped_key = (kv_weight[:, :inner].astype(f32) * root_k).astype(bf16)
    return (
        out_act,
        grad_x,
        kv_share,
        router_share,
        gains_share,
        q_share,
        o_share,
        gate_share,
        up_share,
        down_share,
        clipped_q,
        clipped_key,
    )


def solution(mesh):
    tokens4 = P("dp", None, "expert", None)
    rows2 = P(("dp", "expert"), None)
    weights3 = P("expert", "dp", None)
    return jax.shard_map(
        per_device,
        mesh=mesh,
        in_specs=(tokens4,) * 3 + (P("dp"),) + (rows2,) * 3 + (weights3,) * 5 + (tokens4,),
        out_specs=(tokens4,) * 2 + (rows2,) * 3 + (weights3,) * 6 + (rows2,),
        check_vma=False,
    )
```

```python
import math

import jax
import jax.numpy as jnp
from jax import lax
from jax.experimental import pallas as pl
from jax.experimental.pallas import tpu as pltpu
from jax.sharding import PartitionSpec as P

HEADS = 16
HSZ = 128
TOPK = 2
PIC = 256
MICRO = 2
ORDER = (1, 0)

norm_eps = 1e-06
logit_cap = 8.0
masked_low = -1e30
bf16 = jnp.bfloat16
f32 = jnp.float32


def mm(left, right):
    return jnp.dot(left, right, preferred_element_type=f32)


def mm_t(left, right):
    return lax.dot_general(left, right, (((1,), (1,)), ((), ())), preferred_element_type=f32)


def t_mm(left, right):
    return lax.dot_general(left, right, (((0,), (0,)), ((), ())), preferred_element_type=f32)


def rope_tables(positions):
    half = HSZ // 2
    freq = jnp.exp(jnp.arange(half, dtype=f32) * (-math.log(10000.0) / half))
    angles = positions.astype(f32)[..., None] * freq
    cosine, sine = jnp.cos(angles), jnp.sin(angles)
    return (
        jnp.concatenate([cosine, cosine], axis=-1),
        jnp.concatenate([-sine, sine], axis=-1),
    )


def inverse_rms(values):
    return lax.rsqrt(jnp.mean(values * values, axis=-1, keepdims=True) + norm_eps)


def selection(hot, slots):
    tokens = hot.shape[-1]
    before = jnp.triu(jnp.ones((tokens, tokens), bf16), 1)
    rank = jnp.dot(hot.astype(bf16), before, preferred_element_type=f32)
    slot = jnp.arange(slots, dtype=jnp.int32)[:, None]
    taken = (rank.astype(jnp.int32)[..., None, :] == slot) & (hot[..., None, :] > 0)
    return taken.astype(bf16)


def full_spec(shape):
    return pl.BlockSpec(shape, lambda *_: (0,) * len(shape))


def work(flops, moved, exps=0):
    return pl.CostEstimate(flops=flops, bytes_accessed=moved, transcendentals=exps)


def kv_kernel(a_ref, w_ref, cos_ref, sin_ref, o_ref):
    got = jnp.dot(a_ref[0], w_ref[...], preferred_element_type=f32)
    cosine, sine = cos_ref[0, 0], sin_ref[0, 0]
    for part in range(got.shape[1] // HSZ):
        piece = got[:, part * HSZ : (part + 1) * HSZ]
        turned = piece * cosine + pltpu.roll(piece, HSZ // 2, 1) * sine
        o_ref[0, 0, :, part * HSZ : (part + 1) * HSZ] = turned.astype(bf16)


def project_kv(a_all, kv_cols, cosine, sine):
    micro, rows, width = a_all.shape
    group = kv_cols.shape[1] // 2
    step = min(256, group)
    per = group // step
    table = pl.BlockSpec((1, 1, rows, HSZ), lambda m, g: (m, g // per, 0, 0))
    return pl.pallas_call(
        kv_kernel,
        grid=(micro, 2 * per),
        in_specs=[
            pl.BlockSpec((1, rows, width), lambda m, g: (m, 0, 0)),
            pl.BlockSpec((width, step), lambda m, g: (0, g)),
            table,
            table,
        ],
        out_specs=pl.BlockSpec((1, 1, rows, step), lambda m, g: (m, g // per, 0, g % per)),
        out_shape=jax.ShapeDtypeStruct((micro, 2, rows, group), bf16),
        name="project_kv",
        cost_estimate=work(4 * micro * rows * width * group, 2 * (micro * rows * width + 2 * width * group + 2 * micro * rows * group)),
    )(a_all, kv_cols, cosine, sine)


def probabilities(query, keys, start, qpos, micro):
    parts = []
    for m in range(micro + 1):
        got = lax.dot_general(
            query, keys[m], (((1,), (1,)), ((), ())), preferred_element_type=f32
        ) * (HSZ**-0.5)
        if m == micro:
            kpos = micro * got.shape[1] + lax.broadcasted_iota(jnp.int32, got.shape, 1)
            inside_q = (qpos >= start) & (qpos < start + PIC)
            inside_k = (kpos >= start) & (kpos < start + PIC)
            keep = (kpos <= qpos) | (inside_q & inside_k)
            got = jnp.where(keep, got, masked_low)
        parts.append(got)
    peak = parts[0].max(axis=1, keepdims=True)
    for got in parts[1:]:
        peak = jnp.maximum(peak, got.max(axis=1, keepdims=True))
    lifted = [jnp.exp(got - peak) for got in parts]
    total = lifted[0].sum(axis=1, keepdims=True)
    for got in lifted[1:]:
        total = total + got.sum(axis=1, keepdims=True)
    scale = 1.0 / total
    return [got * scale for got in lifted], peak


def project_q(a_pairs, q_full, cosine, sine, micro, experts):
    total, width = a_pairs.shape
    inner = q_full.shape[1]
    group = inner // experts
    step = min(256, group)
    per = group // step
    rows = total // micro

    def kernel(a_ref, w_ref, cos_ref, sin_ref, o_ref):
        got = jnp.dot(a_ref[...], w_ref[...], preferred_element_type=f32)
        for h in range(step // HSZ):
            lanes = slice(h * HSZ, (h + 1) * HSZ)
            piece = got[:, lanes]
            turned = piece * cos_ref[...] + pltpu.roll(piece, HSZ // 2, 1) * sin_ref[...]
            o_ref[:, 0, :, lanes] = turned.astype(bf16).reshape(micro, rows, HSZ)

    return pl.pallas_call(
        kernel,
        grid=(inner // step,),
        in_specs=[
            full_spec((total, width)),
            pl.BlockSpec((width, step), lambda g: (0, g)),
            full_spec((total, HSZ)),
            full_spec((total, HSZ)),
        ],
        out_specs=pl.BlockSpec((micro, 1, rows, step), lambda g: (0, g // per, 0, g % per)),
        out_shape=jax.ShapeDtypeStruct((micro, experts, rows, group), bf16),
        name="project_q",
        cost_estimate=work(2 * total * width * inner, 2 * (total * width + width * inner + total * inner)),
    )(a_pairs, q_full, cosine, sine)


def attend(query, qpos, kvs, start):
    micro = len(kvs) - 1
    experts, rows, group = query.shape
    hg = group // HSZ
    keys_seen = sum(kv.shape[1] for kv in kvs)

    def kernel(start_ref, q_ref, pos_ref, *rest):
        kv_refs, (mixed_ref, peak_ref) = rest[:-2], rest[-2:]
        for h in range(hg):
            lanes = slice(h * HSZ, (h + 1) * HSZ)
            probs, peak = probabilities(
                q_ref[0, :, lanes],
                [r[0, :, lanes] for r in kv_refs],
                start_ref[0],
                pos_ref[0],
                micro,
            )
            mixed = jnp.zeros((rows, HSZ), f32)
            for m in range(micro + 1):
                mixed = mixed + jnp.dot(
                    probs[m].astype(bf16), kv_refs[m][1, :, lanes], preferred_element_type=f32
                )
            mixed_ref[0, :, lanes] = mixed.astype(bf16)
            peak_ref[0, h] = jnp.full(peak_ref.shape[2:], jnp.max(peak), f32)

    return pl.pallas_call(
        kernel,
        grid_spec=pltpu.PrefetchScalarGridSpec(
            num_scalar_prefetch=1,
            grid=(experts,),
            in_specs=[
                pl.BlockSpec((1, rows, group), lambda g, s: (g, 0, 0)),
                pl.BlockSpec((1, rows, 1), lambda g, s: (g, 0, 0)),
            ]
            + [full_spec(kv.shape) for kv in kvs],
            out_specs=[
                pl.BlockSpec((1, rows, group), lambda g, s: (g, 0, 0)),
                pl.BlockSpec((1, hg, 8, 128), lambda g, s: (g, 0, 0, 0)),
            ],
        ),
        out_shape=[
            jax.ShapeDtypeStruct((experts, rows, group), bf16),
            jax.ShapeDtypeStruct((experts, hg, 8, 128), f32),
        ],
        name="attend",
        cost_estimate=work(4 * experts * rows * group * keys_seen, 4 * experts * rows * group, experts * rows * hg * keys_seen),
    )(start, query, qpos, *kvs)


def attend_back(query, d_mixed, cosine, sine, qpos, kvs, key_cos, key_sin, later, start):
    micro = len(kvs) - 1
    experts, rows, group = query.shape
    keys = kvs[0].shape[1]
    hg = group // HSZ
    held = len(later)

    def kernel(start_ref, q_ref, dm_ref, cos_ref, sin_ref, pos_ref, kcos_ref, ksin_ref, *rest):
        kv_refs = rest[: micro + 1]
        later_refs = rest[micro + 1 : micro + 1 + held]
        dq_ref, dkv_ref = rest[micro + 1 + held : micro + 3 + held]
        sums = rest[micro + 3 + held :]
        step = pl.program_id(0)

        @pl.when(step == 0)
        def _():
            for m in range(micro + 1):
                if held and m == micro:
                    sums[m][...] = later_refs[0][...]
                else:
                    sums[m][...] = jnp.zeros(sums[m].shape, f32)

        for h in range(hg):
            lanes = slice(h * HSZ, (h + 1) * HSZ)
            q, dm = q_ref[0, :, lanes], dm_ref[0, :, lanes]
            probs, _ = probabilities(
                q, [r[0, :, lanes] for r in kv_refs], start_ref[0], pos_ref[0], micro
            )
            d_probs = [
                lax.dot_general(
                    dm, r[1, :, lanes], (((1,), (1,)), ((), ())), preferred_element_type=f32
                )
                for r in kv_refs
            ]
            total = jnp.sum(d_probs[0] * probs[0], axis=1, keepdims=True)
            for m in range(1, micro + 1):
                total = total + jnp.sum(d_probs[m] * probs[m], axis=1, keepdims=True)
            d_q = jnp.zeros((rows, HSZ), f32)
            for m in range(micro + 1):
                d_scores = (probs[m] * (d_probs[m] - total)).astype(bf16)
                d_q = d_q + jnp.dot(d_scores, kv_refs[m][0, :, lanes], preferred_element_type=f32)
                sums[m][0, :, lanes] += lax.dot_general(
                    d_scores, q, (((0,), (0,)), ((), ())), preferred_element_type=f32
                )
                sums[m][1, :, lanes] += lax.dot_general(
                    probs[m].astype(bf16), dm, (((0,), (0,)), ((), ())), preferred_element_type=f32
                )
            d_q = d_q * (HSZ**-0.5)
            back = d_q * cos_ref[0] - pltpu.roll(d_q, HSZ // 2, 1) * sin_ref[0]
            dq_ref[0, :, lanes] = back.astype(bf16)

        @pl.when(step == experts - 1)
        def _():
            for h in range(hg):
                lanes = slice(h * HSZ, (h + 1) * HSZ)
                d_k = sums[micro][0, :, lanes] * (HSZ**-0.5)
                back = d_k * kcos_ref[...] - pltpu.roll(d_k, HSZ // 2, 1) * ksin_ref[...]
                dkv_ref[:, lanes] = back.astype(bf16)
                dkv_ref[:, group + h * HSZ : group + (h + 1) * HSZ] = sums[micro][
                    1, :, lanes
                ].astype(bf16)

    block = pl.BlockSpec((1, rows, group), lambda g, s: (g, 0, 0))
    table = pl.BlockSpec((1, rows, HSZ), lambda g, s: (g, 0, 0))
    sums_shape = jax.ShapeDtypeStruct((2, keys, group), f32)
    return pl.pallas_call(
        kernel,
        grid_spec=pltpu.PrefetchScalarGridSpec(
            num_scalar_prefetch=1,
            grid=(experts,),
            in_specs=[block, block, table, table]
            + [pl.BlockSpec((1, rows, 1), lambda g, s: (g, 0, 0))]
            + [full_spec((keys, HSZ))] * 2
            + [full_spec((2, keys, group))] * (micro + 1 + held),
            out_specs=[block, full_spec((keys, 2 * group))]
            + [full_spec((2, keys, group))] * micro,
            scratch_shapes=[pltpu.VMEM((2, keys, group), f32)],
        ),
        out_shape=[
            jax.ShapeDtypeStruct((experts, rows, group), bf16),
            jax.ShapeDtypeStruct((keys, 2 * group), bf16),
        ]
        + [sums_shape] * micro,
        name="attend_back",
        cost_estimate=work(10 * experts * rows * group * keys * (micro + 1), 12 * experts * rows * group, experts * rows * hg * keys * (micro + 1)),
    )(start, query, d_mixed, cosine, sine, qpos, key_cos, key_sin, *kvs, *later)


def join_groups(got_ref, flat_ref):
    experts, _, group = got_ref.shape
    for e in range(experts):
        flat_ref[:, e * group : (e + 1) * group] = got_ref[e]


def project_o(mixed, o_full, gate):
    experts, rows, group = mixed.shape
    inner, width = o_full.shape
    step = min(512, width)

    def kernel(mixed_ref, o_ref, gate_ref, attn_ref, gated_ref, flat_ref):
        @pl.when(pl.program_id(0) == 0)
        def _():
            join_groups(mixed_ref, flat_ref)

        got = jnp.dot(flat_ref[...], o_ref[...], preferred_element_type=f32)
        attn_ref[...] = got.astype(bf16)
        gated_ref[...] = (got * gate_ref[...]).astype(bf16)

    column = pl.BlockSpec((rows, step), lambda g: (0, g))
    return pl.pallas_call(
        kernel,
        grid=(width // step,),
        in_specs=[
            full_spec(mixed.shape),
            pl.BlockSpec((inner, step), lambda g: (0, g)),
            full_spec((rows, 1)),
        ],
        out_specs=[column, column, full_spec((rows, inner))],
        out_shape=[
            jax.ShapeDtypeStruct((rows, width), bf16),
            jax.ShapeDtypeStruct((rows, width), bf16),
            jax.ShapeDtypeStruct((rows, inner), bf16),
        ],
        name="project_o",
        cost_estimate=work(2 * rows * inner * width, 2 * (inner * width + 4 * rows * width)),
    )(mixed, o_full, gate)


def back_o(got, attn, gate, rest, turn, o_full, experts):
    rows, width = got.shape
    inner = o_full.shape[0]
    group = inner // experts
    lanes = turn.shape[1]

    def kernel(got_ref, attn_ref, gate_ref, rest_ref, turn_ref, o_ref, da_ref, dm_ref, dl_ref):
        @pl.when(pl.program_id(0) == 0)
        def _():
            upstream = got_ref[...].astype(f32)
            da_ref[...] = (gate_ref[...] * upstream).astype(bf16)
            value = jnp.sum(upstream * attn_ref[...].astype(f32), axis=1, keepdims=True)
            d_logits = (gate_ref[...] * rest_ref[...] * value) * turn_ref[...]
            high = d_logits.astype(bf16)
            dl_ref[:, :lanes] = high
            dl_ref[:, lanes:] = (d_logits - high.astype(f32)).astype(bf16)

        dm_ref[0] = lax.dot_general(
            da_ref[...], o_ref[...], (((1,), (1,)), ((), ())), preferred_element_type=f32
        ).astype(bf16)

    return pl.pallas_call(
        kernel,
        grid=(experts,),
        in_specs=[full_spec((rows, width))] * 2
        + [full_spec((rows, 1))] * 2
        + [full_spec((rows, lanes)), pl.BlockSpec((group, width), lambda g: (g, 0))],
        out_specs=[
            full_spec((rows, width)),
            pl.BlockSpec((1, rows, group), lambda g: (g, 0, 0)),
            full_spec((rows, 2 * lanes)),
        ],
        out_shape=[
            jax.ShapeDtypeStruct((rows, width), bf16),
            jax.ShapeDtypeStruct((experts, rows, group), bf16),
            jax.ShapeDtypeStruct((rows, 2 * lanes), bf16),
        ],
        name="back_o",
        cost_estimate=work(2 * rows * inner * width, 2 * (inner * width + 4 * rows * width)),
    )(got, attn, gate, rest, turn, o_full)


def back_q(d_query, q_full, d_logits, router):
    experts, rows, group = d_query.shape
    width, inner = q_full.shape
    step = min(512, width)
    lanes = router.shape[1]

    def kernel(dq_ref, q_ref, dl_ref, router_ref, pair_ref, flat_ref):
        @pl.when(pl.program_id(0) == 0)
        def _():
            join_groups(dq_ref, flat_ref)

        dims = (((1,), (1,)), ((), ()))
        got = lax.dot_general(flat_ref[...], q_ref[...], dims, preferred_element_type=f32)
        for half in range(2):
            got = got + lax.dot_general(
                dl_ref[:, half * lanes : (half + 1) * lanes],
                router_ref[...],
                dims,
                preferred_element_type=f32,
            )
        pair_ref[...] = got.astype(bf16)

    return pl.pallas_call(
        kernel,
        grid=(width // step,),
        in_specs=[
            full_spec(d_query.shape),
            pl.BlockSpec((step, inner), lambda g: (g, 0)),
            full_spec((rows, 2 * lanes)),
            pl.BlockSpec((step, lanes), lambda g: (g, 0)),
        ],
        out_specs=[pl.BlockSpec((rows, step), lambda g: (0, g)), full_spec((rows, inner))],
        out_shape=[
            jax.ShapeDtypeStruct((rows, width), bf16),
            jax.ShapeDtypeStruct((rows, inner), bf16),
        ],
        name="back_q",
        cost_estimate=work(2 * rows * inner * width, 2 * (inner * width + 4 * rows * width)),
    )(d_query, q_full, d_logits, router)


def token_back(d_kv, kv_cols, d_pair, pick):
    span, line = d_kv.shape
    width = kv_cols.shape[0]
    experts, slots, tokens = pick.shape
    step = min(512, width)

    def kernel(dkv_ref, kv_ref, pair_ref, pick_ref, o_ref):
        got = lax.dot_general(
            dkv_ref[...], kv_ref[...], (((1,), (1,)), ((), ())), preferred_element_type=f32
        )
        for e in range(experts):
            extra = lax.dot_general(
                pick_ref[e],
                pair_ref[e * slots : (e + 1) * slots, :],
                (((0,), (0,)), ((), ())),
                preferred_element_type=f32,
            )
            o_ref[e] = (got[e * tokens : (e + 1) * tokens] + extra).astype(bf16)

    return pl.pallas_call(
        kernel,
        grid=(width // step,),
        in_specs=[
            full_spec((span, line)),
            pl.BlockSpec((step, line), lambda g: (g, 0)),
            pl.BlockSpec((experts * slots, step), lambda g: (0, g)),
            full_spec(pick.shape),
        ],
        out_specs=pl.BlockSpec((experts, tokens, step), lambda g: (0, 0, g)),
        out_shape=jax.ShapeDtypeStruct((experts, tokens, width), bf16),
        name="token_back",
        cost_estimate=work(2 * span * line * width, 2 * (line * width + 2 * span * width)),
    )(d_kv, kv_cols, d_pair, pick)


def input_back_kernel(got_ref, x_ref, gain_ref, dm_ref, gx_ref, dg_ref):
    d_a = got_ref[0].astype(f32)
    for e in range(1, got_ref.shape[0]):
        d_a = d_a + got_ref[e].astype(f32)
    x = x_ref[...].astype(f32)
    inverse = lax.rsqrt(jnp.mean(x * x, axis=1, keepdims=True) + norm_eps)
    scaled = d_a * gain_ref[...]
    dg_ref[...] = jnp.sum(d_a * (x * inverse), axis=0, keepdims=True)
    mean = jnp.mean(scaled * x, axis=1, keepdims=True)
    gx_ref[...] = dm_ref[...] + (inverse * scaled - x * (inverse * inverse * inverse * mean))


def input_back(got, x, gain, d_middle):
    tokens, width = x.shape
    return pl.pallas_call(
        input_back_kernel,
        out_shape=[
            jax.ShapeDtypeStruct((tokens, width), f32),
            jax.ShapeDtypeStruct((1, width), f32),
        ],
        name="input_back",
        cost_estimate=work(10 * tokens * width, 20 * tokens * width),
    )(got, x, gain, d_middle)


def combine_kernel(back_ref, pick_ref, x_ref, gain_ref, middle_ref, inv_ref, b_ref):
    summed = lax.dot_general(
        pick_ref[...], back_ref[...], (((0,), (0,)), ((), ())), preferred_element_type=f32
    )
    middle = x_ref[...].astype(f32) + summed
    inverse = lax.rsqrt(jnp.mean(middle * middle, axis=1, keepdims=True) + norm_eps)
    middle_ref[...] = middle
    inv_ref[...] = inverse
    b_ref[...] = (middle * inverse * gain_ref[...]).astype(bf16)


def combine(back, pick, x, gain):
    tokens, width = x.shape
    return pl.pallas_call(
        combine_kernel,
        out_shape=[
            jax.ShapeDtypeStruct((tokens, width), f32),
            jax.ShapeDtypeStruct((tokens, 1), f32),
            jax.ShapeDtypeStruct((tokens, width), bf16),
        ],
        name="combine",
        cost_estimate=work(2 * back.shape[0] * tokens * width, 2 * back.shape[0] * width + 8 * tokens * width),
    )(back, pick, x, gain)


def middle_back_kernel(*refs):
    pieces = refs[:-8]
    middle_ref, inv_ref, cot_ref, gain_ref, pick_ref, dm_ref, dg_ref, rows_ref = refs[-8:]
    d_b = pieces[0][...].astype(f32)
    for piece in pieces[1:]:
        d_b = d_b + piece[...].astype(f32)
    middle, inverse = middle_ref[...], inv_ref[...]
    scaled = d_b * gain_ref[...]
    dg_ref[...] = jnp.sum(d_b * (middle * inverse), axis=0, keepdims=True)
    mean = jnp.mean(scaled * middle, axis=1, keepdims=True)
    d_middle = cot_ref[...].astype(f32) + (
        inverse * scaled - middle * (inverse * inverse * inverse * mean)
    )
    dm_ref[...] = d_middle
    rows_ref[...] = jnp.dot(
        pick_ref[...], d_middle.astype(bf16), preferred_element_type=f32
    ).astype(bf16)


def middle_back(pieces, middle, inverse, cot, gain, pick):
    tokens, width = middle.shape
    return pl.pallas_call(
        middle_back_kernel,
        out_shape=[
            jax.ShapeDtypeStruct((tokens, width), f32),
            jax.ShapeDtypeStruct((1, width), f32),
            jax.ShapeDtypeStruct((pick.shape[0], width), bf16),
        ],
        name="middle_back",
        cost_estimate=work(2 * pick.shape[0] * tokens * width, 2 * pick.shape[0] * width + 20 * tokens * width),
    )(*pieces, middle, inverse, cot, gain, pick)


def dispatch(blocks, pick):
    stages, pairs, tokens = pick.shape
    width = blocks[0].shape[1]
    step = min(512, width)

    def kernel(pick_ref, *refs):
        for k in range(stages):
            refs[-1][:, k] = (
                jnp.dot(pick_ref[k], refs[k][...], preferred_element_type=f32)
                .astype(bf16)
                .reshape(refs[-1].shape[0], refs[-1].shape[2], step)
            )

    return lambda experts: pl.pallas_call(
        kernel,
        grid=(width // step,),
        in_specs=[full_spec(pick.shape)]
        + [pl.BlockSpec((tokens, step), lambda g: (0, g)) for _ in blocks],
        out_specs=pl.BlockSpec((experts, stages, pairs // experts, step), lambda g: (0, 0, 0, g)),
        out_shape=jax.ShapeDtypeStruct((experts, stages, pairs // experts, width), bf16),
        name="dispatch",
        cost_estimate=work(2 * stages * pairs * tokens * width, 2 * stages * (pairs + tokens) * width),
    )(pick, *blocks)


def collect(rows, pick, order):
    experts, stages, slots, width = rows.shape
    tokens = pick.shape[2]

    def kernel(order_ref, pick_ref, rows_ref, o_ref):
        gathered = rows_ref[...].reshape(experts * slots, width)
        o_ref[0] = lax.dot_general(
            pick_ref[0], gathered, (((0,), (0,)), ((), ())), preferred_element_type=f32
        ).astype(bf16)

    return pl.pallas_call(
        kernel,
        grid_spec=pltpu.PrefetchScalarGridSpec(
            num_scalar_prefetch=1,
            grid=(stages,),
            in_specs=[
                pl.BlockSpec((1, experts * slots, tokens), lambda k, o: (k, 0, 0)),
                pl.BlockSpec((experts, 1, slots, width), lambda k, o: (0, k, 0, 0)),
            ],
            out_specs=pl.BlockSpec((1, tokens, width), lambda k, o: (o[k], 0, 0)),
        ),
        out_shape=jax.ShapeDtypeStruct((stages, tokens, width), bf16),
        name="collect",
        cost_estimate=work(2 * stages * experts * slots * tokens * width, 2 * stages * (experts * slots + tokens) * width),
    )(order, pick, rows)


def collect_each(rows, pick):
    experts, stages, slots, width = rows.shape
    tokens = pick.shape[2]

    def kernel(pick_ref, rows_ref, *outs):
        gathered = rows_ref[...].reshape(experts * slots, width)
        summed = lax.dot_general(
            pick_ref[0], gathered, (((0,), (0,)), ((), ())), preferred_element_type=f32
        ).astype(bf16)
        for k in range(stages):

            @pl.when(pl.program_id(0) == k)
            def _(ref=outs[k]):
                ref[...] = summed

    return pl.pallas_call(
        kernel,
        grid=(stages,),
        in_specs=[
            pl.BlockSpec((1, experts * slots, tokens), lambda k: (k, 0, 0)),
            pl.BlockSpec((experts, 1, slots, width), lambda k: (0, k, 0, 0)),
        ],
        out_specs=[full_spec((tokens, width))] * stages,
        out_shape=[jax.ShapeDtypeStruct((tokens, width), bf16)] * stages,
        name="collect_each",
        cost_estimate=work(2 * stages * experts * slots * tokens * width, 2 * stages * (experts * slots + tokens) * width),
    )(pick, rows)


def feed_grads(rows, d_gates, d_ups, d_logits):
    count, width = rows[0].shape
    part, lanes = d_gates[0].shape[1], d_logits[0].shape[1]
    held = len(rows)
    step = min(256, width)

    def kernel(*refs):
        ins, outs = refs[: 4 * held], refs[4 * held :]
        for kind, out in enumerate(outs):
            total = None
            for m in range(held):
                got = lax.dot_general(
                    ins[m][...],
                    ins[held * (kind + 1) + m][...],
                    (((0,), (0,)), ((), ())),
                    preferred_element_type=f32,
                )
                total = got if total is None else total + got
            out[...] = total.astype(out.dtype)

    def resident(array):
        return pl.BlockSpec(array.shape, lambda g: (0, 0), pipeline_mode=pl.Buffered(1))

    others = (*d_gates, *d_ups, *d_logits)
    return pl.pallas_call(
        kernel,
        grid=(width // step,),
        in_specs=[pl.BlockSpec((count, step), lambda g: (0, g)) for _ in rows]
        + [resident(x) for x in others],
        out_specs=[pl.BlockSpec((step, n), lambda g: (g, 0)) for n in (part, part, lanes)],
        out_shape=[
            jax.ShapeDtypeStruct((width, part), bf16),
            jax.ShapeDtypeStruct((width, part), bf16),
            jax.ShapeDtypeStruct((width, lanes), f32),
        ],
        name="feed_grads",
        cost_estimate=work(4 * held * count * width * part, 2 * (held * count * (width + 2 * part) + 2 * width * part)),
    )(*rows, *others)


def cut(place, gate, up):
    rows, hidden = gate.shape
    stages = place.shape[0] - 2
    part = hidden // stages

    def kernel(place_ref, gate_ref, up_ref, *outs):
        for k in range(stages):

            @pl.when(pl.program_id(0) == k)
            def _(ref=outs[k]):
                ref[0] = gate_ref[...]
                ref[1] = up_ref[...]

    block = pl.BlockSpec((rows, part), lambda g, p: (0, p[2 + g]))
    return pl.pallas_call(
        kernel,
        grid_spec=pltpu.PrefetchScalarGridSpec(
            num_scalar_prefetch=1,
            grid=(stages,),
            in_specs=[block, block],
            out_specs=[full_spec((2, rows, part))] * stages,
        ),
        out_shape=[jax.ShapeDtypeStruct((2, rows, part), bf16)] * stages,
        name="cut",
        cost_estimate=work(0, 8 * stages * rows * part),
    )(place, gate, up)


def other_half(place, gate, up, stages):
    width, part = gate.shape
    rows = width // (2 * stages)

    def kernel(place_ref, gate_ref, up_ref, o_ref):
        o_ref[0, 0] = gate_ref[...]
        o_ref[0, 1] = up_ref[...]

    block = pl.BlockSpec((rows, part), lambda g, p: (2 * g + 1 - p[1], 0))
    return pl.pallas_call(
        kernel,
        grid_spec=pltpu.PrefetchScalarGridSpec(
            num_scalar_prefetch=1,
            grid=(stages,),
            in_specs=[block, block],
            out_specs=pl.BlockSpec((1, 2, rows, part), lambda g, p: (g, 0, 0, 0)),
        ),
        out_shape=jax.ShapeDtypeStruct((stages, 2, rows, part), bf16),
        name="other_half",
        cost_estimate=work(0, 8 * stages * rows * part),
    )(place, gate, up)


def own_half(place, gate, up, other):
    stages, _, rows, part = other.shape

    def kernel(place_ref, gate_ref, up_ref, other_ref, *outs):
        for k in range(stages):

            @pl.when(pl.program_id(0) == k)
            def _(ref=outs[k]):
                ref[0] = (gate_ref[...].astype(f32) + other_ref[0, 0].astype(f32)).astype(bf16)
                ref[1] = (up_ref[...].astype(f32) + other_ref[0, 1].astype(f32)).astype(bf16)

    block = pl.BlockSpec((rows, part), lambda g, p: (2 * p[2 + g] + p[1], 0))
    return pl.pallas_call(
        kernel,
        grid_spec=pltpu.PrefetchScalarGridSpec(
            num_scalar_prefetch=1,
            grid=(stages,),
            in_specs=[
                block,
                block,
                pl.BlockSpec((1, 2, rows, part), lambda g, p: (p[2 + g], 0, 0, 0)),
            ],
            out_specs=[full_spec((2, rows, part))] * stages,
        ),
        out_shape=[jax.ShapeDtypeStruct((2, rows, part), bf16)] * stages,
        name="own_half",
        cost_estimate=work(0, 12 * stages * rows * part),
    )(place, gate, up, other)


def assemble(place, mine, theirs):
    stages = len(mine)
    _, rows, part = mine[0].shape

    def kernel(place_ref, *refs):
        ins, (gate_ref, up_ref) = refs[:-2], refs[-2:]
        step = pl.program_id(0)
        hop = (place_ref[0] - step // 2) % stages
        here = step % 2 == place_ref[1]
        for k in range(stages):
            for which in range(2):

                @pl.when((hop == k) & (here == (which == 0)))
                def _(ref=ins[which * stages + k]):
                    gate_ref[...] = ref[0]
                    up_ref[...] = ref[1]

    block = pl.BlockSpec((rows, part), lambda g, p: (g, 0))
    shape = jax.ShapeDtypeStruct((2 * stages * rows, part), bf16)
    return pl.pallas_call(
        kernel,
        grid_spec=pltpu.PrefetchScalarGridSpec(
            num_scalar_prefetch=1,
            grid=(2 * stages,),
            in_specs=[
                pl.BlockSpec((2, rows, part), lambda g, p: (0, 0, 0), pipeline_mode=pl.Buffered(1))
            ]
            * (2 * stages),
            out_specs=[block, block],
        ),
        out_shape=[shape, shape],
        name="assemble",
        cost_estimate=work(0, 12 * stages * rows * part),
    )(place, *mine, *theirs)


def widen(place, got):
    stages = len(got)
    _, rows, part = got[0].shape

    def kernel(place_ref, *refs):
        hop = (place_ref[0] - pl.program_id(1)) % stages
        for k in range(stages):

            @pl.when(hop == k)
            def _(ref=refs[k]):
                refs[-1][...] = ref[...].astype(f32)

    return pl.pallas_call(
        kernel,
        grid_spec=pltpu.PrefetchScalarGridSpec(
            num_scalar_prefetch=1,
            grid=(2, stages),
            in_specs=[pl.BlockSpec((1, rows, part), lambda w, g, p: (w, 0, 0))] * stages,
            out_specs=pl.BlockSpec((1, rows, part), lambda w, g, p: (w, 0, g)),
        ),
        out_shape=jax.ShapeDtypeStruct((2, rows, stages * part), f32),
        name="widen",
        cost_estimate=work(0, 12 * stages * rows * part),
    )(place, *got)


def feed_kernel(own_ref, r_ref, g_ref, other_ref, router_ref, wg_ref, wu_ref, wd_ref, *outs):
    out_ref, db_ref, low_ref, dg_ref, du_ref, dr_ref, dl_ref = outs
    rows, grads = r_ref[...], g_ref[...].astype(f32)
    router = router_ref[...]
    logits = jnp.dot(rows, router, preferred_element_type=f32)
    column = lax.broadcasted_iota(jnp.int32, logits.shape, 1)
    turn = (column == own_ref[0]).astype(f32) - (column == other_ref[...]).astype(f32)
    lead = jnp.sum(logits * turn, axis=1, keepdims=True)
    gate, rest = jax.nn.sigmoid(lead), jax.nn.sigmoid(-lead)
    d_rows = (gate * grads).astype(bf16)
    dr_ref[...] = d_rows
    gate_pre = jnp.dot(rows, wg_ref[...], preferred_element_type=f32)
    up_pre = jnp.dot(rows, wu_ref[...], preferred_element_type=f32)
    d_low = lax.dot_general(
        d_rows, wd_ref[...], (((1,), (1,)), ((), ())), preferred_element_type=f32
    )
    sigma = jax.nn.sigmoid(gate_pre)
    silu = gate_pre * sigma
    low = (silu * up_pre).astype(bf16)
    low_ref[...] = low
    d_up = (d_low * silu).astype(bf16)
    du_ref[...] = d_up
    d_gate = (d_low * up_pre * (sigma + silu * (1.0 - sigma))).astype(bf16)
    dg_ref[...] = d_gate
    result = jnp.dot(low, wd_ref[...], preferred_element_type=f32)
    out_ref[...] = (gate * result).astype(bf16)
    d_value = jnp.sum(grads * result, axis=1, keepdims=True)
    d_logits = (gate * rest * d_value) * turn
    high = d_logits.astype(bf16)
    small = (d_logits - high.astype(f32)).astype(bf16)
    half = high.shape[1]
    dl_ref[:, :half] = high
    dl_ref[:, half:] = small
    d_b = lax.dot_general(
        d_gate, wg_ref[...], (((1,), (1,)), ((), ())), preferred_element_type=f32
    ) + lax.dot_general(d_up, wu_ref[...], (((1,), (1,)), ((), ())), preferred_element_type=f32)
    for piece in (high, small):
        d_b = d_b + lax.dot_general(
            piece, router, (((1,), (1,)), ((), ())), preferred_element_type=f32
        )
    db_ref[...] = d_b.astype(bf16)


def feed(own, rows, grads, other, router, wg, wu, wd):
    count, width = rows.shape
    part = wg.shape[1]
    step = min(256, count)
    lanes = router.shape[1]

    def by_rows(columns):
        return pl.BlockSpec((step, columns), lambda g, s: (g, 0))

    def held(shape):
        return pl.BlockSpec(shape, lambda g, s: (0, 0), pipeline_mode=pl.Buffered(1))

    def shape(columns):
        return jax.ShapeDtypeStruct((count, columns), bf16)

    widths = (width, width, part, part, part, width, 2 * lanes)
    return pl.pallas_call(
        feed_kernel,
        grid_spec=pltpu.PrefetchScalarGridSpec(
            num_scalar_prefetch=1,
            grid=(count // step,),
            in_specs=[by_rows(width), by_rows(width), by_rows(1)]
            + [held(w.shape) for w in (router, wg, wu, wd)],
            out_specs=[by_rows(w) for w in widths],
        ),
        out_shape=[shape(w) for w in widths],
        name="feed",
        cost_estimate=work(12 * count * width * part, 6 * width * part + 2 * count * (5 * width + 3 * part), count * part),
    )(own, rows, grads, other, router, wg, wu, wd)


def after(array, *others):
    return lax.optimization_barrier((array, *others))[0]


def per_device(
    inputs,
    attn_routes,
    mlp_routes,
    pic_start,
    kv_weight,
    router_weight,
    norm_gains,
    q_weight,
    o_weight,
    gate_weight,
    up_weight,
    down_weight,
    cotangent,
):
    experts = lax.axis_size("expert")
    dp_size = lax.axis_size("dp")
    stages = dp_size // 2
    own = lax.axis_index("expert")
    dp_index = lax.axis_index("dp")
    stage, core = dp_index // 2, dp_index % 2
    tokens, width = inputs.shape[2], inputs.shape[3]
    inner = HEADS * HSZ
    group = inner // experts
    slots = tokens * TOPK // experts
    span = tokens * experts
    rows_each = kv_weight.shape[0]
    hidden = gate_weight.shape[2]
    part = hidden // stages
    routed = experts * slots
    same_core = [[z * 2 + c for z in range(stages)] for c in range(2)]

    def exchange(blocks):
        return lax.all_to_all(blocks, "expert", 0, 0, tiled=True)

    def spread(block):
        return exchange(jnp.broadcast_to(block[None], (experts,) + block.shape))

    def along(block, k):
        if k % stages == 0:
            return block
        return lax.ppermute(
            block, "dp", [(j, ((j // 2 + k) % stages) * 2 + j % 2) for j in range(dp_size)]
        )

    def partner(block):
        return lax.ppermute(block, "dp", [(j, j ^ 1) for j in range(dp_size)])

    def pick(array, index, axis=0):
        return lax.dynamic_index_in_dim(array, index, axis, keepdims=False)

    small = jnp.concatenate(
        [
            attn_routes.reshape(-1).astype(bf16),
            mlp_routes.reshape(-1).astype(bf16),
            router_weight.reshape(-1),
            norm_gains.reshape(-1),
        ]
    )
    length = small.shape[0]
    line = 2 * group
    extra = -(-length // (16 * line)) * 16
    small = jnp.pad(small, (0, extra * line - length)).reshape(1, extra, line)
    kv_split = kv_weight.reshape(rows_each, 2, experts, group).transpose(2, 0, 1, 3)
    first = jnp.concatenate(
        [
            jnp.broadcast_to(inputs, (experts, MICRO, tokens, width)).reshape(experts, -1, width),
            kv_split.reshape(experts, rows_each * line // width, width),
            jnp.broadcast_to(small.reshape(1, -1, width), (experts, extra * line // width, width)),
        ],
        axis=1,
    )
    first = exchange(first)
    x_blocks = first[:, : MICRO * tokens].reshape(experts, MICRO, tokens, width)
    kv_rows = first[:, MICRO * tokens :].reshape(experts, rows_each + extra, line)
    stage_order = (stage - jnp.arange(stages, dtype=jnp.int32)) % stages
    place = jnp.arange(experts, dtype=jnp.int32)
    cot_stages = lax.all_gather(cotangent[0], "dp", axis=0, axis_index_groups=same_core)
    route_rows = mlp_routes[0].reshape(-1).astype(bf16)
    route_rows = jnp.pad(route_rows, (0, -route_rows.shape[0] % 128)).reshape(-1, 128)
    own_routes = jnp.stack([along(route_rows, k) for k in range(stages)]).reshape(stages, -1)
    own_routes = own_routes[:, : MICRO * tokens * TOPK].astype(jnp.int32)
    own_routes = own_routes.reshape(stages, MICRO, tokens, TOPK)
    home_m = selection(
        (own_routes[:, None] == place[None, :, None, None, None]).any(-1).astype(f32), slots
    )
    home_m = home_m.transpose(2, 0, 1, 3, 4).reshape(MICRO, stages, experts * slots, tokens)
    q_full = lax.all_gather(after(q_weight[0], cot_stages, first), "dp", axis=0, tiled=True)
    cot_rows = {}
    for m in ORDER:
        blocks = [pick(cot_stages, stage_order[k])[m] for k in range(stages)]
        cot_rows[m] = exchange(dispatch(blocks, home_m[m])(experts))
    kv_rows = after(kv_rows, q_full, cot_rows[ORDER[0]])
    kv_got = lax.all_gather(kv_rows, "dp", axis=0)

    forward_order = (stage + jnp.arange(stages, dtype=jnp.int32)) % stages
    where = jnp.concatenate([jnp.stack([stage, core]), forward_order]).astype(jnp.int32)
    if part % 128 == 0:
        mine = list(cut(where, gate_weight[0], up_weight[0]))
    else:
        both = jnp.stack([gate_weight[0], up_weight[0]]).reshape(2, -1, stages, part)
        mine = [pick(both, forward_order[k], 2) for k in range(stages)]
    for k in range(1, stages):
        mine[k] = along(after(mine[k], kv_rows), k)
    kv_cols = kv_got[:, :, :rows_each].reshape(width, line)
    small = kv_got[:, :, rows_each:].reshape(dp_size, experts, extra * line)
    count = MICRO * tokens * TOPK
    routes_a = pick(small[:, :, :count], dp_index).astype(jnp.int32)
    routes_a = routes_a.reshape(experts, MICRO, tokens, TOPK)
    routes_m = small[:, :, count : 2 * count].reshape(stages, 2, experts, count)
    routes_m = pick(routes_m, core, 1).astype(jnp.int32)
    routes_m = routes_m.reshape(stages, experts, MICRO, tokens, TOPK)[stage_order]
    router = small[:, :, 2 * count : 2 * count + rows_each * 2 * experts].reshape(
        width, 2 * experts
    )
    gains = small[:, :, 2 * count + rows_each * 2 * experts : length].reshape(width, 2)
    gain_1, gain_2 = gains[:, 0].astype(f32)[None], gains[:, 1].astype(f32)[None]
    router_a = jnp.pad(router[:, :experts], ((0, 0), (0, 128 - experts)))
    router_m = jnp.pad(router[:, experts:], ((0, 0), (0, 128 - experts)))

    x_all = x_blocks.transpose(1, 0, 2, 3).reshape(MICRO, span, width).astype(f32)
    a_all = (x_all * inverse_rms(x_all) * gain_1).astype(bf16)

    token = jnp.arange(tokens, dtype=jnp.int32)
    chosen = (routes_a[None] == place[:, None, None, None, None]).any(-1)
    pick_all = selection(chosen.transpose(0, 2, 1, 3).astype(f32), slots)
    query_pos = jnp.einsum(
        "emkst,t->emks", pick_all, token.astype(bf16), preferred_element_type=f32
    ).astype(jnp.int32)
    query_pos = (
        query_pos
        + place[:, None] * tokens
        + jnp.arange(MICRO, dtype=jnp.int32)[:, None, None] * span
    )
    query_pos = query_pos.transpose(1, 0, 2, 3).reshape(MICRO, experts, routed, 1)
    pick_a = pick(pick_all, own)
    other_a = jnp.einsum(
        "mkst,kmt->mks",
        pick_a,
        (routes_a.sum(-1) - own).astype(bf16),
        preferred_element_type=f32,
    ).astype(jnp.int32)
    other_a = other_a.reshape(MICRO, routed, 1)
    home_a = pick(pick_all, own, 2).transpose(1, 0, 2, 3).reshape(MICRO, routed, tokens)
    pick_m = selection((routes_m == own).any(-1).astype(f32), slots)
    other_m = jnp.einsum(
        "kemst,kemt->mkes",
        pick_m,
        (routes_m.sum(-1) - own).astype(bf16),
        preferred_element_type=f32,
    ).astype(jnp.int32)
    other_m = other_m.transpose(0, 2, 1, 3).reshape(MICRO, experts * stages * slots, 1)

    key_cos, key_sin = rope_tables(jnp.arange(MICRO * span, dtype=jnp.int32).reshape(MICRO, span))
    query_cos, query_sin = rope_tables(query_pos[..., 0])
    kv_own = project_kv(
        a_all,
        kv_cols,
        jnp.stack([key_cos, jnp.ones_like(key_cos)], axis=1),
        jnp.stack([key_sin, jnp.zeros_like(key_sin)], axis=1),
    )
    kvs = [kv_own[m] for m in range(MICRO)]

    a_pairs = jnp.einsum(
        "mest,metd->mesd",
        pick_a,
        a_all.reshape(MICRO, experts, tokens, width),
        preferred_element_type=f32,
    ).astype(bf16)
    a_pairs = a_pairs.reshape(MICRO, routed, width)
    column = jnp.arange(128, dtype=jnp.int32)[None, None, :]
    turn_a = (column == own).astype(f32) - (column == other_a).astype(f32)
    lead = jnp.sum(mm(a_pairs, router_a) * turn_a, axis=-1, keepdims=True)
    gate_a, rest_a = jax.nn.sigmoid(lead), jax.nn.sigmoid(-lead)
    q_out = project_q(
        a_pairs.reshape(MICRO * routed, width),
        q_full,
        pick(query_cos, own, 1).reshape(MICRO * routed, HSZ),
        pick(query_sin, own, 1).reshape(MICRO * routed, HSZ),
        MICRO,
        experts,
    )

    down_other = partner(down_weight[0])
    down_w = jnp.concatenate(
        [
            jnp.where(core == 0, down_weight[0], down_other),
            jnp.where(core == 0, down_other, down_weight[0]),
        ]
    )
    start = after(pic_start.astype(jnp.int32), down_w)
    held = lax.optimization_barrier(
        (o_weight[0], *mine, q_out, *kvs, home_a, cot_rows[ORDER[1]], other_m, gate_a, down_w)
    )
    mine = list(held[1 : 1 + stages])
    o_full = lax.all_gather(held[0], "dp", axis=0, tiled=True)
    queries, mixed, peaks, attn, middles, inverses, feeds = {}, {}, {}, {}, {}, {}, {}
    mixed_got = {}
    for m in ORDER:
        queries[m] = exchange(q_out[m])
        heads, peaks[m] = attend(queries[m], query_pos[m], kvs[: m + 1], start)
        mixed_got[m] = exchange(heads)
    for m in ORDER:
        attn[m], gated, mixed[m] = project_o(mixed_got[m], o_full, gate_a[m])
        back = exchange(gated.reshape(experts, slots, width))
        middles[m], inverses[m], b_low = combine(
            back.reshape(routed, width), home_a[m], inputs[0, m], gain_2
        )
        blocks = [along(b_low, k) for k in range(stages)]
        feeds[m] = exchange(dispatch(blocks, home_m[m])(experts))
    mine = list(lax.optimization_barrier((*mine, b_low)))[:-1]
    gate_w, up_w = assemble(where, mine, [partner(piece) for piece in mine])

    pairs = experts * stages * slots
    own_id = own.reshape(1).astype(jnp.int32)
    outs, d_pieces, d_rows, kept_feed = {}, {}, {}, {}
    for m in ORDER:
        rows = feeds[m].reshape(pairs, width)
        if kept_feed:
            rows = after(rows, kept_feed[ORDER[0]][4])
        outs[m], d_b, *kept_feed[m] = feed(
            own_id,
            rows,
            cot_rows[m].reshape(pairs, width),
            other_m[m],
            router_m,
            gate_w,
            up_w,
            down_w,
        )
        d_rows[m] = exchange(d_b.reshape(experts, stages, slots, width))

    def joined(index):
        return jnp.concatenate([kept_feed[m][index] for m in ORDER])

    def over_stages(rows, m):
        summed = collect(rows, home_m[m], stage_order)
        return summed, lax.psum_scatter(
            summed, "dp", scatter_dimension=0, tiled=True, axis_index_groups=same_core
        )[0]

    gate_grad, up_grad, router_m_grad = feed_grads(
        [feeds[m].reshape(pairs, width) for m in ORDER],
        [kept_feed[m][1] for m in ORDER],
        [kept_feed[m][2] for m in ORDER],
        [kept_feed[m][4] for m in ORDER],
    )
    early, d_pieces[ORDER[0]] = over_stages(after(d_rows[ORDER[0]], gate_grad), ORDER[0])
    late, d_pieces[ORDER[1]] = over_stages(after(d_rows[ORDER[1]], early), ORDER[1])
    down_grad = t_mm(after(joined(0), late), joined(3)).astype(bf16)
    out_rows = exchange(
        after(outs[ORDER[0]], d_rows[ORDER[1]]).reshape(experts, stages, slots, width)
    )
    out_sums = {ORDER[0]: over_stages(after(out_rows, late), ORDER[0])[1]}

    other = partner(other_half(where, gate_grad, after(up_grad, late), stages))
    total = list(own_half(where, gate_grad, up_grad, other))

    total[1] = along(total[1], 1)
    d_pieces[ORDER[0]] = after(d_pieces[ORDER[0]], total[0])
    d_pieces[ORDER[1]] = after(d_pieces[ORDER[1]], total[1], down_grad)

    def scattered(grad):
        return lax.psum_scatter(grad, "dp", scatter_dimension=0, tiled=True)

    def ordered(values):
        return jnp.concatenate([values[m] for m in ORDER])

    gain_2_grad = jnp.zeros((1, width), f32)
    d_middles, d_attn, d_flat, d_pairs, d_kvs, logit_grads, later = {}, {}, {}, {}, {}, {}, []
    for m in ORDER:
        d_middles[m], gain_part, sent = middle_back(
            [d_pieces[m]], middles[m], inverses[m], cotangent[0, m], gain_2, home_a[m]
        )
        gain_2_grad = gain_2_grad + gain_part
        if m == ORDER[0]:
            sent = after(sent, out_rows)
        got = exchange(sent.reshape(experts, slots, width)).reshape(routed, width)
        d_attn[m], d_heads, logit_grads[m] = back_o(
            got, attn[m], gate_a[m], rest_a[m], turn_a[m], o_full, experts
        )
        d_heads = exchange(d_heads)
        if m == ORDER[1]:
            o_grad = t_mm(ordered(mixed), ordered(d_attn)).astype(bf16)
            d_heads = after(d_heads, o_grad)
        d_query, d_kvs[m], *later = attend_back(
            queries[m],
            d_heads,
            query_cos[m],
            query_sin[m],
            query_pos[m],
            kvs[: m + 1],
            key_cos[m],
            key_sin[m],
            later,
            start,
        )
        d_query = exchange(d_query)
        if m == ORDER[1]:
            kv_grad = t_mm(ordered(a_all), ordered(d_kvs)).astype(bf16)
            d_query = after(d_query, kv_grad)
        d_pairs[m], d_flat[m] = back_q(d_query, q_full, logit_grads[m], router_a)

    pair_rows = ordered(a_pairs)
    q_grad = t_mm(pair_rows, ordered(d_flat)).astype(bf16)
    d_pairs[ORDER[1]] = after(d_pairs[ORDER[1]], q_grad)
    router_a_grad = t_mm(pair_rows, ordered(logit_grads))
    router_a_grad = router_a_grad[:, :experts] + router_a_grad[:, 128 : 128 + experts]
    o_mine = scattered(o_grad)
    kv_mine = scattered(kv_grad)
    d_pairs[ORDER[1]] = after(d_pairs[ORDER[1]], o_mine)
    for k in range(2, stages):
        piece = after(total[k], q_grad) if k < 4 else after(total[k], total[k - 2])
        total[k] = along(piece, k)
    d_pairs[ORDER[1]] = after(d_pairs[ORDER[1]], *total[2:3])
    if part % 128 == 0:
        shares = widen(where, total)
    else:
        got = jnp.stack(total)[stage_order].astype(f32)
        shares = jnp.concatenate([got[s] for s in range(stages)], axis=2)
    gate_share, up_share = shares[:1], shares[1:]
    o_share = o_mine.astype(f32)[None]
    q_share = scattered(q_grad).astype(f32)[None]
    router_m_grad = router_m_grad[:, :experts] + router_m_grad[:, 128 : 128 + experts]
    down_split = down_grad.reshape(2, part // 2, width)
    down_share = (
        pick(down_split, core).astype(f32) + partner(pick(down_split, 1 - core)).astype(f32)
    )[None]


    gain_1_grad = jnp.zeros((1, width), f32)
    grad_x = [None] * MICRO
    for m in ORDER:
        d_a = exchange(token_back(d_kvs[m], kv_cols, d_pairs[m], pick_a[m]))
        grad_x[m], gain_part = input_back(d_a, inputs[0, m], gain_1, d_middles[m])
        gain_1_grad = gain_1_grad + gain_part
    grad_x = jnp.stack(grad_x)[None]

    out_rows = exchange(after(outs[ORDER[1]], d_a).reshape(experts, stages, slots, width))
    out_sums[ORDER[1]] = over_stages(out_rows, ORDER[1])[1]
    out_act = jnp.stack([middles[m] + out_sums[m].astype(f32) for m in range(MICRO)])
    out_act = out_act.astype(bf16)[None]
    kv_got = exchange(kv_mine.reshape(experts, rows_each, line)).reshape(experts, rows_each, 2, group)
    kv_share = kv_got.transpose(1, 2, 0, 3).reshape(rows_each, 2 * inner).astype(f32)

    tail = jnp.concatenate(
        [router_a_grad.T, router_m_grad.T, gain_1_grad, gain_2_grad], axis=0
    )
    kinds = 2 * experts + 2
    tail = jnp.pad(tail, ((0, -kinds % 8), (0, 0))).reshape(-1, dp_size, width // dp_size)
    tail = lax.psum_scatter(
        tail.transpose(1, 0, 2), "dp", scatter_dimension=0, tiled=True
    )
    tail = tail.reshape(-1, experts, rows_each).transpose(1, 0, 2)
    tail = lax.psum_scatter(tail, "expert", scatter_dimension=0, tiled=True)[0].T
    router_share, gains_share = tail[:, : 2 * experts], tail[:, 2 * experts : kinds]

    largest = jnp.maximum(peaks[0], peaks[1])[:, :, 0, 0]
    mine_here = jnp.arange(HEADS, dtype=jnp.int32) // (HEADS // experts) == own
    largest = jnp.where(mine_here[None], jnp.tile(largest, (1, experts)), masked_low)
    largest = jnp.pad(largest, ((0, 0), (0, 128 - HEADS)))
    for axis, size in (("dp", dp_size), ("expert", experts)):
        hop = 1
        while hop < size:
            largest = jnp.maximum(
                largest, lax.ppermute(largest, axis, [(j, j ^ hop) for j in range(size)])
            )
            hop *= 2
    ratio = logit_cap / jnp.maximum(largest[:, :HEADS], logit_cap)
    root_q = jnp.repeat(jnp.sqrt(pick(ratio, own)), HSZ)[None]
    root_k = jnp.repeat(jnp.sqrt(jnp.min(ratio, axis=0)), HSZ)[None]
    clipped_q = (q_weight.astype(f32) * root_q[None]).astype(bf16)
    clipped_key = (kv_weight[:, :inner].astype(f32) * root_k).astype(bf16)
    return (
        out_act,
        grad_x,
        kv_share,
        router_share,
        gains_share,
        q_share,
        o_share,
        gate_share,
        up_share,
        down_share,
        clipped_q,
        clipped_key,
    )


def solution(mesh):
    tokens4 = P("dp", None, "expert", None)
    rows2 = P(("dp", "expert"), None)
    weights3 = P("expert", "dp", None)
    return jax.shard_map(
        per_device,
        mesh=mesh,
        in_specs=(tokens4,) * 3 + (P("dp"),) + (rows2,) * 3 + (weights3,) * 5 + (tokens4,),
        out_specs=(tokens4,) * 2 + (rows2,) * 3 + (weights3,) * 6 + (rows2,),
        check_vma=False,
    )
```

```python
import math

import jax
import jax.numpy as jnp
from jax import lax
from jax.experimental import pallas as pl
from jax.experimental.pallas import tpu as pltpu
from jax.sharding import PartitionSpec as P

HEADS = 16
HSZ = 128
TOPK = 2
PIC = 256
MICRO = 2
ORDER = (1, 0)

norm_eps = 1e-06
logit_cap = 8.0
masked_low = -1e30
bf16 = jnp.bfloat16
f32 = jnp.float32


def mm(left, right):
    return jnp.dot(left, right, preferred_element_type=f32)


def mm_t(left, right):
    return lax.dot_general(left, right, (((1,), (1,)), ((), ())), preferred_element_type=f32)


def t_mm(left, right):
    return lax.dot_general(left, right, (((0,), (0,)), ((), ())), preferred_element_type=f32)


def rope_tables(positions):
    half = HSZ // 2
    freq = jnp.exp(jnp.arange(half, dtype=f32) * (-math.log(10000.0) / half))
    angles = positions.astype(f32)[..., None] * freq
    cosine, sine = jnp.cos(angles), jnp.sin(angles)
    return (
        jnp.concatenate([cosine, cosine], axis=-1),
        jnp.concatenate([-sine, sine], axis=-1),
    )


def inverse_rms(values):
    return lax.rsqrt(jnp.mean(values * values, axis=-1, keepdims=True) + norm_eps)


def selection(hot, slots):
    tokens = hot.shape[-1]
    before = jnp.triu(jnp.ones((tokens, tokens), bf16), 1)
    rank = jnp.dot(hot.astype(bf16), before, preferred_element_type=f32)
    slot = jnp.arange(slots, dtype=jnp.int32)[:, None]
    taken = (rank.astype(jnp.int32)[..., None, :] == slot) & (hot[..., None, :] > 0)
    return taken.astype(bf16)


def full_spec(shape):
    return pl.BlockSpec(shape, lambda *_: (0,) * len(shape))


def work(flops, moved, exps=0):
    return pl.CostEstimate(flops=flops, bytes_accessed=moved, transcendentals=exps)


def kv_kernel(a_ref, w_ref, cos_ref, sin_ref, o_ref):
    got = jnp.dot(a_ref[0], w_ref[...], preferred_element_type=f32)
    cosine, sine = cos_ref[0, 0], sin_ref[0, 0]
    for part in range(got.shape[1] // HSZ):
        piece = got[:, part * HSZ : (part + 1) * HSZ]
        turned = piece * cosine + pltpu.roll(piece, HSZ // 2, 1) * sine
        o_ref[0, 0, :, part * HSZ : (part + 1) * HSZ] = turned.astype(bf16)


def project_kv(a_all, kv_cols, cosine, sine):
    micro, rows, width = a_all.shape
    group = kv_cols.shape[1] // 2
    step = min(256, group)
    per = group // step
    table = pl.BlockSpec((1, 1, rows, HSZ), lambda m, g: (m, g // per, 0, 0))
    return pl.pallas_call(
        kv_kernel,
        grid=(micro, 2 * per),
        in_specs=[
            pl.BlockSpec((1, rows, width), lambda m, g: (m, 0, 0)),
            pl.BlockSpec((width, step), lambda m, g: (0, g)),
            table,
            table,
        ],
        out_specs=pl.BlockSpec((1, 1, rows, step), lambda m, g: (m, g // per, 0, g % per)),
        out_shape=jax.ShapeDtypeStruct((micro, 2, rows, group), bf16),
        name="project_kv",
        cost_estimate=work(4 * micro * rows * width * group, 2 * (micro * rows * width + 2 * width * group + 2 * micro * rows * group)),
    )(a_all, kv_cols, cosine, sine)


def probabilities(query, keys, start, qpos, micro):
    parts = []
    for m in range(micro + 1):
        got = lax.dot_general(
            query, keys[m], (((1,), (1,)), ((), ())), preferred_element_type=f32
        ) * (HSZ**-0.5)
        if m == micro:
            kpos = micro * got.shape[1] + lax.broadcasted_iota(jnp.int32, got.shape, 1)
            inside_q = (qpos >= start) & (qpos < start + PIC)
            inside_k = (kpos >= start) & (kpos < start + PIC)
            keep = (kpos <= qpos) | (inside_q & inside_k)
            got = jnp.where(keep, got, masked_low)
        parts.append(got)
    peak = parts[0].max(axis=1, keepdims=True)
    for got in parts[1:]:
        peak = jnp.maximum(peak, got.max(axis=1, keepdims=True))
    lifted = [jnp.exp(got - peak) for got in parts]
    total = lifted[0].sum(axis=1, keepdims=True)
    for got in lifted[1:]:
        total = total + got.sum(axis=1, keepdims=True)
    scale = 1.0 / total
    return [got * scale for got in lifted], peak


def project_q(a_pairs, q_full, cosine, sine, micro, experts):
    total, width = a_pairs.shape
    inner = q_full.shape[1]
    group = inner // experts
    step = min(256, group)
    per = group // step
    rows = total // micro

    def kernel(a_ref, w_ref, cos_ref, sin_ref, o_ref):
        got = jnp.dot(a_ref[...], w_ref[...], preferred_element_type=f32)
        for h in range(step // HSZ):
            lanes = slice(h * HSZ, (h + 1) * HSZ)
            piece = got[:, lanes]
            turned = piece * cos_ref[...] + pltpu.roll(piece, HSZ // 2, 1) * sin_ref[...]
            o_ref[:, 0, :, lanes] = turned.astype(bf16).reshape(micro, rows, HSZ)

    return pl.pallas_call(
        kernel,
        grid=(inner // step,),
        in_specs=[
            full_spec((total, width)),
            pl.BlockSpec((width, step), lambda g: (0, g)),
            full_spec((total, HSZ)),
            full_spec((total, HSZ)),
        ],
        out_specs=pl.BlockSpec((micro, 1, rows, step), lambda g: (0, g // per, 0, g % per)),
        out_shape=jax.ShapeDtypeStruct((micro, experts, rows, group), bf16),
        name="project_q",
        cost_estimate=work(2 * total * width * inner, 2 * (total * width + width * inner + total * inner)),
    )(a_pairs, q_full, cosine, sine)


def attend(query, qpos, kvs, start):
    micro = len(kvs) - 1
    experts, rows, group = query.shape
    hg = group // HSZ
    keys_seen = sum(kv.shape[1] for kv in kvs)

    def kernel(start_ref, q_ref, pos_ref, *rest):
        kv_refs, (mixed_ref, peak_ref) = rest[:-2], rest[-2:]
        for h in range(hg):
            lanes = slice(h * HSZ, (h + 1) * HSZ)
            probs, peak = probabilities(
                q_ref[0, :, lanes],
                [r[0, :, lanes] for r in kv_refs],
                start_ref[0],
                pos_ref[0],
                micro,
            )
            mixed = jnp.zeros((rows, HSZ), f32)
            for m in range(micro + 1):
                mixed = mixed + jnp.dot(
                    probs[m].astype(bf16), kv_refs[m][1, :, lanes], preferred_element_type=f32
                )
            mixed_ref[0, :, lanes] = mixed.astype(bf16)
            peak_ref[0, h] = jnp.full(peak_ref.shape[2:], jnp.max(peak), f32)

    return pl.pallas_call(
        kernel,
        grid_spec=pltpu.PrefetchScalarGridSpec(
            num_scalar_prefetch=1,
            grid=(experts,),
            in_specs=[
                pl.BlockSpec((1, rows, group), lambda g, s: (g, 0, 0)),
                pl.BlockSpec((1, rows, 1), lambda g, s: (g, 0, 0)),
            ]
            + [full_spec(kv.shape) for kv in kvs],
            out_specs=[
                pl.BlockSpec((1, rows, group), lambda g, s: (g, 0, 0)),
                pl.BlockSpec((1, hg, 8, 128), lambda g, s: (g, 0, 0, 0)),
            ],
        ),
        out_shape=[
            jax.ShapeDtypeStruct((experts, rows, group), bf16),
            jax.ShapeDtypeStruct((experts, hg, 8, 128), f32),
        ],
        name="attend",
        cost_estimate=work(4 * experts * rows * group * keys_seen, 4 * experts * rows * group, experts * rows * hg * keys_seen),
    )(start, query, qpos, *kvs)


def attend_back(query, d_mixed, cosine, sine, qpos, kvs, key_cos, key_sin, later, start):
    micro = len(kvs) - 1
    experts, rows, group = query.shape
    keys = kvs[0].shape[1]
    hg = group // HSZ
    held = len(later)

    def kernel(start_ref, q_ref, dm_ref, cos_ref, sin_ref, pos_ref, kcos_ref, ksin_ref, *rest):
        kv_refs = rest[: micro + 1]
        later_refs = rest[micro + 1 : micro + 1 + held]
        dq_ref, dkv_ref = rest[micro + 1 + held : micro + 3 + held]
        sums = rest[micro + 3 + held :]
        step = pl.program_id(0)

        @pl.when(step == 0)
        def _():
            for m in range(micro + 1):
                if held and m == micro:
                    sums[m][...] = later_refs[0][...]
                else:
                    sums[m][...] = jnp.zeros(sums[m].shape, f32)

        for h in range(hg):
            lanes = slice(h * HSZ, (h + 1) * HSZ)
            q, dm = q_ref[0, :, lanes], dm_ref[0, :, lanes]
            probs, _ = probabilities(
                q, [r[0, :, lanes] for r in kv_refs], start_ref[0], pos_ref[0], micro
            )
            d_probs = [
                lax.dot_general(
                    dm, r[1, :, lanes], (((1,), (1,)), ((), ())), preferred_element_type=f32
                )
                for r in kv_refs
            ]
            total = jnp.sum(d_probs[0] * probs[0], axis=1, keepdims=True)
            for m in range(1, micro + 1):
                total = total + jnp.sum(d_probs[m] * probs[m], axis=1, keepdims=True)
            d_q = jnp.zeros((rows, HSZ), f32)
            for m in range(micro + 1):
                d_scores = (probs[m] * (d_probs[m] - total)).astype(bf16)
                d_q = d_q + jnp.dot(d_scores, kv_refs[m][0, :, lanes], preferred_element_type=f32)
                sums[m][0, :, lanes] += lax.dot_general(
                    d_scores, q, (((0,), (0,)), ((), ())), preferred_element_type=f32
                )
                sums[m][1, :, lanes] += lax.dot_general(
                    probs[m].astype(bf16), dm, (((0,), (0,)), ((), ())), preferred_element_type=f32
                )
            d_q = d_q * (HSZ**-0.5)
            back = d_q * cos_ref[0] - pltpu.roll(d_q, HSZ // 2, 1) * sin_ref[0]
            dq_ref[0, :, lanes] = back.astype(bf16)

        @pl.when(step == experts - 1)
        def _():
            for h in range(hg):
                lanes = slice(h * HSZ, (h + 1) * HSZ)
                d_k = sums[micro][0, :, lanes] * (HSZ**-0.5)
                back = d_k * kcos_ref[...] - pltpu.roll(d_k, HSZ // 2, 1) * ksin_ref[...]
                dkv_ref[:, lanes] = back.astype(bf16)
                dkv_ref[:, group + h * HSZ : group + (h + 1) * HSZ] = sums[micro][
                    1, :, lanes
                ].astype(bf16)

    block = pl.BlockSpec((1, rows, group), lambda g, s: (g, 0, 0))
    table = pl.BlockSpec((1, rows, HSZ), lambda g, s: (g, 0, 0))
    sums_shape = jax.ShapeDtypeStruct((2, keys, group), f32)
    return pl.pallas_call(
        kernel,
        grid_spec=pltpu.PrefetchScalarGridSpec(
            num_scalar_prefetch=1,
            grid=(experts,),
            in_specs=[block, block, table, table]
            + [pl.BlockSpec((1, rows, 1), lambda g, s: (g, 0, 0))]
            + [full_spec((keys, HSZ))] * 2
            + [full_spec((2, keys, group))] * (micro + 1 + held),
            out_specs=[block, full_spec((keys, 2 * group))]
            + [full_spec((2, keys, group))] * micro,
            scratch_shapes=[pltpu.VMEM((2, keys, group), f32)],
        ),
        out_shape=[
            jax.ShapeDtypeStruct((experts, rows, group), bf16),
            jax.ShapeDtypeStruct((keys, 2 * group), bf16),
        ]
        + [sums_shape] * micro,
        name="attend_back",
        cost_estimate=work(10 * experts * rows * group * keys * (micro + 1), 12 * experts * rows * group, experts * rows * hg * keys * (micro + 1)),
    )(start, query, d_mixed, cosine, sine, qpos, key_cos, key_sin, *kvs, *later)


def join_groups(got_ref, flat_ref):
    experts, _, group = got_ref.shape
    for e in range(experts):
        flat_ref[:, e * group : (e + 1) * group] = got_ref[e]


def project_o(mixed, o_full, gate):
    experts, rows, group = mixed.shape
    inner, width = o_full.shape
    step = min(512, width)

    def kernel(mixed_ref, o_ref, gate_ref, attn_ref, gated_ref, flat_ref):
        @pl.when(pl.program_id(0) == 0)
        def _():
            join_groups(mixed_ref, flat_ref)

        got = jnp.dot(flat_ref[...], o_ref[...], preferred_element_type=f32)
        attn_ref[...] = got.astype(bf16)
        gated_ref[...] = (got * gate_ref[...]).astype(bf16)

    column = pl.BlockSpec((rows, step), lambda g: (0, g))
    return pl.pallas_call(
        kernel,
        grid=(width // step,),
        in_specs=[
            full_spec(mixed.shape),
            pl.BlockSpec((inner, step), lambda g: (0, g)),
            full_spec((rows, 1)),
        ],
        out_specs=[column, column, full_spec((rows, inner))],
        out_shape=[
            jax.ShapeDtypeStruct((rows, width), bf16),
            jax.ShapeDtypeStruct((rows, width), bf16),
            jax.ShapeDtypeStruct((rows, inner), bf16),
        ],
        name="project_o",
        cost_estimate=work(2 * rows * inner * width, 2 * (inner * width + 4 * rows * width)),
    )(mixed, o_full, gate)


def back_o(got, attn, gate, rest, turn, o_full, experts):
    rows, width = got.shape
    inner = o_full.shape[0]
    group = inner // experts
    lanes = turn.shape[1]

    def kernel(got_ref, attn_ref, gate_ref, rest_ref, turn_ref, o_ref, da_ref, dm_ref, dl_ref):
        @pl.when(pl.program_id(0) == 0)
        def _():
            upstream = got_ref[...].astype(f32)
            da_ref[...] = (gate_ref[...] * upstream).astype(bf16)
            value = jnp.sum(upstream * attn_ref[...].astype(f32), axis=1, keepdims=True)
            d_logits = (gate_ref[...] * rest_ref[...] * value) * turn_ref[...]
            high = d_logits.astype(bf16)
            dl_ref[:, :lanes] = high
            dl_ref[:, lanes:] = (d_logits - high.astype(f32)).astype(bf16)

        dm_ref[0] = lax.dot_general(
            da_ref[...], o_ref[...], (((1,), (1,)), ((), ())), preferred_element_type=f32
        ).astype(bf16)

    return pl.pallas_call(
        kernel,
        grid=(experts,),
        in_specs=[full_spec((rows, width))] * 2
        + [full_spec((rows, 1))] * 2
        + [full_spec((rows, lanes)), pl.BlockSpec((group, width), lambda g: (g, 0))],
        out_specs=[
            full_spec((rows, width)),
            pl.BlockSpec((1, rows, group), lambda g: (g, 0, 0)),
            full_spec((rows, 2 * lanes)),
        ],
        out_shape=[
            jax.ShapeDtypeStruct((rows, width), bf16),
            jax.ShapeDtypeStruct((experts, rows, group), bf16),
            jax.ShapeDtypeStruct((rows, 2 * lanes), bf16),
        ],
        name="back_o",
        cost_estimate=work(2 * rows * inner * width, 2 * (inner * width + 4 * rows * width)),
    )(got, attn, gate, rest, turn, o_full)


def back_q(d_query, q_full, d_logits, router):
    experts, rows, group = d_query.shape
    width, inner = q_full.shape
    step = min(512, width)
    lanes = router.shape[1]

    def kernel(dq_ref, q_ref, dl_ref, router_ref, pair_ref, flat_ref):
        @pl.when(pl.program_id(0) == 0)
        def _():
            join_groups(dq_ref, flat_ref)

        dims = (((1,), (1,)), ((), ()))
        got = lax.dot_general(flat_ref[...], q_ref[...], dims, preferred_element_type=f32)
        for half in range(2):
            got = got + lax.dot_general(
                dl_ref[:, half * lanes : (half + 1) * lanes],
                router_ref[...],
                dims,
                preferred_element_type=f32,
            )
        pair_ref[...] = got.astype(bf16)

    return pl.pallas_call(
        kernel,
        grid=(width // step,),
        in_specs=[
            full_spec(d_query.shape),
            pl.BlockSpec((step, inner), lambda g: (g, 0)),
            full_spec((rows, 2 * lanes)),
            pl.BlockSpec((step, lanes), lambda g: (g, 0)),
        ],
        out_specs=[pl.BlockSpec((rows, step), lambda g: (0, g)), full_spec((rows, inner))],
        out_shape=[
            jax.ShapeDtypeStruct((rows, width), bf16),
            jax.ShapeDtypeStruct((rows, inner), bf16),
        ],
        name="back_q",
        cost_estimate=work(2 * rows * inner * width, 2 * (inner * width + 4 * rows * width)),
    )(d_query, q_full, d_logits, router)


def token_back(d_kv, kv_cols, d_pair, pick, rows, inverse):
    span, line = d_kv.shape
    width = kv_cols.shape[0]
    experts, slots, tokens = pick.shape
    step = min(512, width)

    def kernel(dkv_ref, kv_ref, pair_ref, pick_ref, x_ref, inv_ref, o_ref, dg_ref):
        got = lax.dot_general(
            dkv_ref[...], kv_ref[...], (((1,), (1,)), ((), ())), preferred_element_type=f32
        )
        gain = jnp.zeros((1, step), f32)
        for e in range(experts):
            part = slice(e * tokens, (e + 1) * tokens)
            extra = lax.dot_general(
                pick_ref[e],
                pair_ref[e * slots : (e + 1) * slots, :],
                (((0,), (0,)), ((), ())),
                preferred_element_type=f32,
            )
            d_a = got[part] + extra
            o_ref[e] = d_a.astype(bf16)
            scaled = x_ref[part, :].astype(f32) * inv_ref[part, :]
            gain = gain + jnp.sum(d_a * scaled, axis=0, keepdims=True)
        dg_ref[...] = gain

    return pl.pallas_call(
        kernel,
        grid=(width // step,),
        in_specs=[
            full_spec((span, line)),
            pl.BlockSpec((step, line), lambda g: (g, 0)),
            pl.BlockSpec((experts * slots, step), lambda g: (0, g)),
            full_spec(pick.shape),
            pl.BlockSpec((span, step), lambda g: (0, g)),
            full_spec((span, 1)),
        ],
        out_specs=[
            pl.BlockSpec((experts, tokens, step), lambda g: (0, 0, g)),
            pl.BlockSpec((1, step), lambda g: (0, g)),
        ],
        out_shape=[
            jax.ShapeDtypeStruct((experts, tokens, width), bf16),
            jax.ShapeDtypeStruct((1, width), f32),
        ],
        name="token_back",
        cost_estimate=work(2 * span * line * width, 2 * (line * width + 2 * span * width)),
    )(d_kv, kv_cols, d_pair, pick, rows, inverse)


def input_back_kernel(got_ref, x_ref, gain_ref, dm_ref, gx_ref):
    d_a = got_ref[0].astype(f32)
    for e in range(1, got_ref.shape[0]):
        d_a = d_a + got_ref[e].astype(f32)
    x = x_ref[...].astype(f32)
    inverse = lax.rsqrt(jnp.mean(x * x, axis=1, keepdims=True) + norm_eps)
    scaled = d_a * gain_ref[...]
    mean = jnp.mean(scaled * x, axis=1, keepdims=True)
    gx_ref[...] = dm_ref[...] + (inverse * scaled - x * (inverse * inverse * inverse * mean))


def input_back(got, x, gain, d_middle):
    tokens, width = x.shape
    return pl.pallas_call(
        input_back_kernel,
        out_shape=jax.ShapeDtypeStruct((tokens, width), f32),
        name="input_back",
        cost_estimate=work(10 * tokens * width, 20 * tokens * width),
    )(got, x, gain, d_middle)


def combine_kernel(back_ref, pick_ref, x_ref, gain_ref, middle_ref, inv_ref, b_ref):
    summed = lax.dot_general(
        pick_ref[...], back_ref[...], (((0,), (0,)), ((), ())), preferred_element_type=f32
    )
    middle = x_ref[...].astype(f32) + summed
    inverse = lax.rsqrt(jnp.mean(middle * middle, axis=1, keepdims=True) + norm_eps)
    middle_ref[...] = middle
    inv_ref[...] = inverse
    b_ref[...] = (middle * inverse * gain_ref[...]).astype(bf16)


def combine(back, pick, x, gain):
    tokens, width = x.shape
    return pl.pallas_call(
        combine_kernel,
        out_shape=[
            jax.ShapeDtypeStruct((tokens, width), f32),
            jax.ShapeDtypeStruct((tokens, 1), f32),
            jax.ShapeDtypeStruct((tokens, width), bf16),
        ],
        name="combine",
        cost_estimate=work(2 * back.shape[0] * tokens * width, 2 * back.shape[0] * width + 8 * tokens * width),
    )(back, pick, x, gain)


def middle_back_kernel(*refs):
    pieces = refs[:-8]
    middle_ref, inv_ref, cot_ref, gain_ref, pick_ref, dm_ref, dg_ref, rows_ref = refs[-8:]
    d_b = pieces[0][...].astype(f32)
    for piece in pieces[1:]:
        d_b = d_b + piece[...].astype(f32)
    middle, inverse = middle_ref[...], inv_ref[...]
    scaled = d_b * gain_ref[...]
    dg_ref[...] = jnp.sum(d_b * (middle * inverse), axis=0, keepdims=True)
    mean = jnp.mean(scaled * middle, axis=1, keepdims=True)
    d_middle = cot_ref[...].astype(f32) + (
        inverse * scaled - middle * (inverse * inverse * inverse * mean)
    )
    dm_ref[...] = d_middle
    rows_ref[...] = jnp.dot(
        pick_ref[...], d_middle.astype(bf16), preferred_element_type=f32
    ).astype(bf16)


def middle_back(pieces, middle, inverse, cot, gain, pick):
    tokens, width = middle.shape
    return pl.pallas_call(
        middle_back_kernel,
        out_shape=[
            jax.ShapeDtypeStruct((tokens, width), f32),
            jax.ShapeDtypeStruct((1, width), f32),
            jax.ShapeDtypeStruct((pick.shape[0], width), bf16),
        ],
        name="middle_back",
        cost_estimate=work(2 * pick.shape[0] * tokens * width, 2 * pick.shape[0] * width + 20 * tokens * width),
    )(*pieces, middle, inverse, cot, gain, pick)


def dispatch(blocks, pick):
    stages, pairs, tokens = pick.shape
    width = blocks[0].shape[1]
    step = min(512, width)

    def kernel(pick_ref, *refs):
        for k in range(stages):
            refs[-1][:, k] = (
                jnp.dot(pick_ref[k], refs[k][...], preferred_element_type=f32)
                .astype(bf16)
                .reshape(refs[-1].shape[0], refs[-1].shape[2], step)
            )

    return lambda experts: pl.pallas_call(
        kernel,
        grid=(width // step,),
        in_specs=[full_spec(pick.shape)]
        + [pl.BlockSpec((tokens, step), lambda g: (0, g)) for _ in blocks],
        out_specs=pl.BlockSpec((experts, stages, pairs // experts, step), lambda g: (0, 0, 0, g)),
        out_shape=jax.ShapeDtypeStruct((experts, stages, pairs // experts, width), bf16),
        name="dispatch",
        cost_estimate=work(2 * stages * pairs * tokens * width, 2 * stages * (pairs + tokens) * width),
    )(pick, *blocks)


def collect(rows, pick, order):
    experts, stages, slots, width = rows.shape
    tokens = pick.shape[2]

    def kernel(order_ref, pick_ref, rows_ref, o_ref):
        gathered = rows_ref[...].reshape(experts * slots, width)
        o_ref[0] = lax.dot_general(
            pick_ref[0], gathered, (((0,), (0,)), ((), ())), preferred_element_type=f32
        ).astype(bf16)

    return pl.pallas_call(
        kernel,
        grid_spec=pltpu.PrefetchScalarGridSpec(
            num_scalar_prefetch=1,
            grid=(stages,),
            in_specs=[
                pl.BlockSpec((1, experts * slots, tokens), lambda k, o: (k, 0, 0)),
                pl.BlockSpec((experts, 1, slots, width), lambda k, o: (0, k, 0, 0)),
            ],
            out_specs=pl.BlockSpec((1, tokens, width), lambda k, o: (o[k], 0, 0)),
        ),
        out_shape=jax.ShapeDtypeStruct((stages, tokens, width), bf16),
        name="collect",
        cost_estimate=work(2 * stages * experts * slots * tokens * width, 2 * stages * (experts * slots + tokens) * width),
    )(order, pick, rows)


def collect_each(rows, pick):
    experts, stages, slots, width = rows.shape
    tokens = pick.shape[2]

    def kernel(pick_ref, rows_ref, *outs):
        gathered = rows_ref[...].reshape(experts * slots, width)
        summed = lax.dot_general(
            pick_ref[0], gathered, (((0,), (0,)), ((), ())), preferred_element_type=f32
        ).astype(bf16)
        for k in range(stages):

            @pl.when(pl.program_id(0) == k)
            def _(ref=outs[k]):
                ref[...] = summed

    return pl.pallas_call(
        kernel,
        grid=(stages,),
        in_specs=[
            pl.BlockSpec((1, experts * slots, tokens), lambda k: (k, 0, 0)),
            pl.BlockSpec((experts, 1, slots, width), lambda k: (0, k, 0, 0)),
        ],
        out_specs=[full_spec((tokens, width))] * stages,
        out_shape=[jax.ShapeDtypeStruct((tokens, width), bf16)] * stages,
        name="collect_each",
        cost_estimate=work(2 * stages * experts * slots * tokens * width, 2 * stages * (experts * slots + tokens) * width),
    )(pick, rows)


def feed_grads(rows, d_gates, d_ups, d_logits):
    count, width = rows[0].shape
    part, lanes = d_gates[0].shape[1], d_logits[0].shape[1]
    held = len(rows)
    step = min(256, width)

    def kernel(*refs):
        ins, outs = refs[: 4 * held], refs[4 * held :]
        for kind, out in enumerate(outs):
            total = None
            for m in range(held):
                got = lax.dot_general(
                    ins[m][...],
                    ins[held * (kind + 1) + m][...],
                    (((0,), (0,)), ((), ())),
                    preferred_element_type=f32,
                )
                total = got if total is None else total + got
            out[...] = total.astype(out.dtype)

    def resident(array):
        return pl.BlockSpec(array.shape, lambda g: (0, 0), pipeline_mode=pl.Buffered(1))

    others = (*d_gates, *d_ups, *d_logits)
    return pl.pallas_call(
        kernel,
        grid=(width // step,),
        in_specs=[pl.BlockSpec((count, step), lambda g: (0, g)) for _ in rows]
        + [resident(x) for x in others],
        out_specs=[pl.BlockSpec((step, n), lambda g: (g, 0)) for n in (part, part, lanes)],
        out_shape=[
            jax.ShapeDtypeStruct((width, part), bf16),
            jax.ShapeDtypeStruct((width, part), bf16),
            jax.ShapeDtypeStruct((width, lanes), f32),
        ],
        name="feed_grads",
        cost_estimate=work(4 * held * count * width * part, 2 * (held * count * (width + 2 * part) + 2 * width * part)),
    )(*rows, *others)


def cut(place, gate, up):
    rows, hidden = gate.shape
    stages = place.shape[0] - 2
    part = hidden // stages

    def kernel(place_ref, gate_ref, up_ref, *outs):
        for k in range(stages):

            @pl.when(pl.program_id(0) == k)
            def _(ref=outs[k]):
                ref[0] = gate_ref[...]
                ref[1] = up_ref[...]

    block = pl.BlockSpec((rows, part), lambda g, p: (0, p[2 + g]))
    return pl.pallas_call(
        kernel,
        grid_spec=pltpu.PrefetchScalarGridSpec(
            num_scalar_prefetch=1,
            grid=(stages,),
            in_specs=[block, block],
            out_specs=[full_spec((2, rows, part))] * stages,
        ),
        out_shape=[jax.ShapeDtypeStruct((2, rows, part), bf16)] * stages,
        name="cut",
        cost_estimate=work(0, 8 * stages * rows * part),
    )(place, gate, up)


def other_half(place, gate, up, stages):
    width, part = gate.shape
    rows = width // (2 * stages)

    def kernel(place_ref, gate_ref, up_ref, o_ref):
        o_ref[0, 0] = gate_ref[...]
        o_ref[0, 1] = up_ref[...]

    block = pl.BlockSpec((rows, part), lambda g, p: (2 * g + 1 - p[1], 0))
    return pl.pallas_call(
        kernel,
        grid_spec=pltpu.PrefetchScalarGridSpec(
            num_scalar_prefetch=1,
            grid=(stages,),
            in_specs=[block, block],
            out_specs=pl.BlockSpec((1, 2, rows, part), lambda g, p: (g, 0, 0, 0)),
        ),
        out_shape=jax.ShapeDtypeStruct((stages, 2, rows, part), bf16),
        name="other_half",
        cost_estimate=work(0, 8 * stages * rows * part),
    )(place, gate, up)


def own_half(place, gate, up, other):
    stages, _, rows, part = other.shape

    def kernel(place_ref, gate_ref, up_ref, other_ref, *outs):
        for k in range(stages):

            @pl.when(pl.program_id(0) == k)
            def _(ref=outs[k]):
                ref[0] = (gate_ref[...].astype(f32) + other_ref[0, 0].astype(f32)).astype(bf16)
                ref[1] = (up_ref[...].astype(f32) + other_ref[0, 1].astype(f32)).astype(bf16)

    block = pl.BlockSpec((rows, part), lambda g, p: (2 * p[2 + g] + p[1], 0))
    return pl.pallas_call(
        kernel,
        grid_spec=pltpu.PrefetchScalarGridSpec(
            num_scalar_prefetch=1,
            grid=(stages,),
            in_specs=[
                block,
                block,
                pl.BlockSpec((1, 2, rows, part), lambda g, p: (p[2 + g], 0, 0, 0)),
            ],
            out_specs=[full_spec((2, rows, part))] * stages,
        ),
        out_shape=[jax.ShapeDtypeStruct((2, rows, part), bf16)] * stages,
        name="own_half",
        cost_estimate=work(0, 12 * stages * rows * part),
    )(place, gate, up, other)


def assemble(place, mine, theirs):
    stages = len(mine)
    _, rows, part = mine[0].shape

    def kernel(place_ref, *refs):
        ins, (gate_ref, up_ref) = refs[:-2], refs[-2:]
        step = pl.program_id(0)
        hop = (place_ref[0] - step // 2) % stages
        here = step % 2 == place_ref[1]
        for k in range(stages):
            for which in range(2):

                @pl.when((hop == k) & (here == (which == 0)))
                def _(ref=ins[which * stages + k]):
                    gate_ref[...] = ref[0]
                    up_ref[...] = ref[1]

    block = pl.BlockSpec((rows, part), lambda g, p: (g, 0))
    shape = jax.ShapeDtypeStruct((2 * stages * rows, part), bf16)
    return pl.pallas_call(
        kernel,
        grid_spec=pltpu.PrefetchScalarGridSpec(
            num_scalar_prefetch=1,
            grid=(2 * stages,),
            in_specs=[
                pl.BlockSpec((2, rows, part), lambda g, p: (0, 0, 0), pipeline_mode=pl.Buffered(1))
            ]
            * (2 * stages),
            out_specs=[block, block],
        ),
        out_shape=[shape, shape],
        name="assemble",
        cost_estimate=work(0, 12 * stages * rows * part),
    )(place, *mine, *theirs)


def widen(place, got):
    stages = len(got)
    _, rows, part = got[0].shape

    def kernel(place_ref, *refs):
        hop = (place_ref[0] - pl.program_id(0)) % stages
        for k in range(stages):

            @pl.when(hop == k)
            def _(ref=refs[k]):
                for half in range(2):
                    refs[half - 2][0] = ref[half].astype(f32)

    block = pl.BlockSpec((1, rows, part), lambda g, p: (0, 0, g))
    shape = jax.ShapeDtypeStruct((1, rows, stages * part), f32)
    return pl.pallas_call(
        kernel,
        grid_spec=pltpu.PrefetchScalarGridSpec(
            num_scalar_prefetch=1,
            grid=(stages,),
            in_specs=[full_spec((2, rows, part))] * stages,
            out_specs=[block, block],
        ),
        out_shape=[shape, shape],
        name="widen",
        cost_estimate=work(0, 12 * stages * rows * part),
    )(place, *got)


def feed_kernel(own_ref, r_ref, g_ref, other_ref, router_ref, wg_ref, wu_ref, wd_ref, *outs):
    out_ref, db_ref, low_ref, dg_ref, du_ref, dr_ref, dl_ref = outs
    rows, grads = r_ref[...], g_ref[...].astype(f32)
    router = router_ref[...]
    logits = jnp.dot(rows, router, preferred_element_type=f32)
    column = lax.broadcasted_iota(jnp.int32, logits.shape, 1)
    turn = (column == own_ref[0]).astype(f32) - (column == other_ref[...]).astype(f32)
    lead = jnp.sum(logits * turn, axis=1, keepdims=True)
    gate, rest = jax.nn.sigmoid(lead), jax.nn.sigmoid(-lead)
    d_rows = (gate * grads).astype(bf16)
    dr_ref[...] = d_rows
    gate_pre = jnp.dot(rows, wg_ref[...], preferred_element_type=f32)
    up_pre = jnp.dot(rows, wu_ref[...], preferred_element_type=f32)
    d_low = lax.dot_general(
        d_rows, wd_ref[...], (((1,), (1,)), ((), ())), preferred_element_type=f32
    )
    sigma = jax.nn.sigmoid(gate_pre)
    silu = gate_pre * sigma
    low = (silu * up_pre).astype(bf16)
    low_ref[...] = low
    d_up = (d_low * silu).astype(bf16)
    du_ref[...] = d_up
    d_gate = (d_low * up_pre * (sigma + silu * (1.0 - sigma))).astype(bf16)
    dg_ref[...] = d_gate
    result = jnp.dot(low, wd_ref[...], preferred_element_type=f32)
    out_ref[...] = (gate * result).astype(bf16)
    d_value = jnp.sum(grads * result, axis=1, keepdims=True)
    d_logits = (gate * rest * d_value) * turn
    high = d_logits.astype(bf16)
    small = (d_logits - high.astype(f32)).astype(bf16)
    half = high.shape[1]
    dl_ref[:, :half] = high
    dl_ref[:, half:] = small
    d_b = lax.dot_general(
        d_gate, wg_ref[...], (((1,), (1,)), ((), ())), preferred_element_type=f32
    ) + lax.dot_general(d_up, wu_ref[...], (((1,), (1,)), ((), ())), preferred_element_type=f32)
    for piece in (high, small):
        d_b = d_b + lax.dot_general(
            piece, router, (((1,), (1,)), ((), ())), preferred_element_type=f32
        )
    db_ref[...] = d_b.astype(bf16)


def feed(own, rows, grads, other, router, wg, wu, wd):
    count, width = rows.shape
    part = wg.shape[1]
    step = min(256, count)
    lanes = router.shape[1]

    def by_rows(columns):
        return pl.BlockSpec((step, columns), lambda g, s: (g, 0))

    def held(shape):
        return pl.BlockSpec(shape, lambda g, s: (0, 0), pipeline_mode=pl.Buffered(1))

    def shape(columns):
        return jax.ShapeDtypeStruct((count, columns), bf16)

    widths = (width, width, part, part, part, width, 2 * lanes)
    return pl.pallas_call(
        feed_kernel,
        grid_spec=pltpu.PrefetchScalarGridSpec(
            num_scalar_prefetch=1,
            grid=(count // step,),
            in_specs=[by_rows(width), by_rows(width), by_rows(1)]
            + [held(w.shape) for w in (router, wg, wu, wd)],
            out_specs=[by_rows(w) for w in widths],
        ),
        out_shape=[shape(w) for w in widths],
        name="feed",
        cost_estimate=work(12 * count * width * part, 6 * width * part + 2 * count * (5 * width + 3 * part), count * part),
    )(own, rows, grads, other, router, wg, wu, wd)


def after(array, *others):
    return lax.optimization_barrier((array, *others))[0]


def per_device(
    inputs,
    attn_routes,
    mlp_routes,
    pic_start,
    kv_weight,
    router_weight,
    norm_gains,
    q_weight,
    o_weight,
    gate_weight,
    up_weight,
    down_weight,
    cotangent,
):
    experts = lax.axis_size("expert")
    dp_size = lax.axis_size("dp")
    stages = dp_size // 2
    own = lax.axis_index("expert")
    dp_index = lax.axis_index("dp")
    stage, core = dp_index // 2, dp_index % 2
    tokens, width = inputs.shape[2], inputs.shape[3]
    inner = HEADS * HSZ
    group = inner // experts
    slots = tokens * TOPK // experts
    span = tokens * experts
    rows_each = kv_weight.shape[0]
    hidden = gate_weight.shape[2]
    part = hidden // stages
    routed = experts * slots
    same_core = [[z * 2 + c for z in range(stages)] for c in range(2)]

    def exchange(blocks):
        return lax.all_to_all(blocks, "expert", 0, 0, tiled=True)

    def spread(block):
        return exchange(jnp.broadcast_to(block[None], (experts,) + block.shape))

    def along(block, k):
        if k % stages == 0:
            return block
        return lax.ppermute(
            block, "dp", [(j, ((j // 2 + k) % stages) * 2 + j % 2) for j in range(dp_size)]
        )

    def partner(block):
        return lax.ppermute(block, "dp", [(j, j ^ 1) for j in range(dp_size)])

    def pick(array, index, axis=0):
        return lax.dynamic_index_in_dim(array, index, axis, keepdims=False)

    small = jnp.concatenate(
        [
            attn_routes.reshape(-1).astype(bf16),
            mlp_routes.reshape(-1).astype(bf16),
            router_weight.reshape(-1),
            norm_gains.reshape(-1),
        ]
    )
    length = small.shape[0]
    line = 2 * group
    extra = -(-length // (16 * line)) * 16
    small = jnp.pad(small, (0, extra * line - length)).reshape(1, extra, line)
    kv_split = kv_weight.reshape(rows_each, 2, experts, group).transpose(2, 0, 1, 3)
    first = jnp.concatenate(
        [
            jnp.broadcast_to(inputs, (experts, MICRO, tokens, width)).reshape(experts, -1, width),
            kv_split.reshape(experts, rows_each * line // width, width),
            jnp.broadcast_to(small.reshape(1, -1, width), (experts, extra * line // width, width)),
        ],
        axis=1,
    )
    first = exchange(first)
    x_blocks = first[:, : MICRO * tokens].reshape(experts, MICRO, tokens, width)
    kv_rows = first[:, MICRO * tokens :].reshape(experts, rows_each + extra, line)
    stage_order = (stage - jnp.arange(stages, dtype=jnp.int32)) % stages
    place = jnp.arange(experts, dtype=jnp.int32)
    cot_stages = lax.all_gather(cotangent[0], "dp", axis=0, axis_index_groups=same_core)
    route_rows = mlp_routes[0].reshape(-1).astype(bf16)
    route_rows = jnp.pad(route_rows, (0, -route_rows.shape[0] % 128)).reshape(-1, 128)
    own_routes = jnp.stack([along(route_rows, k) for k in range(stages)]).reshape(stages, -1)
    own_routes = own_routes[:, : MICRO * tokens * TOPK].astype(jnp.int32)
    own_routes = own_routes.reshape(stages, MICRO, tokens, TOPK)
    home_m = selection(
        (own_routes[:, None] == place[None, :, None, None, None]).any(-1).astype(f32), slots
    )
    home_m = home_m.transpose(2, 0, 1, 3, 4).reshape(MICRO, stages, experts * slots, tokens)
    q_full = lax.all_gather(after(q_weight[0], cot_stages, first), "dp", axis=0, tiled=True)
    cot_rows = {}
    for m in ORDER:
        blocks = [pick(cot_stages, stage_order[k])[m] for k in range(stages)]
        cot_rows[m] = exchange(dispatch(blocks, home_m[m])(experts))
    kv_rows = after(kv_rows, q_full, cot_rows[ORDER[0]])
    kv_got = lax.all_gather(kv_rows, "dp", axis=0)

    forward_order = (stage + jnp.arange(stages, dtype=jnp.int32)) % stages
    where = jnp.concatenate([jnp.stack([stage, core]), forward_order]).astype(jnp.int32)
    if part % 128 == 0:
        mine = list(cut(where, gate_weight[0], up_weight[0]))
    else:
        both = jnp.stack([gate_weight[0], up_weight[0]]).reshape(2, -1, stages, part)
        mine = [pick(both, forward_order[k], 2) for k in range(stages)]
    for k in range(1, stages):
        mine[k] = along(after(mine[k], kv_rows), k)
    kv_cols = kv_got[:, :, :rows_each].reshape(width, line)
    small = kv_got[:, :, rows_each:].reshape(dp_size, experts, extra * line)
    count = MICRO * tokens * TOPK
    routes_a = pick(small[:, :, :count], dp_index).astype(jnp.int32)
    routes_a = routes_a.reshape(experts, MICRO, tokens, TOPK)
    routes_m = small[:, :, count : 2 * count].reshape(stages, 2, experts, count)
    routes_m = pick(routes_m, core, 1).astype(jnp.int32)
    routes_m = routes_m.reshape(stages, experts, MICRO, tokens, TOPK)[stage_order]
    router = small[:, :, 2 * count : 2 * count + rows_each * 2 * experts].reshape(
        width, 2 * experts
    )
    gains = small[:, :, 2 * count + rows_each * 2 * experts : length].reshape(width, 2)
    gain_1, gain_2 = gains[:, 0].astype(f32)[None], gains[:, 1].astype(f32)[None]
    router_a = jnp.pad(router[:, :experts], ((0, 0), (0, 128 - experts)))
    router_m = jnp.pad(router[:, experts:], ((0, 0), (0, 128 - experts)))

    x_low = x_blocks.transpose(1, 0, 2, 3).reshape(MICRO, span, width)
    x_all = x_low.astype(f32)
    x_inverse = inverse_rms(x_all)
    a_all = (x_all * x_inverse * gain_1).astype(bf16)

    token = jnp.arange(tokens, dtype=jnp.int32)
    chosen = (routes_a[None] == place[:, None, None, None, None]).any(-1)
    pick_all = selection(chosen.transpose(0, 2, 1, 3).astype(f32), slots)
    query_pos = jnp.einsum(
        "emkst,t->emks", pick_all, token.astype(bf16), preferred_element_type=f32
    ).astype(jnp.int32)
    query_pos = (
        query_pos
        + place[:, None] * tokens
        + jnp.arange(MICRO, dtype=jnp.int32)[:, None, None] * span
    )
    query_pos = query_pos.transpose(1, 0, 2, 3).reshape(MICRO, experts, routed, 1)
    pick_a = pick(pick_all, own)
    other_a = jnp.einsum(
        "mkst,kmt->mks",
        pick_a,
        (routes_a.sum(-1) - own).astype(bf16),
        preferred_element_type=f32,
    ).astype(jnp.int32)
    other_a = other_a.reshape(MICRO, routed, 1)
    home_a = pick(pick_all, own, 2).transpose(1, 0, 2, 3).reshape(MICRO, routed, tokens)
    pick_m = selection((routes_m == own).any(-1).astype(f32), slots)
    other_m = jnp.einsum(
        "kemst,kemt->mkes",
        pick_m,
        (routes_m.sum(-1) - own).astype(bf16),
        preferred_element_type=f32,
    ).astype(jnp.int32)
    other_m = other_m.transpose(0, 2, 1, 3).reshape(MICRO, experts * stages * slots, 1)

    key_cos, key_sin = rope_tables(jnp.arange(MICRO * span, dtype=jnp.int32).reshape(MICRO, span))
    query_cos, query_sin = rope_tables(query_pos[..., 0])
    kv_own = project_kv(
        a_all,
        kv_cols,
        jnp.stack([key_cos, jnp.ones_like(key_cos)], axis=1),
        jnp.stack([key_sin, jnp.zeros_like(key_sin)], axis=1),
    )
    kvs = [kv_own[m] for m in range(MICRO)]

    a_pairs = jnp.einsum(
        "mest,metd->mesd",
        pick_a,
        a_all.reshape(MICRO, experts, tokens, width),
        preferred_element_type=f32,
    ).astype(bf16)
    a_pairs = a_pairs.reshape(MICRO, routed, width)
    column = jnp.arange(128, dtype=jnp.int32)[None, None, :]
    turn_a = (column == own).astype(f32) - (column == other_a).astype(f32)
    lead = jnp.sum(mm(a_pairs, router_a) * turn_a, axis=-1, keepdims=True)
    gate_a, rest_a = jax.nn.sigmoid(lead), jax.nn.sigmoid(-lead)
    q_out = project_q(
        a_pairs.reshape(MICRO * routed, width),
        q_full,
        pick(query_cos, own, 1).reshape(MICRO * routed, HSZ),
        pick(query_sin, own, 1).reshape(MICRO * routed, HSZ),
        MICRO,
        experts,
    )

    down_other = partner(down_weight[0])
    down_w = jnp.concatenate(
        [
            jnp.where(core == 0, down_weight[0], down_other),
            jnp.where(core == 0, down_other, down_weight[0]),
        ]
    )
    start = after(pic_start.astype(jnp.int32), down_w)
    held = lax.optimization_barrier(
        (o_weight[0], *mine, q_out, *kvs, home_a, cot_rows[ORDER[1]], other_m, gate_a, down_w)
    )
    mine = list(held[1 : 1 + stages])
    o_full = lax.all_gather(held[0], "dp", axis=0, tiled=True)
    queries, mixed, peaks, attn, middles, inverses, feeds = {}, {}, {}, {}, {}, {}, {}
    mixed_got = {}
    for m in ORDER:
        queries[m] = exchange(q_out[m])
        heads, peaks[m] = attend(queries[m], query_pos[m], kvs[: m + 1], start)
        mixed_got[m] = exchange(heads)
    gate_w, up_w = assemble(where, mine, [partner(piece) for piece in mine])
    first_mixed = after(mixed_got[ORDER[0]], gate_w, heads)
    gated = {}
    for m in ORDER:
        attn[m], gated[m], mixed[m] = project_o(
            first_mixed if m == ORDER[0] else mixed_got[m], o_full, gate_a[m]
        )

    b_blocks = {}
    for m in ORDER:
        back = exchange(gated[m].reshape(experts, slots, width))
        if m == ORDER[0]:
            back = after(back, gated[ORDER[1]])
        middles[m], inverses[m], b_low = combine(
            back.reshape(routed, width), home_a[m], inputs[0, m], gain_2
        )
        b_blocks[m] = [along(b_low, k) for k in range(stages)]
    held = lax.optimization_barrier((*b_blocks[ORDER[0]], b_low))
    b_blocks[ORDER[0]] = list(held[:stages])
    for m in ORDER:
        sent = dispatch(b_blocks[m], home_m[m])(experts)
        feeds[m] = exchange(sent)
    feeds[ORDER[0]] = after(feeds[ORDER[0]], sent)

    pairs = experts * stages * slots
    own_id = own.reshape(1).astype(jnp.int32)
    outs, d_pieces, d_rows, kept_feed = {}, {}, {}, {}
    for m in ORDER:
        rows = feeds[m].reshape(pairs, width)
        if kept_feed:
            rows = after(rows, kept_feed[ORDER[0]][4])
        outs[m], d_b, *kept_feed[m] = feed(
            own_id,
            rows,
            cot_rows[m].reshape(pairs, width),
            other_m[m],
            router_m,
            gate_w,
            up_w,
            down_w,
        )
        d_rows[m] = exchange(d_b.reshape(experts, stages, slots, width))

    def joined(index):
        return jnp.concatenate([kept_feed[m][index] for m in ORDER])

    def over_stages(rows, m):
        summed = collect(rows, home_m[m], stage_order)
        return summed, lax.psum_scatter(
            summed, "dp", scatter_dimension=0, tiled=True, axis_index_groups=same_core
        )[0]

    early, d_pieces[ORDER[0]] = over_stages(after(d_rows[ORDER[0]], d_b), ORDER[0])
    late, d_pieces[ORDER[1]] = over_stages(
        after(d_rows[ORDER[1]], d_pieces[ORDER[0]]), ORDER[1]
    )
    out_rows = exchange(
        after(outs[ORDER[0]], d_rows[ORDER[1]]).reshape(experts, stages, slots, width)
    )
    gate_grad, up_grad, router_m_grad = feed_grads(
        [after(feeds[m].reshape(pairs, width), d_pieces[ORDER[1]]) for m in ORDER],
        [kept_feed[m][1] for m in ORDER],
        [kept_feed[m][2] for m in ORDER],
        [kept_feed[m][4] for m in ORDER],
    )
    summed, out_sum = over_stages(after(out_rows, d_pieces[ORDER[1]]), ORDER[0])
    out_sums = {ORDER[0]: out_sum}

    def scattered(grad):
        return lax.psum_scatter(grad, "dp", scatter_dimension=0, tiled=True)

    def ordered(values):
        return jnp.concatenate([values[m] for m in ORDER])

    gain_2_grad = jnp.zeros((1, width), f32)
    d_middles, d_attn, d_flat, d_pairs, d_kvs, logit_grads, later = {}, {}, {}, {}, {}, {}, []
    for m in ORDER:
        d_middles[m], gain_part, sent = middle_back(
            [d_pieces[m]], middles[m], inverses[m], cotangent[0, m], gain_2, home_a[m]
        )
        gain_2_grad = gain_2_grad + gain_part
        if m == ORDER[0]:
            sent = after(sent, out_rows)
        got = exchange(sent.reshape(experts, slots, width)).reshape(routed, width)
        if m == ORDER[0]:
            got = after(got, gate_grad, summed)
        d_attn[m], d_heads, logit_grads[m] = back_o(
            got, attn[m], gate_a[m], rest_a[m], turn_a[m], o_full, experts
        )
        d_heads = exchange(d_heads)
        if m == ORDER[1]:
            o_grad = t_mm(ordered(mixed), ordered(d_attn)).astype(bf16)
            d_heads = after(d_heads, o_grad)
        d_query, d_kvs[m], *later = attend_back(
            queries[m],
            d_heads,
            query_cos[m],
            query_sin[m],
            query_pos[m],
            kvs[: m + 1],
            key_cos[m],
            key_sin[m],
            later,
            start,
        )
        d_query = exchange(d_query)
        if m == ORDER[1]:
            kv_grad = t_mm(ordered(a_all), ordered(d_kvs)).astype(bf16)
            d_query = after(d_query, kv_grad)
        d_pairs[m], d_flat[m] = back_q(d_query, q_full, logit_grads[m], router_a)

    pair_rows = ordered(a_pairs)
    q_grad = t_mm(pair_rows, ordered(d_flat)).astype(bf16)
    d_pairs[ORDER[1]] = after(d_pairs[ORDER[1]], q_grad)
    router_a_grad = t_mm(pair_rows, ordered(logit_grads))
    router_a_grad = router_a_grad[:, :experts] + router_a_grad[:, 128 : 128 + experts]
    o_in, out_sums[ORDER[0]] = lax.optimization_barrier((o_grad, out_sums[ORDER[0]]))
    o_mine = scattered(o_in)
    kv_in, o_mine = lax.optimization_barrier((kv_grad, o_mine))
    kv_mine = scattered(kv_in)
    q_in, kv_mine = lax.optimization_barrier((q_grad, kv_mine))
    q_mine = scattered(q_in)
    other = partner(other_half(where, gate_grad, after(up_grad, q_grad), stages))
    total = list(own_half(where, gate_grad, up_grad, other))
    own_ready = total[0]
    total[1] = along(total[1], 1)
    down_grad = t_mm(after(joined(0), own_ready), joined(3)).astype(bf16)
    o_share = o_mine.astype(f32)[None]
    router_m_grad = router_m_grad[:, :experts] + router_m_grad[:, 128 : 128 + experts]
    down_split = down_grad.reshape(2, part // 2, width)
    down_share = (
        pick(down_split, core).astype(f32) + partner(pick(down_split, 1 - core)).astype(f32)
    )[None]


    d_pairs[ORDER[0]], total[0] = lax.optimization_barrier((d_pairs[ORDER[0]], total[0]))
    d_pairs[ORDER[1]], total[1] = lax.optimization_barrier((d_pairs[ORDER[1]], total[1]))
    for k in range(2, stages):
        total[k] = along(after(total[k], total[k - 1] if k == 2 else total[k - 2]), k)
    grad_x = [None] * MICRO
    d_as, gain_1_grad = {}, jnp.zeros((1, width), f32)
    for m in ORDER:
        d_a, gain_part = token_back(
            d_kvs[m], kv_cols, d_pairs[m], pick_a[m], x_low[m], x_inverse[m]
        )
        d_as[m] = exchange(d_a)
        gain_1_grad = gain_1_grad + gain_part
    out_rows = exchange(
        after(outs[ORDER[1]], d_query).reshape(experts, stages, slots, width)
    )
    summed = collect(out_rows, home_m[ORDER[1]], stage_order)
    out_in, q_mine = lax.optimization_barrier((summed, q_mine))
    out_sums[ORDER[1]] = lax.psum_scatter(
        out_in, "dp", scatter_dimension=0, tiled=True, axis_index_groups=same_core
    )[0]
    for m in ORDER:
        got = d_as[m]
        if m == ORDER[0]:
            got, total[2] = lax.optimization_barrier((got, total[2]))
        grad_x[m] = input_back(got, inputs[0, m], gain_1, d_middles[m])
    if part % 128 == 0:
        gate_share, up_share = widen(where, total)
    else:
        got = jnp.stack(total)[stage_order].astype(f32)
        shares = jnp.concatenate([got[s] for s in range(stages)], axis=2)
        gate_share, up_share = shares[:1], shares[1:]
    grad_x = jnp.stack(grad_x)[None]

    out_act = jnp.stack([middles[m] + out_sums[m].astype(f32) for m in range(MICRO)])
    out_act = out_act.astype(bf16)[None]
    kv_got = exchange(kv_mine.reshape(experts, rows_each, line)).reshape(experts, rows_each, 2, group)
    kv_share = kv_got.transpose(1, 2, 0, 3).reshape(rows_each, 2 * inner).astype(f32)

    tail = jnp.concatenate(
        [router_a_grad.T, router_m_grad.T, gain_1_grad, gain_2_grad], axis=0
    )
    kinds = 2 * experts + 2
    tail, q_mine = lax.optimization_barrier((jnp.pad(tail, ((0, -kinds % 8), (0, 0))), q_mine))
    q_share = q_mine.astype(f32)[None]
    tail = tail.reshape(-1, dp_size, width // dp_size)
    tail = lax.psum_scatter(
        tail.transpose(1, 0, 2), "dp", scatter_dimension=0, tiled=True
    )
    tail = tail.reshape(-1, experts, rows_each).transpose(1, 0, 2)
    tail = lax.psum_scatter(tail, "expert", scatter_dimension=0, tiled=True)[0].T
    router_share, gains_share = tail[:, : 2 * experts], tail[:, 2 * experts : kinds]

    largest = after(jnp.maximum(peaks[0], peaks[1])[:, :, 0, 0], summed, grad_x)
    mine_here = jnp.arange(HEADS, dtype=jnp.int32) // (HEADS // experts) == own
    largest = jnp.where(mine_here[None], jnp.tile(largest, (1, experts)), masked_low)
    largest = jnp.pad(largest, ((0, 0), (0, 128 - HEADS)))
    for axis, size in (("dp", dp_size), ("expert", experts)):
        hop = 1
        while hop < size:
            largest = jnp.maximum(
                largest, lax.ppermute(largest, axis, [(j, j ^ hop) for j in range(size)])
            )
            hop *= 2
    ratio = logit_cap / jnp.maximum(largest[:, :HEADS], logit_cap)
    root_q = jnp.repeat(jnp.sqrt(pick(ratio, own)), HSZ)[None]
    root_k = jnp.repeat(jnp.sqrt(jnp.min(ratio, axis=0)), HSZ)[None]
    clipped_q = (q_weight.astype(f32) * root_q[None]).astype(bf16)
    clipped_key = (kv_weight[:, :inner].astype(f32) * root_k).astype(bf16)
    return (
        out_act,
        grad_x,
        kv_share,
        router_share,
        gains_share,
        q_share,
        o_share,
        gate_share,
        up_share,
        down_share,
        clipped_q,
        clipped_key,
    )


def solution(mesh):
    tokens4 = P("dp", None, "expert", None)
    rows2 = P(("dp", "expert"), None)
    weights3 = P("expert", "dp", None)
    return jax.shard_map(
        per_device,
        mesh=mesh,
        in_specs=(tokens4,) * 3 + (P("dp"),) + (rows2,) * 3 + (weights3,) * 5 + (tokens4,),
        out_specs=(tokens4,) * 2 + (rows2,) * 3 + (weights3,) * 6 + (rows2,),
        check_vma=False,
    )
```

```python
import math

import jax
import jax.numpy as jnp
from jax import lax
from jax.experimental import pallas as pl
from jax.experimental.pallas import tpu as pltpu
from jax.sharding import PartitionSpec as P

HEADS = 16
HSZ = 128
TOPK = 2
PIC = 256
MICRO = 2
ORDER = (1, 0)

norm_eps = 1e-06
logit_cap = 8.0
masked_low = -1e30
bf16 = jnp.bfloat16
f32 = jnp.float32


def mm(left, right):
    return jnp.dot(left, right, preferred_element_type=f32)


def mm_t(left, right):
    return lax.dot_general(left, right, (((1,), (1,)), ((), ())), preferred_element_type=f32)


def t_mm(left, right):
    return lax.dot_general(left, right, (((0,), (0,)), ((), ())), preferred_element_type=f32)


def rope_tables(positions):
    half = HSZ // 2
    freq = jnp.exp(jnp.arange(half, dtype=f32) * (-math.log(10000.0) / half))
    angles = positions.astype(f32)[..., None] * freq
    cosine, sine = jnp.cos(angles), jnp.sin(angles)
    return (
        jnp.concatenate([cosine, cosine], axis=-1),
        jnp.concatenate([-sine, sine], axis=-1),
    )


def inverse_rms(values):
    return lax.rsqrt(jnp.mean(values * values, axis=-1, keepdims=True) + norm_eps)


def selection(hot, slots):
    tokens = hot.shape[-1]
    before = jnp.triu(jnp.ones((tokens, tokens), bf16), 1)
    rank = jnp.dot(hot.astype(bf16), before, preferred_element_type=f32)
    slot = jnp.arange(slots, dtype=jnp.int32)[:, None]
    taken = (rank.astype(jnp.int32)[..., None, :] == slot) & (hot[..., None, :] > 0)
    return taken.astype(bf16)


def full_spec(shape):
    return pl.BlockSpec(shape, lambda *_: (0,) * len(shape))


def work(flops, moved, exps=0):
    return pl.CostEstimate(flops=flops, bytes_accessed=moved, transcendentals=exps)


def kv_kernel(a_ref, w_ref, cos_ref, sin_ref, o_ref):
    got = jnp.dot(a_ref[0], w_ref[...], preferred_element_type=f32)
    cosine, sine = cos_ref[0, 0], sin_ref[0, 0]
    for part in range(got.shape[1] // HSZ):
        piece = got[:, part * HSZ : (part + 1) * HSZ]
        turned = piece * cosine + pltpu.roll(piece, HSZ // 2, 1) * sine
        o_ref[0, 0, :, part * HSZ : (part + 1) * HSZ] = turned.astype(bf16)


def project_kv(a_all, kv_cols, cosine, sine):
    micro, rows, width = a_all.shape
    group = kv_cols.shape[1] // 2
    step = min(256, group)
    per = group // step
    table = pl.BlockSpec((1, 1, rows, HSZ), lambda m, g: (m, g // per, 0, 0))
    return pl.pallas_call(
        kv_kernel,
        grid=(micro, 2 * per),
        in_specs=[
            pl.BlockSpec((1, rows, width), lambda m, g: (m, 0, 0)),
            pl.BlockSpec((width, step), lambda m, g: (0, g)),
            table,
            table,
        ],
        out_specs=pl.BlockSpec((1, 1, rows, step), lambda m, g: (m, g // per, 0, g % per)),
        out_shape=jax.ShapeDtypeStruct((micro, 2, rows, group), bf16),
        name="project_kv",
        cost_estimate=work(4 * micro * rows * width * group, 2 * (micro * rows * width + 2 * width * group + 2 * micro * rows * group)),
    )(a_all, kv_cols, cosine, sine)


def probabilities(query, keys, start, qpos, micro):
    parts = []
    for m in range(micro + 1):
        got = lax.dot_general(
            query, keys[m], (((1,), (1,)), ((), ())), preferred_element_type=f32
        ) * (HSZ**-0.5)
        if m == micro:
            kpos = micro * got.shape[1] + lax.broadcasted_iota(jnp.int32, got.shape, 1)
            inside_q = (qpos >= start) & (qpos < start + PIC)
            inside_k = (kpos >= start) & (kpos < start + PIC)
            keep = (kpos <= qpos) | (inside_q & inside_k)
            got = jnp.where(keep, got, masked_low)
        parts.append(got)
    peak = parts[0].max(axis=1, keepdims=True)
    for got in parts[1:]:
        peak = jnp.maximum(peak, got.max(axis=1, keepdims=True))
    lifted = [jnp.exp(got - peak) for got in parts]
    total = lifted[0].sum(axis=1, keepdims=True)
    for got in lifted[1:]:
        total = total + got.sum(axis=1, keepdims=True)
    scale = 1.0 / total
    return [got * scale for got in lifted], peak


def project_q(a_pairs, q_full, cosine, sine, micro, experts):
    total, width = a_pairs.shape
    inner = q_full.shape[1]
    group = inner // experts
    step = min(256, group)
    per = group // step
    rows = total // micro

    def kernel(a_ref, w_ref, cos_ref, sin_ref, o_ref):
        got = jnp.dot(a_ref[...], w_ref[...], preferred_element_type=f32)
        for h in range(step // HSZ):
            lanes = slice(h * HSZ, (h + 1) * HSZ)
            piece = got[:, lanes]
            turned = piece * cos_ref[...] + pltpu.roll(piece, HSZ // 2, 1) * sin_ref[...]
            o_ref[:, 0, :, lanes] = turned.astype(bf16).reshape(micro, rows, HSZ)

    return pl.pallas_call(
        kernel,
        grid=(inner // step,),
        in_specs=[
            full_spec((total, width)),
            pl.BlockSpec((width, step), lambda g: (0, g)),
            full_spec((total, HSZ)),
            full_spec((total, HSZ)),
        ],
        out_specs=pl.BlockSpec((micro, 1, rows, step), lambda g: (0, g // per, 0, g % per)),
        out_shape=jax.ShapeDtypeStruct((micro, experts, rows, group), bf16),
        name="project_q",
        cost_estimate=work(2 * total * width * inner, 2 * (total * width + width * inner + total * inner)),
    )(a_pairs, q_full, cosine, sine)


def attend(query, qpos, kvs, start):
    micro = len(kvs) - 1
    experts, rows, group = query.shape
    hg = group // HSZ
    keys_seen = sum(kv.shape[1] for kv in kvs)

    def kernel(start_ref, q_ref, pos_ref, *rest):
        kv_refs, (mixed_ref, peak_ref) = rest[:-2], rest[-2:]
        for h in range(hg):
            lanes = slice(h * HSZ, (h + 1) * HSZ)
            probs, peak = probabilities(
                q_ref[0, :, lanes],
                [r[0, :, lanes] for r in kv_refs],
                start_ref[0],
                pos_ref[0],
                micro,
            )
            mixed = jnp.zeros((rows, HSZ), f32)
            for m in range(micro + 1):
                mixed = mixed + jnp.dot(
                    probs[m].astype(bf16), kv_refs[m][1, :, lanes], preferred_element_type=f32
                )
            mixed_ref[0, :, lanes] = mixed.astype(bf16)
            peak_ref[0, h] = jnp.full(peak_ref.shape[2:], jnp.max(peak), f32)

    return pl.pallas_call(
        kernel,
        grid_spec=pltpu.PrefetchScalarGridSpec(
            num_scalar_prefetch=1,
            grid=(experts,),
            in_specs=[
                pl.BlockSpec((1, rows, group), lambda g, s: (g, 0, 0)),
                pl.BlockSpec((1, rows, 1), lambda g, s: (g, 0, 0)),
            ]
            + [full_spec(kv.shape) for kv in kvs],
            out_specs=[
                pl.BlockSpec((1, rows, group), lambda g, s: (g, 0, 0)),
                pl.BlockSpec((1, hg, 8, 128), lambda g, s: (g, 0, 0, 0)),
            ],
        ),
        out_shape=[
            jax.ShapeDtypeStruct((experts, rows, group), bf16),
            jax.ShapeDtypeStruct((experts, hg, 8, 128), f32),
        ],
        name="attend",
        cost_estimate=work(4 * experts * rows * group * keys_seen, 4 * experts * rows * group, experts * rows * hg * keys_seen),
    )(start, query, qpos, *kvs)


def attend_back(query, d_mixed, cosine, sine, qpos, kvs, key_cos, key_sin, later, start):
    micro = len(kvs) - 1
    experts, rows, group = query.shape
    keys = kvs[0].shape[1]
    hg = group // HSZ
    held = len(later)

    def kernel(start_ref, q_ref, dm_ref, cos_ref, sin_ref, pos_ref, kcos_ref, ksin_ref, *rest):
        kv_refs = rest[: micro + 1]
        later_refs = rest[micro + 1 : micro + 1 + held]
        dq_ref, dkv_ref = rest[micro + 1 + held : micro + 3 + held]
        sums = rest[micro + 3 + held :]
        step = pl.program_id(0)

        @pl.when(step == 0)
        def _():
            for m in range(micro + 1):
                if held and m == micro:
                    sums[m][...] = later_refs[0][...]
                else:
                    sums[m][...] = jnp.zeros(sums[m].shape, f32)

        for h in range(hg):
            lanes = slice(h * HSZ, (h + 1) * HSZ)
            q, dm = q_ref[0, :, lanes], dm_ref[0, :, lanes]
            probs, _ = probabilities(
                q, [r[0, :, lanes] for r in kv_refs], start_ref[0], pos_ref[0], micro
            )
            d_probs = [
                lax.dot_general(
                    dm, r[1, :, lanes], (((1,), (1,)), ((), ())), preferred_element_type=f32
                )
                for r in kv_refs
            ]
            total = jnp.sum(d_probs[0] * probs[0], axis=1, keepdims=True)
            for m in range(1, micro + 1):
                total = total + jnp.sum(d_probs[m] * probs[m], axis=1, keepdims=True)
            d_q = jnp.zeros((rows, HSZ), f32)
            for m in range(micro + 1):
                d_scores = (probs[m] * (d_probs[m] - total)).astype(bf16)
                d_q = d_q + jnp.dot(d_scores, kv_refs[m][0, :, lanes], preferred_element_type=f32)
                sums[m][0, :, lanes] += lax.dot_general(
                    d_scores, q, (((0,), (0,)), ((), ())), preferred_element_type=f32
                )
                sums[m][1, :, lanes] += lax.dot_general(
                    probs[m].astype(bf16), dm, (((0,), (0,)), ((), ())), preferred_element_type=f32
                )
            d_q = d_q * (HSZ**-0.5)
            back = d_q * cos_ref[0] - pltpu.roll(d_q, HSZ // 2, 1) * sin_ref[0]
            dq_ref[0, :, lanes] = back.astype(bf16)

        @pl.when(step == experts - 1)
        def _():
            for h in range(hg):
                lanes = slice(h * HSZ, (h + 1) * HSZ)
                d_k = sums[micro][0, :, lanes] * (HSZ**-0.5)
                back = d_k * kcos_ref[...] - pltpu.roll(d_k, HSZ // 2, 1) * ksin_ref[...]
                dkv_ref[:, lanes] = back.astype(bf16)
                dkv_ref[:, group + h * HSZ : group + (h + 1) * HSZ] = sums[micro][
                    1, :, lanes
                ].astype(bf16)

    block = pl.BlockSpec((1, rows, group), lambda g, s: (g, 0, 0))
    table = pl.BlockSpec((1, rows, HSZ), lambda g, s: (g, 0, 0))
    sums_shape = jax.ShapeDtypeStruct((2, keys, group), f32)
    return pl.pallas_call(
        kernel,
        grid_spec=pltpu.PrefetchScalarGridSpec(
            num_scalar_prefetch=1,
            grid=(experts,),
            in_specs=[block, block, table, table]
            + [pl.BlockSpec((1, rows, 1), lambda g, s: (g, 0, 0))]
            + [full_spec((keys, HSZ))] * 2
            + [full_spec((2, keys, group))] * (micro + 1 + held),
            out_specs=[block, full_spec((keys, 2 * group))]
            + [full_spec((2, keys, group))] * micro,
            scratch_shapes=[pltpu.VMEM((2, keys, group), f32)],
        ),
        out_shape=[
            jax.ShapeDtypeStruct((experts, rows, group), bf16),
            jax.ShapeDtypeStruct((keys, 2 * group), bf16),
        ]
        + [sums_shape] * micro,
        name="attend_back",
        cost_estimate=work(10 * experts * rows * group * keys * (micro + 1), 12 * experts * rows * group, experts * rows * hg * keys * (micro + 1)),
    )(start, query, d_mixed, cosine, sine, qpos, key_cos, key_sin, *kvs, *later)


def join_groups(got_ref, flat_ref):
    experts, _, group = got_ref.shape
    for e in range(experts):
        flat_ref[:, e * group : (e + 1) * group] = got_ref[e]


def project_o(mixed, o_full, gate):
    experts, rows, group = mixed.shape
    inner, width = o_full.shape
    step = min(512, width)

    def kernel(mixed_ref, o_ref, gate_ref, attn_ref, gated_ref, flat_ref):
        @pl.when(pl.program_id(0) == 0)
        def _():
            join_groups(mixed_ref, flat_ref)

        got = jnp.dot(flat_ref[...], o_ref[...], preferred_element_type=f32)
        attn_ref[...] = got.astype(bf16)
        gated_ref[...] = (got * gate_ref[...]).astype(bf16)

    column = pl.BlockSpec((rows, step), lambda g: (0, g))
    return pl.pallas_call(
        kernel,
        grid=(width // step,),
        in_specs=[
            full_spec(mixed.shape),
            pl.BlockSpec((inner, step), lambda g: (0, g)),
            full_spec((rows, 1)),
        ],
        out_specs=[column, column, full_spec((rows, inner))],
        out_shape=[
            jax.ShapeDtypeStruct((rows, width), bf16),
            jax.ShapeDtypeStruct((rows, width), bf16),
            jax.ShapeDtypeStruct((rows, inner), bf16),
        ],
        name="project_o",
        cost_estimate=work(2 * rows * inner * width, 2 * (inner * width + 4 * rows * width)),
    )(mixed, o_full, gate)


def back_o(got, attn, gate, rest, turn, o_full, experts):
    rows, width = got.shape
    inner = o_full.shape[0]
    group = inner // experts
    lanes = turn.shape[1]

    def kernel(got_ref, attn_ref, gate_ref, rest_ref, turn_ref, o_ref, da_ref, dm_ref, dl_ref):
        @pl.when(pl.program_id(0) == 0)
        def _():
            upstream = got_ref[...].astype(f32)
            da_ref[...] = (gate_ref[...] * upstream).astype(bf16)
            value = jnp.sum(upstream * attn_ref[...].astype(f32), axis=1, keepdims=True)
            d_logits = (gate_ref[...] * rest_ref[...] * value) * turn_ref[...]
            high = d_logits.astype(bf16)
            dl_ref[:, :lanes] = high
            dl_ref[:, lanes:] = (d_logits - high.astype(f32)).astype(bf16)

        dm_ref[0] = lax.dot_general(
            da_ref[...], o_ref[...], (((1,), (1,)), ((), ())), preferred_element_type=f32
        ).astype(bf16)

    return pl.pallas_call(
        kernel,
        grid=(experts,),
        in_specs=[full_spec((rows, width))] * 2
        + [full_spec((rows, 1))] * 2
        + [full_spec((rows, lanes)), pl.BlockSpec((group, width), lambda g: (g, 0))],
        out_specs=[
            full_spec((rows, width)),
            pl.BlockSpec((1, rows, group), lambda g: (g, 0, 0)),
            full_spec((rows, 2 * lanes)),
        ],
        out_shape=[
            jax.ShapeDtypeStruct((rows, width), bf16),
            jax.ShapeDtypeStruct((experts, rows, group), bf16),
            jax.ShapeDtypeStruct((rows, 2 * lanes), bf16),
        ],
        name="back_o",
        cost_estimate=work(2 * rows * inner * width, 2 * (inner * width + 4 * rows * width)),
    )(got, attn, gate, rest, turn, o_full)


def back_q(d_query, q_full, d_logits, router):
    experts, rows, group = d_query.shape
    width, inner = q_full.shape
    step = min(512, width)
    lanes = router.shape[1]

    def kernel(dq_ref, q_ref, dl_ref, router_ref, pair_ref, flat_ref):
        @pl.when(pl.program_id(0) == 0)
        def _():
            join_groups(dq_ref, flat_ref)

        dims = (((1,), (1,)), ((), ()))
        got = lax.dot_general(flat_ref[...], q_ref[...], dims, preferred_element_type=f32)
        for half in range(2):
            got = got + lax.dot_general(
                dl_ref[:, half * lanes : (half + 1) * lanes],
                router_ref[...],
                dims,
                preferred_element_type=f32,
            )
        pair_ref[...] = got.astype(bf16)

    return pl.pallas_call(
        kernel,
        grid=(width // step,),
        in_specs=[
            full_spec(d_query.shape),
            pl.BlockSpec((step, inner), lambda g: (g, 0)),
            full_spec((rows, 2 * lanes)),
            pl.BlockSpec((step, lanes), lambda g: (g, 0)),
        ],
        out_specs=[pl.BlockSpec((rows, step), lambda g: (0, g)), full_spec((rows, inner))],
        out_shape=[
            jax.ShapeDtypeStruct((rows, width), bf16),
            jax.ShapeDtypeStruct((rows, inner), bf16),
        ],
        name="back_q",
        cost_estimate=work(2 * rows * inner * width, 2 * (inner * width + 4 * rows * width)),
    )(d_query, q_full, d_logits, router)


def token_back(d_kv, kv_cols, d_pair, pick, rows, inverse):
    span, line = d_kv.shape
    width = kv_cols.shape[0]
    experts, slots, tokens = pick.shape
    step = min(512, width)

    def kernel(dkv_ref, kv_ref, pair_ref, pick_ref, x_ref, inv_ref, o_ref, dg_ref):
        got = lax.dot_general(
            dkv_ref[...], kv_ref[...], (((1,), (1,)), ((), ())), preferred_element_type=f32
        )
        gain = jnp.zeros((1, step), f32)
        for e in range(experts):
            part = slice(e * tokens, (e + 1) * tokens)
            extra = lax.dot_general(
                pick_ref[e],
                pair_ref[e * slots : (e + 1) * slots, :],
                (((0,), (0,)), ((), ())),
                preferred_element_type=f32,
            )
            d_a = got[part] + extra
            o_ref[e] = d_a.astype(bf16)
            scaled = x_ref[part, :].astype(f32) * inv_ref[part, :]
            gain = gain + jnp.sum(d_a * scaled, axis=0, keepdims=True)
        dg_ref[...] = gain

    return pl.pallas_call(
        kernel,
        grid=(width // step,),
        in_specs=[
            full_spec((span, line)),
            pl.BlockSpec((step, line), lambda g: (g, 0)),
            pl.BlockSpec((experts * slots, step), lambda g: (0, g)),
            full_spec(pick.shape),
            pl.BlockSpec((span, step), lambda g: (0, g)),
            full_spec((span, 1)),
        ],
        out_specs=[
            pl.BlockSpec((experts, tokens, step), lambda g: (0, 0, g)),
            pl.BlockSpec((1, step), lambda g: (0, g)),
        ],
        out_shape=[
            jax.ShapeDtypeStruct((experts, tokens, width), bf16),
            jax.ShapeDtypeStruct((1, width), f32),
        ],
        name="token_back",
        cost_estimate=work(2 * span * line * width, 2 * (line * width + 2 * span * width)),
    )(d_kv, kv_cols, d_pair, pick, rows, inverse)


def input_back_kernel(got_ref, x_ref, gain_ref, dm_ref, gx_ref):
    d_a = got_ref[0].astype(f32)
    for e in range(1, got_ref.shape[0]):
        d_a = d_a + got_ref[e].astype(f32)
    x = x_ref[...].astype(f32)
    inverse = lax.rsqrt(jnp.mean(x * x, axis=1, keepdims=True) + norm_eps)
    scaled = d_a * gain_ref[...]
    mean = jnp.mean(scaled * x, axis=1, keepdims=True)
    gx_ref[...] = dm_ref[...] + (inverse * scaled - x * (inverse * inverse * inverse * mean))


def input_back(got, x, gain, d_middle):
    tokens, width = x.shape
    return pl.pallas_call(
        input_back_kernel,
        out_shape=jax.ShapeDtypeStruct((tokens, width), f32),
        name="input_back",
        cost_estimate=work(10 * tokens * width, 20 * tokens * width),
    )(got, x, gain, d_middle)


def combine_kernel(back_ref, pick_ref, x_ref, gain_ref, middle_ref, inv_ref, b_ref):
    summed = lax.dot_general(
        pick_ref[...], back_ref[...], (((0,), (0,)), ((), ())), preferred_element_type=f32
    )
    middle = x_ref[...].astype(f32) + summed
    inverse = lax.rsqrt(jnp.mean(middle * middle, axis=1, keepdims=True) + norm_eps)
    middle_ref[...] = middle
    inv_ref[...] = inverse
    b_ref[...] = (middle * inverse * gain_ref[...]).astype(bf16)


def combine(back, pick, x, gain):
    tokens, width = x.shape
    return pl.pallas_call(
        combine_kernel,
        out_shape=[
            jax.ShapeDtypeStruct((tokens, width), f32),
            jax.ShapeDtypeStruct((tokens, 1), f32),
            jax.ShapeDtypeStruct((tokens, width), bf16),
        ],
        name="combine",
        cost_estimate=work(2 * back.shape[0] * tokens * width, 2 * back.shape[0] * width + 8 * tokens * width),
    )(back, pick, x, gain)


def middle_back_kernel(*refs):
    pieces = refs[:-8]
    middle_ref, inv_ref, cot_ref, gain_ref, pick_ref, dm_ref, dg_ref, rows_ref = refs[-8:]
    d_b = pieces[0][...].astype(f32)
    for piece in pieces[1:]:
        d_b = d_b + piece[...].astype(f32)
    middle, inverse = middle_ref[...], inv_ref[...]
    scaled = d_b * gain_ref[...]
    dg_ref[...] = jnp.sum(d_b * (middle * inverse), axis=0, keepdims=True)
    mean = jnp.mean(scaled * middle, axis=1, keepdims=True)
    d_middle = cot_ref[...].astype(f32) + (
        inverse * scaled - middle * (inverse * inverse * inverse * mean)
    )
    dm_ref[...] = d_middle
    rows_ref[...] = jnp.dot(
        pick_ref[...], d_middle.astype(bf16), preferred_element_type=f32
    ).astype(bf16)


def middle_back(pieces, middle, inverse, cot, gain, pick):
    tokens, width = middle.shape
    return pl.pallas_call(
        middle_back_kernel,
        out_shape=[
            jax.ShapeDtypeStruct((tokens, width), f32),
            jax.ShapeDtypeStruct((1, width), f32),
            jax.ShapeDtypeStruct((pick.shape[0], width), bf16),
        ],
        name="middle_back",
        cost_estimate=work(2 * pick.shape[0] * tokens * width, 2 * pick.shape[0] * width + 20 * tokens * width),
    )(*pieces, middle, inverse, cot, gain, pick)


def dispatch(blocks, pick):
    stages, pairs, tokens = pick.shape
    width = blocks[0].shape[1]
    step = min(512, width)

    def kernel(pick_ref, *refs):
        for k in range(stages):
            refs[-1][:, k] = (
                jnp.dot(pick_ref[k], refs[k][...], preferred_element_type=f32)
                .astype(bf16)
                .reshape(refs[-1].shape[0], refs[-1].shape[2], step)
            )

    return lambda experts: pl.pallas_call(
        kernel,
        grid=(width // step,),
        in_specs=[full_spec(pick.shape)]
        + [pl.BlockSpec((tokens, step), lambda g: (0, g)) for _ in blocks],
        out_specs=pl.BlockSpec((experts, stages, pairs // experts, step), lambda g: (0, 0, 0, g)),
        out_shape=jax.ShapeDtypeStruct((experts, stages, pairs // experts, width), bf16),
        name="dispatch",
        cost_estimate=work(2 * stages * pairs * tokens * width, 2 * stages * (pairs + tokens) * width),
    )(pick, *blocks)


def collect(rows, pick, order):
    experts, stages, slots, width = rows.shape
    tokens = pick.shape[2]

    def kernel(order_ref, pick_ref, rows_ref, o_ref):
        gathered = rows_ref[...].reshape(experts * slots, width)
        o_ref[0] = lax.dot_general(
            pick_ref[0], gathered, (((0,), (0,)), ((), ())), preferred_element_type=f32
        ).astype(bf16)

    return pl.pallas_call(
        kernel,
        grid_spec=pltpu.PrefetchScalarGridSpec(
            num_scalar_prefetch=1,
            grid=(stages,),
            in_specs=[
                pl.BlockSpec((1, experts * slots, tokens), lambda k, o: (k, 0, 0)),
                pl.BlockSpec((experts, 1, slots, width), lambda k, o: (0, k, 0, 0)),
            ],
            out_specs=pl.BlockSpec((1, tokens, width), lambda k, o: (o[k], 0, 0)),
        ),
        out_shape=jax.ShapeDtypeStruct((stages, tokens, width), bf16),
        name="collect",
        cost_estimate=work(2 * stages * experts * slots * tokens * width, 2 * stages * (experts * slots + tokens) * width),
    )(order, pick, rows)


def collect_each(rows, pick):
    experts, stages, slots, width = rows.shape
    tokens = pick.shape[2]

    def kernel(pick_ref, rows_ref, *outs):
        gathered = rows_ref[...].reshape(experts * slots, width)
        summed = lax.dot_general(
            pick_ref[0], gathered, (((0,), (0,)), ((), ())), preferred_element_type=f32
        ).astype(bf16)
        for k in range(stages):

            @pl.when(pl.program_id(0) == k)
            def _(ref=outs[k]):
                ref[...] = summed

    return pl.pallas_call(
        kernel,
        grid=(stages,),
        in_specs=[
            pl.BlockSpec((1, experts * slots, tokens), lambda k: (k, 0, 0)),
            pl.BlockSpec((experts, 1, slots, width), lambda k: (0, k, 0, 0)),
        ],
        out_specs=[full_spec((tokens, width))] * stages,
        out_shape=[jax.ShapeDtypeStruct((tokens, width), bf16)] * stages,
        name="collect_each",
        cost_estimate=work(2 * stages * experts * slots * tokens * width, 2 * stages * (experts * slots + tokens) * width),
    )(pick, rows)


def feed_grads(rows, d_gates, d_ups, d_logits):
    count, width = rows[0].shape
    part, lanes = d_gates[0].shape[1], d_logits[0].shape[1]
    held = len(rows)
    step = min(256, width)

    def kernel(*refs):
        ins, outs = refs[: 4 * held], refs[4 * held :]
        for kind, out in enumerate(outs):
            total = None
            for m in range(held):
                got = lax.dot_general(
                    ins[m][...],
                    ins[held * (kind + 1) + m][...],
                    (((0,), (0,)), ((), ())),
                    preferred_element_type=f32,
                )
                total = got if total is None else total + got
            out[...] = total.astype(out.dtype)

    def resident(array):
        return pl.BlockSpec(array.shape, lambda g: (0, 0), pipeline_mode=pl.Buffered(1))

    others = (*d_gates, *d_ups, *d_logits)
    return pl.pallas_call(
        kernel,
        grid=(width // step,),
        in_specs=[pl.BlockSpec((count, step), lambda g: (0, g)) for _ in rows]
        + [resident(x) for x in others],
        out_specs=[pl.BlockSpec((step, n), lambda g: (g, 0)) for n in (part, part, lanes)],
        out_shape=[
            jax.ShapeDtypeStruct((width, part), bf16),
            jax.ShapeDtypeStruct((width, part), bf16),
            jax.ShapeDtypeStruct((width, lanes), f32),
        ],
        name="feed_grads",
        cost_estimate=work(4 * held * count * width * part, 2 * (held * count * (width + 2 * part) + 2 * width * part)),
    )(*rows, *others)


def cut(place, gate, up):
    rows, hidden = gate.shape
    stages = place.shape[0] - 2
    part = hidden // stages

    def kernel(place_ref, gate_ref, up_ref, *outs):
        for k in range(stages):

            @pl.when(pl.program_id(0) == k)
            def _(ref=outs[k]):
                ref[0] = gate_ref[...]
                ref[1] = up_ref[...]

    block = pl.BlockSpec((rows, part), lambda g, p: (0, p[2 + g]))
    return pl.pallas_call(
        kernel,
        grid_spec=pltpu.PrefetchScalarGridSpec(
            num_scalar_prefetch=1,
            grid=(stages,),
            in_specs=[block, block],
            out_specs=[full_spec((2, rows, part))] * stages,
        ),
        out_shape=[jax.ShapeDtypeStruct((2, rows, part), bf16)] * stages,
        name="cut",
        cost_estimate=work(0, 8 * stages * rows * part),
    )(place, gate, up)


def other_half(place, gate, up, stages):
    width, part = gate.shape
    rows = width // (2 * stages)

    def kernel(place_ref, gate_ref, up_ref, o_ref):
        o_ref[0, 0] = gate_ref[...]
        o_ref[0, 1] = up_ref[...]

    block = pl.BlockSpec((rows, part), lambda g, p: (2 * g + 1 - p[1], 0))
    return pl.pallas_call(
        kernel,
        grid_spec=pltpu.PrefetchScalarGridSpec(
            num_scalar_prefetch=1,
            grid=(stages,),
            in_specs=[block, block],
            out_specs=pl.BlockSpec((1, 2, rows, part), lambda g, p: (g, 0, 0, 0)),
        ),
        out_shape=jax.ShapeDtypeStruct((stages, 2, rows, part), bf16),
        name="other_half",
        cost_estimate=work(0, 8 * stages * rows * part),
    )(place, gate, up)


def own_half(place, gate, up, other):
    stages, _, rows, part = other.shape

    def kernel(place_ref, gate_ref, up_ref, other_ref, *outs):
        for k in range(stages):

            @pl.when(pl.program_id(0) == k)
            def _(ref=outs[k]):
                ref[0] = (gate_ref[...].astype(f32) + other_ref[0, 0].astype(f32)).astype(bf16)
                ref[1] = (up_ref[...].astype(f32) + other_ref[0, 1].astype(f32)).astype(bf16)

    block = pl.BlockSpec((rows, part), lambda g, p: (2 * p[2 + g] + p[1], 0))
    return pl.pallas_call(
        kernel,
        grid_spec=pltpu.PrefetchScalarGridSpec(
            num_scalar_prefetch=1,
            grid=(stages,),
            in_specs=[
                block,
                block,
                pl.BlockSpec((1, 2, rows, part), lambda g, p: (p[2 + g], 0, 0, 0)),
            ],
            out_specs=[full_spec((2, rows, part))] * stages,
        ),
        out_shape=[jax.ShapeDtypeStruct((2, rows, part), bf16)] * stages,
        name="own_half",
        cost_estimate=work(0, 12 * stages * rows * part),
    )(place, gate, up, other)


def assemble(place, mine, theirs):
    stages = len(mine)
    _, rows, part = mine[0].shape

    def kernel(place_ref, *refs):
        ins, (gate_ref, up_ref) = refs[:-2], refs[-2:]
        step = pl.program_id(0)
        hop = (place_ref[0] - step // 2) % stages
        here = step % 2 == place_ref[1]
        for k in range(stages):
            for which in range(2):

                @pl.when((hop == k) & (here == (which == 0)))
                def _(ref=ins[which * stages + k]):
                    gate_ref[...] = ref[0]
                    up_ref[...] = ref[1]

    block = pl.BlockSpec((rows, part), lambda g, p: (g, 0))
    shape = jax.ShapeDtypeStruct((2 * stages * rows, part), bf16)
    return pl.pallas_call(
        kernel,
        grid_spec=pltpu.PrefetchScalarGridSpec(
            num_scalar_prefetch=1,
            grid=(2 * stages,),
            in_specs=[
                pl.BlockSpec((2, rows, part), lambda g, p: (0, 0, 0), pipeline_mode=pl.Buffered(1))
            ]
            * (2 * stages),
            out_specs=[block, block],
        ),
        out_shape=[shape, shape],
        name="assemble",
        cost_estimate=work(0, 12 * stages * rows * part),
    )(place, *mine, *theirs)


def widen(place, got):
    stages = len(got)
    _, rows, part = got[0].shape

    def kernel(place_ref, *refs):
        hop = (place_ref[0] - pl.program_id(0)) % stages
        for k in range(stages):

            @pl.when(hop == k)
            def _(ref=refs[k]):
                for half in range(2):
                    refs[half - 2][0] = ref[half].astype(f32)

    block = pl.BlockSpec((1, rows, part), lambda g, p: (0, 0, g))
    shape = jax.ShapeDtypeStruct((1, rows, stages * part), f32)
    return pl.pallas_call(
        kernel,
        grid_spec=pltpu.PrefetchScalarGridSpec(
            num_scalar_prefetch=1,
            grid=(stages,),
            in_specs=[full_spec((2, rows, part))] * stages,
            out_specs=[block, block],
        ),
        out_shape=[shape, shape],
        name="widen",
        cost_estimate=work(0, 12 * stages * rows * part),
    )(place, *got)


def feed_kernel(own_ref, r_ref, g_ref, other_ref, router_ref, wg_ref, wu_ref, wd_ref, *outs):
    out_ref, db_ref, low_ref, dg_ref, du_ref, dr_ref, dl_ref = outs
    rows, grads = r_ref[...], g_ref[...].astype(f32)
    router = router_ref[...]
    logits = jnp.dot(rows, router, preferred_element_type=f32)
    column = lax.broadcasted_iota(jnp.int32, logits.shape, 1)
    turn = (column == own_ref[0]).astype(f32) - (column == other_ref[...]).astype(f32)
    lead = jnp.sum(logits * turn, axis=1, keepdims=True)
    gate, rest = jax.nn.sigmoid(lead), jax.nn.sigmoid(-lead)
    d_rows = (gate * grads).astype(bf16)
    dr_ref[...] = d_rows
    gate_pre = jnp.dot(rows, wg_ref[...], preferred_element_type=f32)
    up_pre = jnp.dot(rows, wu_ref[...], preferred_element_type=f32)
    d_low = lax.dot_general(
        d_rows, wd_ref[...], (((1,), (1,)), ((), ())), preferred_element_type=f32
    )
    sigma = jax.nn.sigmoid(gate_pre)
    silu = gate_pre * sigma
    low = (silu * up_pre).astype(bf16)
    low_ref[...] = low
    d_up = (d_low * silu).astype(bf16)
    du_ref[...] = d_up
    d_gate = (d_low * up_pre * (sigma + silu * (1.0 - sigma))).astype(bf16)
    dg_ref[...] = d_gate
    result = jnp.dot(low, wd_ref[...], preferred_element_type=f32)
    out_ref[...] = (gate * result).astype(bf16)
    d_value = jnp.sum(grads * result, axis=1, keepdims=True)
    d_logits = (gate * rest * d_value) * turn
    high = d_logits.astype(bf16)
    small = (d_logits - high.astype(f32)).astype(bf16)
    half = high.shape[1]
    dl_ref[:, :half] = high
    dl_ref[:, half:] = small
    d_b = lax.dot_general(
        d_gate, wg_ref[...], (((1,), (1,)), ((), ())), preferred_element_type=f32
    ) + lax.dot_general(d_up, wu_ref[...], (((1,), (1,)), ((), ())), preferred_element_type=f32)
    for piece in (high, small):
        d_b = d_b + lax.dot_general(
            piece, router, (((1,), (1,)), ((), ())), preferred_element_type=f32
        )
    db_ref[...] = d_b.astype(bf16)


def feed(own, rows, grads, other, router, wg, wu, wd):
    count, width = rows.shape
    part = wg.shape[1]
    step = min(256, count)
    lanes = router.shape[1]

    def by_rows(columns):
        return pl.BlockSpec((step, columns), lambda g, s: (g, 0))

    def held(shape):
        return pl.BlockSpec(shape, lambda g, s: (0, 0), pipeline_mode=pl.Buffered(1))

    def shape(columns):
        return jax.ShapeDtypeStruct((count, columns), bf16)

    widths = (width, width, part, part, part, width, 2 * lanes)
    return pl.pallas_call(
        feed_kernel,
        grid_spec=pltpu.PrefetchScalarGridSpec(
            num_scalar_prefetch=1,
            grid=(count // step,),
            in_specs=[by_rows(width), by_rows(width), by_rows(1)]
            + [held(w.shape) for w in (router, wg, wu, wd)],
            out_specs=[by_rows(w) for w in widths],
        ),
        out_shape=[shape(w) for w in widths],
        name="feed",
        cost_estimate=work(12 * count * width * part, 6 * width * part + 2 * count * (5 * width + 3 * part), count * part),
    )(own, rows, grads, other, router, wg, wu, wd)


def after(array, *others):
    return lax.optimization_barrier((array, *others))[0]


def per_device(
    inputs,
    attn_routes,
    mlp_routes,
    pic_start,
    kv_weight,
    router_weight,
    norm_gains,
    q_weight,
    o_weight,
    gate_weight,
    up_weight,
    down_weight,
    cotangent,
):
    experts = lax.axis_size("expert")
    dp_size = lax.axis_size("dp")
    stages = dp_size // 2
    own = lax.axis_index("expert")
    dp_index = lax.axis_index("dp")
    stage, core = dp_index // 2, dp_index % 2
    tokens, width = inputs.shape[2], inputs.shape[3]
    inner = HEADS * HSZ
    group = inner // experts
    slots = tokens * TOPK // experts
    span = tokens * experts
    rows_each = kv_weight.shape[0]
    hidden = gate_weight.shape[2]
    part = hidden // stages
    routed = experts * slots
    same_core = [[z * 2 + c for z in range(stages)] for c in range(2)]

    def exchange(blocks):
        return lax.all_to_all(blocks, "expert", 0, 0, tiled=True)

    def spread(block):
        return exchange(jnp.broadcast_to(block[None], (experts,) + block.shape))

    def along(block, k):
        if k % stages == 0:
            return block
        return lax.ppermute(
            block, "dp", [(j, ((j // 2 + k) % stages) * 2 + j % 2) for j in range(dp_size)]
        )

    def partner(block):
        return lax.ppermute(block, "dp", [(j, j ^ 1) for j in range(dp_size)])

    def pick(array, index, axis=0):
        return lax.dynamic_index_in_dim(array, index, axis, keepdims=False)

    small = jnp.concatenate(
        [
            attn_routes.reshape(-1).astype(bf16),
            mlp_routes.reshape(-1).astype(bf16),
            router_weight.reshape(-1),
            norm_gains.reshape(-1),
        ]
    )
    length = small.shape[0]
    line = 2 * group
    extra = -(-length // (8 * line)) * 8
    small = jnp.pad(small, (0, extra * line - length)).reshape(1, extra, line)
    kv_split = kv_weight.reshape(rows_each, 2, experts, group).transpose(2, 0, 1, 3)
    first = jnp.concatenate(
        [
            jnp.broadcast_to(inputs, (experts, MICRO, tokens, width)).reshape(experts, -1, width),
            kv_split.reshape(experts, rows_each * line // width, width),
            jnp.broadcast_to(small.reshape(1, -1, width), (experts, extra * line // width, width)),
        ],
        axis=1,
    )
    first = exchange(first)
    x_blocks = first[:, : MICRO * tokens].reshape(experts, MICRO, tokens, width)
    kv_rows = first[:, MICRO * tokens :].reshape(experts, rows_each + extra, line)
    stage_order = (stage - jnp.arange(stages, dtype=jnp.int32)) % stages
    place = jnp.arange(experts, dtype=jnp.int32)
    cot_stages = lax.all_gather(cotangent[0], "dp", axis=0, axis_index_groups=same_core)
    route_rows = mlp_routes[0].reshape(-1).astype(bf16)
    route_rows = jnp.pad(route_rows, (0, -route_rows.shape[0] % 128)).reshape(-1, 128)
    own_routes = jnp.stack([along(route_rows, k) for k in range(stages)]).reshape(stages, -1)
    own_routes = own_routes[:, : MICRO * tokens * TOPK].astype(jnp.int32)
    own_routes = own_routes.reshape(stages, MICRO, tokens, TOPK)
    home_m = selection(
        (own_routes[:, None] == place[None, :, None, None, None]).any(-1).astype(f32), slots
    )
    home_m = home_m.transpose(2, 0, 1, 3, 4).reshape(MICRO, stages, experts * slots, tokens)
    q_full = lax.all_gather(after(q_weight[0], cot_stages, first), "dp", axis=0, tiled=True)
    cot_rows = {}
    for m in ORDER:
        blocks = [pick(cot_stages, stage_order[k])[m] for k in range(stages)]
        cot_rows[m] = exchange(dispatch(blocks, home_m[m])(experts))
    kv_rows = after(kv_rows, q_full, cot_rows[ORDER[0]])
    kv_got = lax.all_gather(kv_rows, "dp", axis=0)

    forward_order = (stage + jnp.arange(stages, dtype=jnp.int32)) % stages
    where = jnp.concatenate([jnp.stack([stage, core]), forward_order]).astype(jnp.int32)
    if part % 128 == 0:
        mine = list(cut(where, gate_weight[0], up_weight[0]))
    else:
        both = jnp.stack([gate_weight[0], up_weight[0]]).reshape(2, -1, stages, part)
        mine = [pick(both, forward_order[k], 2) for k in range(stages)]
    for k in range(1, stages):
        mine[k] = along(after(mine[k], kv_rows), k)
    kv_cols = kv_got[:, :, :rows_each].reshape(width, line)
    small = kv_got[:, :, rows_each:].reshape(dp_size, experts, extra * line)
    count = MICRO * tokens * TOPK
    routes_a = pick(small[:, :, :count], dp_index).astype(jnp.int32)
    routes_a = routes_a.reshape(experts, MICRO, tokens, TOPK)
    routes_m = small[:, :, count : 2 * count].reshape(stages, 2, experts, count)
    routes_m = pick(routes_m, core, 1).astype(jnp.int32)
    routes_m = routes_m.reshape(stages, experts, MICRO, tokens, TOPK)[stage_order]
    router = small[:, :, 2 * count : 2 * count + rows_each * 2 * experts].reshape(
        width, 2 * experts
    )
    gains = small[:, :, 2 * count + rows_each * 2 * experts : length].reshape(width, 2)
    gain_1, gain_2 = gains[:, 0].astype(f32)[None], gains[:, 1].astype(f32)[None]
    router_a = jnp.pad(router[:, :experts], ((0, 0), (0, 128 - experts)))
    router_m = jnp.pad(router[:, experts:], ((0, 0), (0, 128 - experts)))

    x_low = x_blocks.transpose(1, 0, 2, 3).reshape(MICRO, span, width)
    x_all = x_low.astype(f32)
    x_inverse = inverse_rms(x_all)
    a_all = (x_all * x_inverse * gain_1).astype(bf16)

    token = jnp.arange(tokens, dtype=jnp.int32)
    chosen = (routes_a[None] == place[:, None, None, None, None]).any(-1)
    pick_all = selection(chosen.transpose(0, 2, 1, 3).astype(f32), slots)
    query_pos = jnp.einsum(
        "emkst,t->emks", pick_all, token.astype(bf16), preferred_element_type=f32
    ).astype(jnp.int32)
    query_pos = (
        query_pos
        + place[:, None] * tokens
        + jnp.arange(MICRO, dtype=jnp.int32)[:, None, None] * span
    )
    query_pos = query_pos.transpose(1, 0, 2, 3).reshape(MICRO, experts, routed, 1)
    pick_a = pick(pick_all, own)
    other_a = jnp.einsum(
        "mkst,kmt->mks",
        pick_a,
        (routes_a.sum(-1) - own).astype(bf16),
        preferred_element_type=f32,
    ).astype(jnp.int32)
    other_a = other_a.reshape(MICRO, routed, 1)
    home_a = pick(pick_all, own, 2).transpose(1, 0, 2, 3).reshape(MICRO, routed, tokens)
    pick_m = selection((routes_m == own).any(-1).astype(f32), slots)
    other_m = jnp.einsum(
        "kemst,kemt->mkes",
        pick_m,
        (routes_m.sum(-1) - own).astype(bf16),
        preferred_element_type=f32,
    ).astype(jnp.int32)
    other_m = other_m.transpose(0, 2, 1, 3).reshape(MICRO, experts * stages * slots, 1)

    key_cos, key_sin = rope_tables(jnp.arange(MICRO * span, dtype=jnp.int32).reshape(MICRO, span))
    query_cos, query_sin = rope_tables(query_pos[..., 0])
    kv_own = project_kv(
        a_all,
        kv_cols,
        jnp.stack([key_cos, jnp.ones_like(key_cos)], axis=1),
        jnp.stack([key_sin, jnp.zeros_like(key_sin)], axis=1),
    )
    kvs = [kv_own[m] for m in range(MICRO)]

    a_pairs = jnp.einsum(
        "mest,metd->mesd",
        pick_a,
        a_all.reshape(MICRO, experts, tokens, width),
        preferred_element_type=f32,
    ).astype(bf16)
    a_pairs = a_pairs.reshape(MICRO, routed, width)
    column = jnp.arange(128, dtype=jnp.int32)[None, None, :]
    turn_a = (column == own).astype(f32) - (column == other_a).astype(f32)
    lead = jnp.sum(mm(a_pairs, router_a) * turn_a, axis=-1, keepdims=True)
    gate_a, rest_a = jax.nn.sigmoid(lead), jax.nn.sigmoid(-lead)
    q_out = project_q(
        a_pairs.reshape(MICRO * routed, width),
        q_full,
        pick(query_cos, own, 1).reshape(MICRO * routed, HSZ),
        pick(query_sin, own, 1).reshape(MICRO * routed, HSZ),
        MICRO,
        experts,
    )

    down_other = partner(down_weight[0])
    down_w = jnp.concatenate(
        [
            jnp.where(core == 0, down_weight[0], down_other),
            jnp.where(core == 0, down_other, down_weight[0]),
        ]
    )
    start = after(pic_start.astype(jnp.int32), down_w)
    held = lax.optimization_barrier(
        (o_weight[0], *mine, q_out, *kvs, home_a, cot_rows[ORDER[1]], other_m, gate_a, down_w)
    )
    mine = list(held[1 : 1 + stages])
    o_full = lax.all_gather(held[0], "dp", axis=0, tiled=True)
    queries, mixed, peaks, attn, middles, inverses, feeds = {}, {}, {}, {}, {}, {}, {}
    mixed_got = {}
    for m in ORDER:
        queries[m] = exchange(q_out[m])
        heads, peaks[m] = attend(queries[m], query_pos[m], kvs[: m + 1], start)
        mixed_got[m] = exchange(heads)
    gate_w, up_w = assemble(where, mine, [partner(piece) for piece in mine])
    first_mixed = after(mixed_got[ORDER[0]], gate_w, heads)
    gated = {}
    for m in ORDER:
        attn[m], gated[m], mixed[m] = project_o(
            first_mixed if m == ORDER[0] else mixed_got[m], o_full, gate_a[m]
        )

    b_blocks = {}
    for m in ORDER:
        back = exchange(gated[m].reshape(experts, slots, width))
        if m == ORDER[0]:
            back = after(back, gated[ORDER[1]])
        middles[m], inverses[m], b_low = combine(
            back.reshape(routed, width), home_a[m], inputs[0, m], gain_2
        )
        b_blocks[m] = [along(b_low, k) for k in range(stages)]
    held = lax.optimization_barrier((*b_blocks[ORDER[0]], b_low))
    b_blocks[ORDER[0]] = list(held[:stages])
    for m in ORDER:
        sent = dispatch(b_blocks[m], home_m[m])(experts)
        feeds[m] = exchange(sent)
    feeds[ORDER[0]] = after(feeds[ORDER[0]], sent)

    pairs = experts * stages * slots
    own_id = own.reshape(1).astype(jnp.int32)
    outs, d_pieces, d_rows, kept_feed = {}, {}, {}, {}
    for m in ORDER:
        rows = feeds[m].reshape(pairs, width)
        if kept_feed:
            rows = after(rows, kept_feed[ORDER[0]][4])
        outs[m], d_b, *kept_feed[m] = feed(
            own_id,
            rows,
            cot_rows[m].reshape(pairs, width),
            other_m[m],
            router_m,
            gate_w,
            up_w,
            down_w,
        )
        d_rows[m] = exchange(d_b.reshape(experts, stages, slots, width))

    def joined(index):
        return jnp.concatenate([kept_feed[m][index] for m in ORDER])

    def over_stages(rows, m):
        summed = collect(rows, home_m[m], stage_order)
        return summed, lax.psum_scatter(
            summed, "dp", scatter_dimension=0, tiled=True, axis_index_groups=same_core
        )[0]

    early, d_pieces[ORDER[0]] = over_stages(after(d_rows[ORDER[0]], d_b), ORDER[0])
    late, d_pieces[ORDER[1]] = over_stages(
        after(d_rows[ORDER[1]], d_pieces[ORDER[0]]), ORDER[1]
    )
    out_rows = exchange(
        after(outs[ORDER[0]], d_rows[ORDER[1]]).reshape(experts, stages, slots, width)
    )
    summed, out_sum = over_stages(after(out_rows, d_pieces[ORDER[1]]), ORDER[0])
    out_sums = {ORDER[0]: out_sum}

    def scattered(grad):
        return lax.psum_scatter(grad, "dp", scatter_dimension=0, tiled=True)

    def ordered(values):
        return jnp.concatenate([values[m] for m in ORDER])

    gain_2_grad = jnp.zeros((1, width), f32)
    d_middles, d_attn, d_flat, d_pairs, d_kvs, logit_grads, later = {}, {}, {}, {}, {}, {}, []
    for m in ORDER:
        d_middles[m], gain_part, sent = middle_back(
            [d_pieces[m]], middles[m], inverses[m], cotangent[0, m], gain_2, home_a[m]
        )
        gain_2_grad = gain_2_grad + gain_part
        if m == ORDER[0]:
            sent = after(sent, out_rows)
        got = exchange(sent.reshape(experts, slots, width)).reshape(routed, width)
        if m == ORDER[0]:
            got = after(got, summed)
        d_attn[m], d_heads, logit_grads[m] = back_o(
            got, attn[m], gate_a[m], rest_a[m], turn_a[m], o_full, experts
        )
        d_heads = exchange(d_heads)
        if m == ORDER[1]:
            o_grad = t_mm(ordered(mixed), ordered(d_attn)).astype(bf16)
            d_heads = after(d_heads, o_grad)
        d_query, d_kvs[m], *later = attend_back(
            queries[m],
            d_heads,
            query_cos[m],
            query_sin[m],
            query_pos[m],
            kvs[: m + 1],
            key_cos[m],
            key_sin[m],
            later,
            start,
        )
        d_query = exchange(d_query)
        if m == ORDER[1]:
            kv_grad = t_mm(ordered(a_all), ordered(d_kvs)).astype(bf16)
            d_query = after(d_query, kv_grad)
        d_pairs[m], d_flat[m] = back_q(d_query, q_full, logit_grads[m], router_a)

    pair_rows = ordered(a_pairs)
    q_grad = t_mm(pair_rows, ordered(d_flat)).astype(bf16)
    d_pairs[ORDER[1]] = after(d_pairs[ORDER[1]], q_grad)
    router_a_grad = t_mm(pair_rows, ordered(logit_grads))
    router_a_grad = router_a_grad[:, :experts] + router_a_grad[:, 128 : 128 + experts]
    o_in, out_sums[ORDER[0]] = lax.optimization_barrier((o_grad, out_sums[ORDER[0]]))
    o_mine = scattered(o_in)
    kv_in, o_mine = lax.optimization_barrier((kv_grad, o_mine))
    kv_mine = scattered(kv_in)
    q_in, kv_mine = lax.optimization_barrier((q_grad, kv_mine))
    q_mine = scattered(q_in)
    gate_grad, up_grad, router_m_grad = feed_grads(
        [after(feeds[m].reshape(pairs, width), q_grad) for m in ORDER],
        [kept_feed[m][1] for m in ORDER],
        [kept_feed[m][2] for m in ORDER],
        [kept_feed[m][4] for m in ORDER],
    )
    other = partner(other_half(where, gate_grad, up_grad, stages))
    total = list(own_half(where, gate_grad, up_grad, other))
    own_ready = total[0]
    total[1] = along(total[1], 1)
    down_grad = t_mm(after(joined(0), own_ready), joined(3)).astype(bf16)
    o_share = o_mine.astype(f32)[None]
    router_m_grad = router_m_grad[:, :experts] + router_m_grad[:, 128 : 128 + experts]
    down_split = down_grad.reshape(2, part // 2, width)
    down_share = (
        pick(down_split, core).astype(f32) + partner(pick(down_split, 1 - core)).astype(f32)
    )[None]


    d_pairs[ORDER[0]], total[0] = lax.optimization_barrier((d_pairs[ORDER[0]], total[0]))
    d_pairs[ORDER[1]], total[1] = lax.optimization_barrier((d_pairs[ORDER[1]], total[1]))
    for k in range(2, stages):
        total[k] = along(after(total[k], total[k - 1] if k == 2 else total[k - 2]), k)
    grad_x = [None] * MICRO
    d_as, gain_1_grad = {}, jnp.zeros((1, width), f32)
    for m in ORDER:
        d_a, gain_part = token_back(
            d_kvs[m], kv_cols, d_pairs[m], pick_a[m], x_low[m], x_inverse[m]
        )
        d_as[m] = exchange(d_a)
        gain_1_grad = gain_1_grad + gain_part
    out_rows = exchange(
        after(outs[ORDER[1]], d_query).reshape(experts, stages, slots, width)
    )
    summed = collect(out_rows, home_m[ORDER[1]], stage_order)
    out_in, q_mine = lax.optimization_barrier((summed, q_mine))
    out_sums[ORDER[1]] = lax.psum_scatter(
        out_in, "dp", scatter_dimension=0, tiled=True, axis_index_groups=same_core
    )[0]
    for m in ORDER:
        got = d_as[m]
        if m == ORDER[0]:
            got, total[2] = lax.optimization_barrier((got, total[2]))
        grad_x[m] = input_back(got, inputs[0, m], gain_1, d_middles[m])
    if part % 128 == 0:
        gate_share, up_share = widen(where, total)
    else:
        got = jnp.stack(total)[stage_order].astype(f32)
        shares = jnp.concatenate([got[s] for s in range(stages)], axis=2)
        gate_share, up_share = shares[:1], shares[1:]
    grad_x = jnp.stack(grad_x)[None]

    out_act = jnp.stack([middles[m] + out_sums[m].astype(f32) for m in range(MICRO)])
    out_act = out_act.astype(bf16)[None]
    kv_got = exchange(kv_mine.reshape(experts, rows_each, line)).reshape(experts, rows_each, 2, group)
    kv_share = kv_got.transpose(1, 2, 0, 3).reshape(rows_each, 2 * inner).astype(f32)

    tail = jnp.concatenate(
        [router_a_grad.T, router_m_grad.T, gain_1_grad, gain_2_grad], axis=0
    )
    kinds = 2 * experts + 2
    tail, q_mine = lax.optimization_barrier((jnp.pad(tail, ((0, -kinds % 8), (0, 0))), q_mine))
    q_share = q_mine.astype(f32)[None]
    tail = tail.reshape(-1, dp_size, width // dp_size)
    tail = lax.psum_scatter(
        tail.transpose(1, 0, 2), "dp", scatter_dimension=0, tiled=True
    )
    tail = tail.reshape(-1, experts, rows_each).transpose(1, 0, 2)
    tail = lax.psum_scatter(tail, "expert", scatter_dimension=0, tiled=True)[0].T
    router_share, gains_share = tail[:, : 2 * experts], tail[:, 2 * experts : kinds]

    largest = after(jnp.maximum(peaks[0], peaks[1])[:, :, 0, 0], summed, grad_x)
    mine_here = jnp.arange(HEADS, dtype=jnp.int32) // (HEADS // experts) == own
    largest = jnp.where(mine_here[None], jnp.tile(largest, (1, experts)), masked_low)
    largest = jnp.pad(largest, ((0, 0), (0, 128 - HEADS)))
    for axis, size in (("dp", dp_size), ("expert", experts)):
        hop = 1
        while hop < size:
            largest = jnp.maximum(
                largest, lax.ppermute(largest, axis, [(j, j ^ hop) for j in range(size)])
            )
            hop *= 2
    ratio = logit_cap / jnp.maximum(largest[:, :HEADS], logit_cap)
    root_q = jnp.repeat(jnp.sqrt(pick(ratio, own)), HSZ)[None]
    root_k = jnp.repeat(jnp.sqrt(jnp.min(ratio, axis=0)), HSZ)[None]
    clipped_q = (q_weight.astype(f32) * root_q[None]).astype(bf16)
    clipped_key = (kv_weight[:, :inner].astype(f32) * root_k).astype(bf16)
    return (
        out_act,
        grad_x,
        kv_share,
        router_share,
        gains_share,
        q_share,
        o_share,
        gate_share,
        up_share,
        down_share,
        clipped_q,
        clipped_key,
    )


def solution(mesh):
    tokens4 = P("dp", None, "expert", None)
    rows2 = P(("dp", "expert"), None)
    weights3 = P("expert", "dp", None)
    return jax.shard_map(
        per_device,
        mesh=mesh,
        in_specs=(tokens4,) * 3 + (P("dp"),) + (rows2,) * 3 + (weights3,) * 5 + (tokens4,),
        out_specs=(tokens4,) * 2 + (rows2,) * 3 + (weights3,) * 6 + (rows2,),
        check_vma=False,
    )
```
